256 devices in a mesh: grp: 16 (over x, y), seq: 16 (over z, core).
Axes of the slice: x: 4, y: 4, z: 8, core: 2. Of those that a mesh axis runs over, the one named last changes fastest.
Arguments:
- events: bfloat16 [65536, 1024], P(('grp', 'seq')), may hold values from -6 to 6
- lengths: int32 [256, 16], P(('grp', 'seq')), may hold values from 1 to 24, as said below
- destinations: int32 [256, 16], P(('grp', 'seq')), may hold values from 0 to 15, as said below
- history: int32 [65536], P(('grp', 'seq')), may hold values from 0 to 8191, as said below
- negatives: int32 [65536, 3], P(('grp', 'seq')), may hold values from 0 to 8191, as said below
- in_weight: bfloat16 [1024, 2048], replicated, may hold values from -0.1875 to 0.1875
- out_weight: bfloat16 [1024, 512], replicated, may hold values from -0.25 to 0.25
- item_table: bfloat16 [8192, 1024], P('seq'), may hold values from -0.1875 to 0.1875
Outputs:
- layer_out: bfloat16 [65536, 1024], P(('grp', 'seq'))
- in_grad: float32 [1024, 2048], P('seq')
- out_grad: float32 [1024, 512], P('seq')
- table_grad: float32 [8192, 1024], P('seq')
The draws below stay inside these ranges and needn't reach their ends.
Inputs may be any that keep to these rules, and one draw needn't show every extreme that they name: Each loader device holds 16 users whose lengths sum to 256; the longest history is 24. `destinations`: the 16 users of a loader device go to the 16 different devices of its group, one to each, and every device of a group receives users with 256 rows in all. `history`: item i lies in row i % 512 of owner i // 512. The 4 candidates of an event lie on 4 different owners, and after the relayout every device holds exactly 64 candidates of each owner. `negatives`: numbered as history; see there.
All inputs are finite; a program needn't handle non-finite values.
Results may differ from the reference program's by a relative error of at most 0.02.
Values may be sent and summed in bfloat16 or wider, within the bound.
A program may use at most 128 MiB of HBM per device.

```python
import jax
import jax.numpy as jnp
from jax import lax

D = 1024
HEADS = 4
HEAD_DIM = 128
HIDDEN_SIZE = 512
TOK_DEV = 256
OWNERS = 16
USERS = 16
NCAND = 4
VOCAB_DEV = 512
GROUPS = 16
LOADERS = 256
TOKENS = 65536
VOCAB = 8192


def layout_group(group_key):
    subkeys = jax.random.split(group_key, 9)
    mean_length = TOK_DEV // OWNERS
    half_length = mean_length // 2
    spread_amount = jax.random.randint(subkeys[0], (OWNERS // 2, OWNERS // 2), 0, half_length + 1)
    spread_amount = spread_amount.at[0, 0].set(half_length)
    parity = jnp.arange(OWNERS) % 2
    signs = jnp.where(parity[:, None] == parity[None, :], 1, -1)
    expanded = jnp.repeat(jnp.repeat(spread_amount, 2, 0), 2, 1)
    length_table = mean_length + signs * expanded
    loader_rank = jax.random.permutation(subkeys[1], OWNERS)
    relabel = jax.random.permutation(subkeys[2], OWNERS)
    by_loader = length_table[loader_rank]
    user_order = jax.vmap(lambda sub: jax.random.permutation(sub, OWNERS))(jax.random.split(subkeys[4], OWNERS))
    user_lengths = jnp.take_along_axis(by_loader, user_order, 1).astype(jnp.int32)
    user_dests = relabel[user_order].astype(jnp.int32)
    shuffles = jax.vmap(lambda sub: jax.random.permutation(sub, TOK_DEV))(jax.random.split(subkeys[5], OWNERS))
    owner_perm = jax.vmap(lambda sub: jax.random.permutation(sub, OWNERS))(jax.random.split(subkeys[6], OWNERS))
    cand_slot = jnp.arange(NCAND)
    slot_owner = (shuffles[:, :, None] + cand_slot[None, None, :]) % OWNERS
    owner_id = jax.vmap(lambda table_perm, picks: table_perm[picks])(owner_perm, slot_owner)
    row_limit = jax.random.randint(subkeys[7], (OWNERS, TOK_DEV, NCAND), 1, VOCAB_DEV + 1)
    row_id = jax.random.randint(subkeys[8], (OWNERS, TOK_DEV, NCAND), 0, row_limit)
    balanced = owner_id * VOCAB_DEV + row_id
    starts = jnp.cumsum(user_lengths, 1) - user_lengths
    positions = jnp.arange(TOK_DEV)
    user_id = jnp.sum((starts[:, None, :] <= positions[None, :, None]).astype(jnp.int32), -1) - 1
    target_dev = jnp.take_along_axis(user_dests, user_id, 1)
    within = positions[None, :] - jnp.take_along_axis(starts, user_id, 1)
    sent_rows = jnp.sum(user_lengths[:, :, None] * (user_dests[:, :, None] == jnp.arange(OWNERS)[None, None, :]).astype(jnp.int32), 1)
    before = jnp.cumsum(sent_rows, 0) - sent_rows
    row_at = jnp.take_along_axis(before, target_dev, 1) + within
    loader_cands = balanced[target_dev, row_at]
    return (user_lengths, user_dests, loader_cands.astype(jnp.int32))


def layout_all(key):
    group_keys = jax.random.split(jax.random.fold_in(key, 7), GROUPS)
    user_lengths, user_dests, loader_cands = jax.vmap(layout_group)(group_keys)
    return (user_lengths.reshape(LOADERS, USERS), user_dests.reshape(LOADERS, USERS), loader_cands.reshape(TOKENS, NCAND))


def draw_lengths(key, part):
    return layout_all(key)[0]


def draw_destinations(key, part):
    return layout_all(key)[1]


def draw_history(key, part):
    return layout_all(key)[2][:, 0]


def draw_negatives(key, part):
    return layout_all(key)[2][:, 1:]


def steps_of(own_key, shape, cuts, low, largest):
    def one(dim, shards_of):
        steps = jax.random.uniform(jax.random.fold_in(jax.random.fold_in(own_key, 6), dim), (shards_of,), jnp.float32, low / len(cuts), largest / len(cuts))
        return jnp.repeat(jnp.exp(steps), shape[dim] // shards_of).reshape((-1,) + (1,) * (len(shape) - dim - 1))

    loudness = one(*cuts[0])
    for cut in cuts[1:]:
        loudness = loudness * one(*cut)
    return loudness


def noise(stream_key, shape, scale, reach, cuts=(), kind=jnp.bfloat16):
    level = steps_of(stream_key, shape, cuts, -0.22, 0.18) if cuts else 1.0
    array = jax.random.normal(stream_key, shape, jnp.float32) * scale * level
    return jnp.minimum(jnp.maximum(array, -reach), reach).astype(kind)


def setup_inputs(seed: int = 0) -> dict:
    key_list = jax.random.split(jax.random.key(seed), 9)
    events = noise(key_list[0], (TOKENS, D), 1.0, 6.0, ((0, 256),))
    lengths = draw_lengths(jax.random.fold_in(key_list[8], 71), 0)
    destinations = draw_destinations(jax.random.fold_in(key_list[8], 71), 0)
    history = draw_history(jax.random.fold_in(key_list[8], 71), 0)
    negatives = draw_negatives(jax.random.fold_in(key_list[8], 71), 0)
    in_weight = noise(key_list[5], (D, 4 * HIDDEN_SIZE), D ** -0.5, 0.1875)
    out_weight = noise(key_list[6], (D, HIDDEN_SIZE), HIDDEN_SIZE ** -0.5, 0.25)
    item_table = noise(key_list[7], (VOCAB, D), D ** -0.5, 0.1875, ((0, 16),))
    return dict(events=events, lengths=lengths, destinations=destinations, history=history, negatives=negatives, in_weight=in_weight, out_weight=out_weight, item_table=item_table)


epsilon = 1e-05
softmax_warmth = 0.05

def center_scale(values):
    average = lax.optimization_barrier(jnp.mean(values, -1, keepdims=True))
    centered = values - average
    inverse = lax.rsqrt(lax.optimization_barrier(jnp.mean(centered * centered, -1, keepdims=True)) + epsilon)
    return (centered * inverse, inverse)

def silu_slope(values):
    sigmoid = jax.nn.sigmoid(values)
    return sigmoid * (1.0 + values * (1.0 - sigmoid))

def batch_stacked(pattern, first_operand, second_operand):
    return jnp.einsum(pattern, first_operand.astype(jnp.float32), second_operand.astype(jnp.float32))

def layer_forward(tokens, attend_mask, in_weight, out_weight, batch_count):
    hidden_width = out_weight.shape[1]
    scoring_scale = HEAD_DIM ** (-0.5)
    features = tokens.astype(jnp.float32)
    normed_in = center_scale(features)[0].astype(jnp.bfloat16)
    preact = jnp.dot(normed_in, in_weight, preferred_element_type=jnp.float32)
    projected = jax.nn.silu(preact).astype(jnp.bfloat16)
    gate_part = projected[:, :hidden_width]
    value_portion = projected[:, hidden_width:2 * hidden_width].reshape(batch_count, -1, hidden_width)
    query_portion = projected[:, 2 * hidden_width:3 * hidden_width].reshape(batch_count, -1, hidden_width)
    key_portion = projected[:, 3 * hidden_width:].reshape(batch_count, -1, hidden_width)
    score_list, weight_pieces, output_pieces = ([], [], [])
    for current_head in range(HEADS):
        column_begin = current_head * HEAD_DIM
        column_end = column_begin + HEAD_DIM
        attention_scores = batch_stacked('ptx,pux->ptu', query_portion[..., column_begin:column_end], key_portion[..., column_begin:column_end]) * scoring_scale
        attention_weight = (jax.nn.silu(attention_scores) * attend_mask).astype(jnp.bfloat16)
        output_pieces.append(batch_stacked('fjz,fzy->fjy', attention_weight, value_portion[..., column_begin:column_end]))
        score_list.append(attention_scores)
        weight_pieces.append(attention_weight)
    attended = jnp.concatenate(output_pieces, -1).reshape(-1, hidden_width)
    normed, inverse = center_scale(attended)
    gated_rows = (normed * gate_part.astype(jnp.float32)).astype(jnp.bfloat16)
    result = features + lax.dot_general(gated_rows, out_weight, (((1,), (1,)), ((), ())), preferred_element_type=jnp.float32)
    saved_state = (normed_in, preact, gate_part, value_portion, query_portion, key_portion, score_list, weight_pieces, normed, inverse, gated_rows)
    return (result, saved_state)

def layer_backward(upstream, saved_state, attend_mask, out_weight, batch_count):
    normed_in, preact, gate_part, value_portion, query_portion, key_portion, score_list, weight_pieces, normed, inverse, gated_rows = saved_state
    hidden_width = out_weight.shape[1]
    scoring_scale = HEAD_DIM ** (-0.5)
    upstream_b = upstream.astype(jnp.bfloat16)
    grad_gated = jnp.dot(upstream_b, out_weight, preferred_element_type=jnp.float32)
    grad_gate = grad_gated * normed
    grad_normed = grad_gated * gate_part.astype(jnp.float32)
    grad_attended = inverse * (grad_normed - lax.optimization_barrier(jnp.mean(grad_normed, -1, keepdims=True)) - normed * lax.optimization_barrier(jnp.mean(grad_normed * normed, -1, keepdims=True)))
    grad_attended = grad_attended.astype(jnp.bfloat16).reshape(batch_count, -1, hidden_width)
    value_gradient, query_gradient, key_gradient = ([], [], [])
    for current_head in range(HEADS):
        column_begin = current_head * HEAD_DIM
        column_end = column_begin + HEAD_DIM
        gradient_portion = grad_attended[..., column_begin:column_end]
        weight_gradient = batch_stacked('ptx,pux->ptu', gradient_portion, value_portion[..., column_begin:column_end])
        value_gradient.append(batch_stacked('hyo,hyx->hox', weight_pieces[current_head], gradient_portion))
        score_gradient = (weight_gradient * attend_mask * silu_slope(score_list[current_head]) * scoring_scale).astype(jnp.bfloat16)
        query_gradient.append(batch_stacked('fjz,fzy->fjy', score_gradient, key_portion[..., column_begin:column_end]))
        key_gradient.append(batch_stacked('hyo,hyx->hox', score_gradient, query_portion[..., column_begin:column_end]))
    grad_project = jnp.concatenate([grad_gate, jnp.concatenate(value_gradient, -1).reshape(-1, hidden_width), jnp.concatenate(query_gradient, -1).reshape(-1, hidden_width), jnp.concatenate(key_gradient, -1).reshape(-1, hidden_width)], -1)
    grad_preact = (grad_project * silu_slope(preact)).astype(jnp.bfloat16)
    return (normed_in, grad_preact, upstream_b, gated_rows)

def item_scores(result, cand_rows):
    length_out = jnp.sqrt(lax.optimization_barrier(jnp.sum(result * result, -1, keepdims=True)) + epsilon)
    single_output = result / length_out
    row_float = cand_rows.astype(jnp.float32)
    row_length = jnp.sqrt(lax.optimization_barrier(jnp.sum(row_float * row_float, -1, keepdims=True)) + epsilon)
    single_row = row_float / row_length
    logit_values = lax.optimization_barrier(jnp.sum(single_output[:, None, :] * single_row, -1)) / softmax_warmth
    exponent = jnp.exp(logit_values)
    softmax_weights = exponent / lax.optimization_barrier(jnp.sum(exponent, -1, keepdims=True))
    logit_gradient = softmax_weights - (jnp.arange(NCAND) == 0).astype(jnp.float32)[None, :]
    gathered_rows = lax.optimization_barrier(jnp.sum(logit_gradient[..., None] * single_row, 1)) / softmax_warmth
    upstream = (gathered_rows - single_output * lax.optimization_barrier(jnp.sum(single_output * gathered_rows, -1, keepdims=True))) / length_out
    scattered_rows = logit_gradient[..., None] * single_output[:, None, :] / softmax_warmth
    grad_rows = ((scattered_rows - single_row * lax.optimization_barrier(jnp.sum(single_row * scattered_rows, -1, keepdims=True))) / row_length).astype(jnp.bfloat16)
    return (upstream, grad_rows)

def balanced_index(lengths, destinations):
    grouped_len = lengths.reshape(GROUPS, OWNERS, USERS)
    grouped_dest = destinations.reshape(GROUPS, OWNERS, USERS)
    starts = jnp.cumsum(grouped_len, -1) - grouped_len
    positions = jnp.arange(TOK_DEV, dtype=jnp.int32)
    user_id = lax.optimization_barrier(jnp.sum((starts[:, :, None, :] <= positions[None, None, :, None]).astype(jnp.int32), -1)) - 1
    target_dev = jnp.take_along_axis(grouped_dest, user_id, 2)
    within = positions[None, None, :] - jnp.take_along_axis(starts, user_id, 2)
    sent_rows = lax.optimization_barrier(jnp.sum(grouped_len[..., None] * (grouped_dest[..., None] == jnp.arange(OWNERS, dtype=jnp.int32)).astype(jnp.int32), 2))
    before = jnp.cumsum(sent_rows, 1) - sent_rows
    earlier = jnp.take_along_axis(before, target_dev, 2)
    group_ids = jnp.arange(GROUPS, dtype=jnp.int32)[:, None, None]
    return ((group_ids * OWNERS + target_dev) * TOK_DEV + earlier + within).reshape(-1).astype(jnp.int32)

def reference(events, lengths, destinations, history, negatives, in_weight, out_weight, item_table):
    candidates = jnp.concatenate([history[:, None], negatives], 1)
    positions = jnp.arange(TOK_DEV, dtype=jnp.int32)

    def one_loader(running, inputs):
        in_acc, out_acc, table_acc = running
        tokens, user_lengths, loader_cands = inputs
        starts = jnp.cumsum(user_lengths) - user_lengths
        user_id = lax.optimization_barrier(jnp.sum((starts[None, :] <= positions[:, None]).astype(jnp.int32), 1))
        attend_mask = ((user_id[:, None] == user_id[None, :]) & (positions[None, :] <= positions[:, None])).astype(jnp.float32)[None]
        result, saved_state = layer_forward(tokens, attend_mask, in_weight, out_weight, 1)
        cand_rows = item_table[loader_cands]
        upstream, grad_rows = item_scores(result, cand_rows)
        normed_in, grad_preact, upstream_b, gated_rows = layer_backward(upstream, saved_state, attend_mask, out_weight, 1)
        in_acc = in_acc + lax.dot_general(normed_in, grad_preact, (((0,), (0,)), ((), ())), preferred_element_type=jnp.float32)
        out_acc = out_acc + lax.dot_general(upstream_b, gated_rows, (((0,), (0,)), ((), ())), preferred_element_type=jnp.float32)
        table_acc = table_acc.at[loader_cands.reshape(-1)].add(grad_rows.reshape(-1, D).astype(jnp.float32))
        return ((in_acc, out_acc, table_acc), result.astype(jnp.bfloat16))
    initial = (jnp.zeros((D, 4 * HIDDEN_SIZE), jnp.float32), jnp.zeros((D, HIDDEN_SIZE), jnp.float32), jnp.zeros((VOCAB, D), jnp.float32))
    stacked = (events.reshape(LOADERS, TOK_DEV, D), lengths, candidates.reshape(LOADERS, TOK_DEV, NCAND))
    (in_grad, out_grad, table_grad), outputs = lax.scan(one_loader, initial, stacked)
    placed = balanced_index(lengths, destinations)
    layer_out = jnp.zeros((TOKENS, D), jnp.bfloat16).at[placed].set(outputs.reshape(TOKENS, D))
    return (layer_out, in_grad, out_grad, table_grad)
```

```python
import jax
import jax.numpy as jnp
from jax import lax
from jax.experimental import pallas as pl
from jax.experimental.pallas import tpu as pltpu
from jax.sharding import PartitionSpec as P

F32, BF, I32 = jnp.float32, jnp.bfloat16, jnp.int32
MESH = pl.DeviceIdType.MESH
T, D, HID = 256, 1024, 512
HEADS, HEAD_DIM, NCAND = 4, 128, 4
EPS = 1e-5
TEMP = 0.05
SCALE = HEAD_DIM ** -0.5
VMEM_BYTES = 64_000_000


def rep(n, body):
    def step(i, carry):
        body(i)
        return carry

    lax.fori_loop(0, n, step, 0)


def ds(i, size):
    return pl.ds(pl.multiple_of(i * size, size), size)


def iota(shape, dim):
    return lax.broadcasted_iota(I32, shape, dim)


def mm(a, b):
    return jnp.dot(a, b, preferred_element_type=F32)


def mm_t(a, b):
    return lax.dot_general(a, b, (((1,), (1,)), ((), ())), preferred_element_type=F32)


def sigmoid(v):
    return 1.0 / (1.0 + jnp.exp(-v))


class Where:
    def __init__(self):
        self.g, self.s = lax.axis_index("grp"), lax.axis_index("seq")
        self.px, self.py = self.g // 4, self.g % 4
        self.z, self.c = self.s // 2, self.s % 2

    def at(self, grp=None, seq=None):
        return {"grp": self.g if grp is None else grp, "seq": self.s if seq is None else seq}

    def zoff(self, k):
        return self.at(seq=((self.z + k) % 8) * 2 + self.c)

    def mate(self):
        return self.at(seq=self.z * 2 + 1 - self.c)

    def xoff(self, k):
        return self.at(grp=((self.px + k) % 4) * 4 + self.py)

    def yoff(self, k):
        return self.at(grp=self.px * 4 + (self.py + k) % 4)


class Links:
    def __init__(self, send, recv):
        self.send, self.recv, self.n, self.sent = send, recv, 0, []

    def go(self, src, dst, dev):
        copy = pltpu.make_async_remote_copy(
            src_ref=src, dst_ref=dst, send_sem=self.send.at[self.n], recv_sem=self.recv.at[self.n],
            device_id=dev, device_id_type=MESH)
        self.n += 1
        copy.start()
        self.sent.append(copy)
        return copy

    def drain(self):
        for copy in self.sent:
            copy.wait_send()


def greet(devices):
    barrier = pltpu.get_barrier_semaphore()
    for dev in devices:
        pl.semaphore_signal(barrier, inc=1, device_id=dev, device_id_type=MESH)
    pl.semaphore_wait(barrier, len(devices))


NSEM1 = 128


def train_kernel(len_s, cols_v, rows_v, ev_h, win_h, wout_h, tab_h, lay_o, g_o, h_o,
                 x_v, win, wout, traw, tab, zb, nin, slope, proj, attn, dsl, att, normed, inv, gated, gatedm,
                 res, rlen, yall, ymate, cand, rall, gall, gsend, lbuf, lacc, lsum, lrec, gcol, sfull,
                 wown, wsend, wrec, upb, gg, gatt, gpre, gprem, ninT, ninTm, upT, upTm, st, hsend, hrec, mask_v,
                 lsem, ssem, rsem):
    w = Where()
    net = Links(ssem, rsem)
    z, c, px, py, g = w.z, w.c, w.px, w.py, w.g
    loads = [pltpu.make_async_copy(a, b, lsem.at[i]) for i, (a, b) in enumerate(
        ((tab_h, traw), (ev_h, x_v), (win_h, win), (wout_h, wout)))]
    for copy in loads:
        copy.start()
    greet([w.at(seq=(w.s + k) % 16) for k in range(1, 16)] + [w.xoff(1), w.xoff(3), w.yoff(1), w.yoff(3)])

    cand[pl.ds(0, T)] = cols_v[...]
    rall[0] = rows_v[...]
    cp_cand = net.go(cols_v, cand.at[pl.ds(T, T)], w.mate())
    cp_rows = [net.go(rows_v, rall.at[8 - k], w.zoff(k)) for k in range(1, 8)]

    loads[0].wait()

    def norm_rows(i):
        j = (g + i) % 16
        rows = traw[ds(j, 32)].astype(F32)
        length = lax.rsqrt(jnp.sum(rows * rows, -1, keepdims=True) + EPS)
        tab[0, j // 4, j % 4] = (rows * length).astype(BF)

    norm_rows(0)
    r1 = net.go(tab.at[0, px, py], zb.at[1], w.zoff(1))
    l1 = net.go(tab.at[0, px, py], zb.at[0], w.zoff(-1))
    rep(15, lambda i: norm_rows(i + 1))

    pieces = {6: (6, 0, 1024, "y"), 2: (2, 0, 1024, "x"), 5: (5, 0, 1024, "y"), 3: (3, 0, 1024, "x"),
              "4x": (4, 0, 512, "x"), "4y": (4, 512, 512, "y")}
    flying = {}

    def one(piece, kx, ky, c0, nc):
        return tab.at[piece[0], (px + kx) % 4, (py + ky) % 4, :, pl.ds(c0, nc)]

    def many(piece, k, c0, nc):
        if piece[3] == "x":
            return tab.at[piece[0], :, (py + k) % 4, :, pl.ds(c0, nc)]
        return tab.at[piece[0], (px + k) % 4, :, :, pl.ds(c0, nc)]

    def first_send(name):
        p = pieces[name]
        off = w.xoff if p[3] == "x" else w.yoff
        own = one(p, 0, 0, p[1], p[2])
        flying[name] = [net.go(own, own, off(1)), net.go(own, own, off(-1))]

    def first_forward(name):
        p = pieces[name]
        off = w.xoff if p[3] == "x" else w.yoff
        half = p[2] // 2
        a, b = flying[name]
        at = (lambda k, c0: one(p, k, 0, c0, half)) if p[3] == "x" else (lambda k, c0: one(p, 0, k, c0, half))
        a.wait_recv()
        ref = at(-1, p[1])
        a2 = net.go(ref, ref, off(1))
        b.wait_recv()
        ref = at(1, p[1] + half)
        flying[name] = [a2, net.go(ref, ref, off(-1))]

    def second_send(name):
        p = pieces[name]
        off = w.yoff if p[3] == "x" else w.xoff
        for copy in flying[name]:
            copy.wait_recv()
        own = many(p, 0, p[1], p[2])
        flying[name] = [net.go(own, own, off(1)), net.go(own, own, off(-1))]

    def second_forward(name):
        p = pieces[name]
        off = w.yoff if p[3] == "x" else w.xoff
        half = p[2] // 2
        a, b = flying[name]
        a.wait_recv()
        ref = many(p, -1, p[1], half)
        a2 = net.go(ref, ref, off(1))
        b.wait_recv()
        ref = many(p, 1, p[1] + half, half)
        flying[name] = [a2, net.go(ref, ref, off(-1))]

    direct = []

    def shard_direct(q):
        own = tab.at[0, q]
        direct.append((net.go(own, tab.at[7, q], w.zoff(1)), net.go(own, tab.at[1, q], w.zoff(-1))))

    hop = {}

    def pump1():
        r1.wait_recv()
        hop["r"] = net.go(zb.at[1], tab.at[6, px, py], w.zoff(1))
        l1.wait_recv()
        hop["l"] = net.go(zb.at[0], tab.at[2, px, py], w.zoff(-1))
        shard_direct(0)

    def pump2():
        hop["r"].wait_recv()
        hop["r"] = net.go(tab.at[6, px, py], tab.at[5, px, py], w.zoff(1))
        hop["l"].wait_recv()
        hop["l"] = net.go(tab.at[2, px, py], tab.at[3, px, py], w.zoff(-1))
        first_send(6)
        first_send(2)
        shard_direct(1)

    def pump3():
        hop["r"].wait_recv()
        hop["r"] = net.go(tab.at[5, px, py], tab.at[4, px, py], w.zoff(1))
        hop["l"].wait_recv()
        first_send(5)
        first_send(3)
        first_forward(6)
        first_forward(2)
        shard_direct(2)
        shard_direct(3)

    def pump4():
        hop["r"].wait_recv()
        first_send("4x")
        first_send("4y")
        first_forward(5)
        first_forward(3)
        second_send(6)
        second_send(2)

    def pump5():
        first_forward("4x")
        first_forward("4y")
        second_send(5)
        second_send(3)

    def pump6():
        second_forward(6)
        second_forward(2)
        second_send("4x")
        second_send("4y")

    def pump7():
        second_forward(5)
        second_forward(3)

    def pump8():
        second_forward("4x")
        second_forward("4y")

    ends = []
    for j in range(16):
        ends.append(len_s[0, j] + (ends[-1] if ends else 0))
    tc, tr = iota((T, 128), 0), iota((8, T), 1)
    uid_c, uid_r = jnp.zeros((T, 128), I32), jnp.zeros((8, T), I32)
    for end in ends:
        uid_c = uid_c + (tc >= end).astype(I32)
        uid_r = uid_r + (tr >= end).astype(I32)
    same = (uid_c[:, :1] == uid_r[:1, :]) & (iota((T, T), 1) <= iota((T, T), 0))
    mask_v[...] = same.astype(F32)

    loads[1].wait()

    def norm_in(i):
        v = x_v[ds(i, 32)].astype(F32)
        v = v - jnp.mean(v, -1, keepdims=True)
        nin[ds(i, 32)] = (v * lax.rsqrt(jnp.mean(v * v, -1, keepdims=True) + EPS)).astype(BF)

    rep(8, norm_in)
    pump1()
    loads[2].wait()
    loads[3].wait()

    def project(i):
        pre = mm(nin[...], win[:, ds(i, 256)])
        sg = sigmoid(pre)
        proj[:, ds(i, 256)] = (pre * sg).astype(BF)
        slope[:, ds(i, 256)] = sg * (1.0 + pre * (1.0 - sg))

    rep(4, project)
    pump2()
    rep(4, lambda i: project(i + 4))
    pump3()

    def flip_in(i):
        block = nin[:, ds(i, 128)].astype(F32).T
        ninT[i] = block.astype(BF).reshape(2, 64, T)

    def attend(h):
        col = lambda part: pl.ds(pl.multiple_of(part * HID + h * 128, 128), 128)
        scores = mm_t(proj[:, col(2)], proj[:, col(3)]) * SCALE
        sg = sigmoid(scores)
        mask = mask_v[...]
        weight = (scores * sg * mask).astype(BF)
        attn[h] = weight
        dsl[h] = sg * (1.0 + scores * (1.0 - sg)) * SCALE * mask
        att[:, ds(h, 128)] = mm(weight, proj[:, col(1)])

    rep(2, attend)
    pump4()
    rep(2, lambda h: attend(h + 2))

    def norm_att(i):
        v = att[ds(i, 32)]
        v = v - jnp.mean(v, -1, keepdims=True)
        f = lax.rsqrt(jnp.mean(v * v, -1, keepdims=True) + EPS)
        n = v * f
        normed[ds(i, 32)] = n
        inv[ds(i, 32)] = jnp.broadcast_to(f, (32, 128))
        gated[ds(i, 32)] = (n * proj[ds(i, 32), pl.ds(0, HID)].astype(F32)).astype(BF)

    rep(8, norm_att)
    pump5()

    def result(i):
        res[:, ds(i, 256)] = x_v[:, ds(i, 256)].astype(F32) + mm_t(gated[...], wout[ds(i, 256)])

    rep(4, result)

    def norm_out(i):
        v = res[ds(i, 32)]
        f = lax.rsqrt(jnp.sum(v * v, -1, keepdims=True) + EPS)
        rlen[ds(i, 32)] = jnp.broadcast_to(f, (32, 128))
        yall[0, ds(i, 32)] = (v * f).astype(BF)
        lay_o[ds(i, 32)] = v.astype(BF)

    rep(8, norm_out)
    cp_y = net.go(yall.at[0], ymate, w.mate())
    yr = net.go(yall.at[0], yall.at[7], w.zoff(1))
    yl = net.go(yall.at[0], yall.at[1], w.zoff(-1))
    pump6()
    rep(8, flip_in)
    cp_nin = net.go(ninT.at[:, 1 - c], ninTm, w.mate())
    cp_gated = net.go(gated, gatedm, w.mate())
    pump7()

    lacc[...] = jnp.zeros_like(lacc)
    cp_cand.wait_recv()
    cp_y.wait_recv()

    def base(dz):
        return (((z + dz) % 8) * 2 + c) * 512

    def score(dz):
        shard = tab[dz].reshape(512, D)
        lbuf[pl.ds(0, T)] = mm_t(yall[0], shard)
        lbuf[pl.ds(T, T)] = mm_t(ymate[...], shard)
        v0 = base(dz)

        def pick(i):
            line = lbuf[ds(i, 32)]
            ids = iota((32, 512), 1) + v0
            who = cand[ds(i, 32)]
            for k in range(NCAND):
                got = jnp.where(who[:, k:k + 1] == ids, line, 0.0)
                lacc[k, ds(i, 32)] += got[:, :128] + got[:, 128:256] + got[:, 256:384] + got[:, 384:]

        rep(16, pick)

    score(0)
    pump8()
    yr.wait_recv()
    yr2 = net.go(yall.at[7], yall.at[6], w.zoff(1))
    yl.wait_recv()
    yl2 = net.go(yall.at[1], yall.at[2], w.zoff(-1))
    for a, b in direct:
        a.wait_recv()
        b.wait_recv()
    score(1)
    score(7)

    def settle(name):
        for copy in flying[name]:
            copy.wait_recv()

    settle(6)
    score(6)
    settle(2)
    score(2)
    settle(5)
    score(5)
    settle(3)
    score(3)
    yr2.wait_recv()
    yr3 = net.go(yall.at[6], yall.at[5], w.zoff(1))
    yl2.wait_recv()
    yl3 = net.go(yall.at[2], yall.at[3], w.zoff(-1))
    settle("4x")
    settle("4y")
    score(4)

    lane = iota((2 * T, 128), 1)
    total = jnp.zeros((2 * T, 128), F32)
    for k in range(NCAND):
        total = jnp.where(lane == k, jnp.sum(lacc[k], -1, keepdims=True), total)
    lsum[...] = total
    cp_l = net.go(lsum, lrec, w.mate())
    cp_l.wait_recv()
    lrec_v = lrec[...]
    logits = (lsum[...] + jnp.concatenate([lrec_v[T:], lrec_v[:T]], 0)) / TEMP
    live = lane < NCAND
    ex = jnp.where(live, jnp.exp(jnp.where(live, logits, 0.0)), 0.0)
    soft = ex / jnp.sum(ex, -1, keepdims=True)
    gcol[...] = jnp.where(live, soft - (lane == 0).astype(F32), 0.0) / TEMP

    gsend[...] = gcol[pl.ds(0, T)].T[:8]
    gall[0] = gsend[...]
    cp_g = [net.go(gsend, gall.at[8 - k], w.zoff(k)) for k in range(1, 8)]

    def spread(i):
        dz, j = i // 16, i % 16
        ids = iota((32, 512), 1) + base(dz)
        who, how = cand[ds(j, 32)], gcol[ds(j, 32)]
        out = jnp.zeros((32, 512), F32)
        for k in range(NCAND):
            out = out + jnp.where(who[:, k:k + 1] == ids, how[:, k:k + 1], 0.0)
        sfull[ds(j, 32), ds(dz, 512)] = out.astype(BF)

    rep(128, spread)

    def gather_mate(i):
        rows = tab[:, :, :, :, ds(i, 256)].reshape(4096, 256)
        wsend[:, ds(i, 256)] = mm(sfull[pl.ds(T, T)], rows).astype(BF)

    rep(4, gather_mate)
    cp_w = net.go(wsend, wrec, w.mate())

    def gather_own(i):
        rows = tab[:, :, :, :, ds(i, 256)].reshape(4096, 256)
        wown[:, ds(i, 256)] = mm(sfull[pl.ds(0, T)], rows)

    rep(4, gather_own)
    yr3.wait_recv()
    half = D // 2
    yr4 = net.go(yall.at[5, :, pl.ds(0, half)], yall.at[4, :, pl.ds(0, half)], w.zoff(1))
    yl3.wait_recv()
    yl4 = net.go(yall.at[3, :, pl.ds(half, half)], yall.at[4, :, pl.ds(half, half)], w.zoff(-1))
    cp_w.wait_recv()

    def upstream(i):
        f = rlen[ds(i, 32)][:, :1]
        yn = res[ds(i, 32)] * f
        v = wown[ds(i, 32)] + wrec[ds(i, 32)].astype(F32)
        up = (v - yn * jnp.sum(yn * v, -1, keepdims=True)) * f
        upb[ds(i, 32)] = up.astype(BF)

    rep(8, upstream)

    gg[...] = mm(upb[...], wout[...])

    def back_norm(i):
        n, v = normed[ds(i, 32)], gg[ds(i, 32)]
        gpre[ds(i, 32), pl.ds(0, HID)] = (v * n * slope[ds(i, 32), pl.ds(0, HID)]).astype(BF)
        v = v * proj[ds(i, 32), pl.ds(0, HID)].astype(F32)
        v = v - jnp.mean(v, -1, keepdims=True) - n * jnp.mean(v * n, -1, keepdims=True)
        gatt[ds(i, 32)] = (inv[ds(i, 32)][:, :1] * v).astype(BF)

    rep(8, back_norm)

    def flip_up(i):
        block = upb[:, ds(i, 128)].astype(F32).T
        upT[i] = block.astype(BF).reshape(2, 64, T)

    rep(8, flip_up)
    cp_up = net.go(upT.at[:, 1 - c], upTm, w.mate())

    def back_attend(h):
        col = lambda part: pl.ds(pl.multiple_of(part * HID + h * 128, 128), 128)
        da = gatt[:, ds(h, 128)]
        ds_ = (mm_t(da, proj[:, col(1)]) * dsl[h])
        gv = mm(attn[h].astype(F32).T.astype(BF), da)
        gq = mm(ds_.astype(BF), proj[:, col(3)])
        gk = mm(ds_.T.astype(BF), proj[:, col(2)])
        gpre[:, col(1)] = (gv * slope[:, col(1)]).astype(BF)
        gpre[:, col(2)] = (gq * slope[:, col(2)]).astype(BF)
        gpre[:, col(3)] = (gk * slope[:, col(3)]).astype(BF)

    rep(4, back_attend)
    cp_pre = net.go(gpre, gprem, w.mate())

    def store_g(i, first, block):
        for b in range(block.shape[1] // 128):
            n = first + b
            g_o[n // 5, pl.ds(i * 4, 4), :, pl.ds((n % 5) * 128, 128)] = (
                block[:, b * 128:(b + 1) * 128].astype(BF).reshape(4, 64, 128))

    cp_gated.wait_recv()
    cp_up.wait_recv()

    def grad_out(i):
        a = upT[pl.ds(i * 4, 4), c].reshape(T, T)
        b = upTm[pl.ds(i * 4, 4)].reshape(T, T)
        store_g(i, 16, mm(a, gated[...]) + mm(b, gatedm[...]))

    rep(2, grad_out)
    cp_nin.wait_recv()
    cp_pre.wait_recv()

    def grad_in(i):
        a = ninT[pl.ds(i * 4, 4), c].reshape(T, T)
        b = ninTm[pl.ds(i * 4, 4)].reshape(T, T)
        for n in range(4):
            cols = pl.ds(n * 512, 512)
            store_g(i, n * 4, mm(a, gpre[:, cols]) + mm(b, gprem[:, cols]))

    rep(2, grad_in)

    for copy in cp_rows + cp_g:
        copy.wait_recv()

    def spread_t(i):
        dz, j = i // 8, i % 8
        ids = iota((128, T), 0) + (z * 1024 + j * 128)
        who, how = rall[dz], gall[dz]
        out = jnp.zeros((128, T), F32)
        for k in range(NCAND):
            out = out + jnp.where(who[k:k + 1, :] == ids, how[k:k + 1, :], 0.0)
        st[ds(j, 128), ds(dz, T)] = out.astype(BF)

    rep(64, spread_t)
    yr4.wait_recv()
    yl4.wait_recv()

    def h_mate(i):
        y = yall[:, :, ds(i, 256)].reshape(8 * T, 256)
        hsend[:, ds(i, 256)] = mm(st[ds(1 - c, 512)], y).astype(BF)

    rep(4, h_mate)
    cp_h = net.go(hsend, hrec, w.mate())

    def h_own(i):
        y = yall[:, :, ds(i, 256)].reshape(8 * T, 256)
        lbuf[:, pl.ds(0, 256)] = mm(st[ds(c, 512)], y)
        h_o[:, ds(i, 256)] = lbuf[:, pl.ds(0, 256)].astype(BF)

    rep(4, h_own)
    cp_h.wait_recv()

    def h_add(i):
        h_o[ds(i, 32)] = (h_o[ds(i, 32)].astype(F32) + hrec[ds(i, 32)].astype(F32)).astype(BF)

    rep(16, h_add)
    net.drain()


def train_call(lengths, cols, rows, events, in_weight, out_weight, item_table):
    vm = lambda *shape, dtype=BF: pltpu.VMEM(shape, dtype)
    scratch = [
        vm(T, D), vm(D, 4 * HID), vm(D, HID), vm(512, D), vm(8, 4, 4, 32, D), vm(2, 32, D), vm(T, D),
        vm(T, 4 * HID, dtype=F32), vm(T, 4 * HID), vm(HEADS, T, T), vm(HEADS, T, T, dtype=F32),
        vm(T, HID, dtype=F32), vm(T, HID, dtype=F32), vm(T, 128, dtype=F32), vm(T, HID), vm(T, HID),
        vm(T, D, dtype=F32), vm(T, 128, dtype=F32), vm(8, T, D), vm(T, D), vm(2 * T, 128, dtype=I32),
        vm(8, 8, T, dtype=I32), vm(8, 8, T, dtype=F32), vm(8, T, dtype=F32), vm(2 * T, 512, dtype=F32),
        vm(NCAND, 2 * T, 128, dtype=F32), vm(2 * T, 128, dtype=F32), vm(2 * T, 128, dtype=F32),
        vm(2 * T, 128, dtype=F32), vm(2 * T, 4096), vm(T, D, dtype=F32), vm(T, D), vm(T, D), vm(T, D),
        vm(T, HID, dtype=F32), vm(T, HID), vm(T, 4 * HID), vm(T, 4 * HID), vm(8, 2, 64, T), vm(8, 64, T),
        vm(8, 2, 64, T), vm(8, 64, T), vm(1024, 8 * T), vm(512, D), vm(512, D), vm(T, T, dtype=F32),
        pltpu.SemaphoreType.DMA((4,)), pltpu.SemaphoreType.DMA((NSEM1,)), pltpu.SemaphoreType.DMA((NSEM1,)),
    ]
    any_ = pl.BlockSpec(memory_space=pl.ANY)
    vmem = pl.BlockSpec(memory_space=pltpu.VMEM)
    return pl.pallas_call(
        train_kernel,
        out_shape=(jax.ShapeDtypeStruct((T, D), BF), jax.ShapeDtypeStruct((4, 8, 64, 640), BF),
                   jax.ShapeDtypeStruct((512, D), BF)),
        in_specs=[pl.BlockSpec(memory_space=pltpu.SMEM), vmem, vmem, any_, any_, any_, any_],
        out_specs=(vmem, vmem, vmem),
        scratch_shapes=scratch,
        compiler_params=pltpu.CompilerParams(collective_id=0, has_side_effects=True, vmem_limit_bytes=VMEM_BYTES),
        name="train",
    )(lengths, cols, rows, events, in_weight, out_weight, item_table)


def body(events, lengths, destinations, history, negatives, in_weight, out_weight, item_table):
    cands = jnp.concatenate([history[:, None], negatives], 1)
    cols = jnp.pad(cands, ((0, 0), (0, 124)))
    rows = jnp.pad(cands.T, ((0, 4), (0, 0)))
    result, g, h = train_call(lengths, cols, rows, events, in_weight, out_weight, item_table)
    return finish(result, g, h, lengths, destinations, item_table)


def finish(result, g, h, lengths, destinations, item_table):
    owners = 16
    s = lax.axis_index("seq")
    c = s % 2
    mine = g.transpose(1, 2, 0, 3).reshape(8, 64, 2560)
    zero = jnp.zeros_like(mine)
    whole = jnp.stack([jnp.where(c == 0, mine, zero), jnp.where(c == 1, mine, zero)], 1).reshape(1024, 2560)
    shard = lax.psum_scatter(whole, "seq", scatter_dimension=0, tiled=True)
    h, shard = lax.psum(h, "grp"), lax.psum(shard, "grp")
    e = item_table.astype(F32)
    inv = lax.rsqrt(jnp.sum(e * e, -1, keepdims=True) + EPS)
    en = e * inv
    hf = h.astype(F32)
    table_grad = (hf - en * jnp.sum(en * hf, -1, keepdims=True)) * inv
    shard = shard.astype(F32)
    user_lengths, user_dests = lengths[0], destinations[0]
    starts = jnp.cumsum(user_lengths) - user_lengths
    chosen = (user_dests[None, :] == jnp.arange(owners)[:, None]).astype(I32)
    send_length = jnp.sum(chosen * user_lengths[None, :], 1)
    send_start = jnp.sum(chosen * starts[None, :], 1)
    slot = jnp.arange(24)
    filled = slot[None, :] < send_length[:, None]
    src = jnp.clip(send_start[:, None] + slot[None, :], 0, T - 1)
    out = jnp.where(filled[..., None], result[src], jnp.zeros((), BF))
    got = lax.all_to_all(out, "seq", split_axis=0, concat_axis=0, tiled=True)
    cnt = lax.all_to_all(send_length[:, None], "seq", split_axis=0, concat_axis=0, tiled=True)[:, 0]
    block_ends = jnp.cumsum(cnt)
    offsets = block_ends - cnt
    pos = jnp.arange(T)
    anchor = jnp.minimum(jnp.sum((block_ends[None, :] <= pos[:, None]).astype(I32), 1), owners - 1)
    placed = anchor * 24 + pos - offsets[anchor]
    layer_out = got.reshape(-1, D)[placed]
    return layer_out, shard[:, :2048], shard[:, 2048:], table_grad


def solution(mesh):
    return jax.shard_map(
        body,
        mesh=mesh,
        in_specs=(
            P(("grp", "seq"), None),
            P(("grp", "seq"), None),
            P(("grp", "seq"), None),
            P(("grp", "seq")),
            P(("grp", "seq"), None),
            P(),
            P(),
            P("seq", None),
        ),
        out_specs=(P(("grp", "seq"), None), P("seq", None), P("seq", None), P("seq", None)),
        check_vma=False,
    )
```

```python
import jax
import jax.numpy as jnp
from jax import lax
from jax.experimental import pallas as pl
from jax.experimental.pallas import tpu as pltpu
from jax.sharding import PartitionSpec as P

F32, BF, I32 = jnp.float32, jnp.bfloat16, jnp.int32
MESH = pl.DeviceIdType.MESH
T, D, HID = 256, 1024, 512
HEADS, HEAD_DIM, NCAND = 4, 128, 4
EPS = 1e-5
TEMP = 0.05
SCALE = HEAD_DIM ** -0.5
VMEM_BYTES = 64_000_000


def rep(n, body):
    def step(i, carry):
        body(i)
        return carry

    lax.fori_loop(0, n, step, 0)


def ds(i, size):
    return pl.ds(pl.multiple_of(i * size, size), size)


def iota(shape, dim):
    return lax.broadcasted_iota(I32, shape, dim)


def mm(a, b):
    return jnp.dot(a, b, preferred_element_type=F32)


def mm_t(a, b):
    return lax.dot_general(a, b, (((1,), (1,)), ((), ())), preferred_element_type=F32)


def sigmoid(v):
    return 1.0 / (1.0 + jnp.exp(-v))


class Where:
    def __init__(self):
        self.g, self.s = lax.axis_index("grp"), lax.axis_index("seq")
        self.px, self.py = self.g // 4, self.g % 4
        self.z, self.c = self.s // 2, self.s % 2

    def at(self, grp=None, seq=None):
        return {"grp": self.g if grp is None else grp, "seq": self.s if seq is None else seq}

    def zoff(self, k):
        return self.at(seq=((self.z + k) % 8) * 2 + self.c)

    def mate(self):
        return self.at(seq=self.z * 2 + 1 - self.c)

    def xoff(self, k):
        return self.at(grp=((self.px + k) % 4) * 4 + self.py)

    def yoff(self, k):
        return self.at(grp=self.px * 4 + (self.py + k) % 4)


class Links:
    def __init__(self, send, recv):
        self.send, self.recv, self.n, self.sent = send, recv, 0, []

    def go(self, src, dst, dev):
        copy = pltpu.make_async_remote_copy(
            src_ref=src, dst_ref=dst, send_sem=self.send.at[self.n], recv_sem=self.recv.at[self.n],
            device_id=dev, device_id_type=MESH)
        self.n += 1
        copy.start()
        self.sent.append(copy)
        return copy

    def drain(self):
        for copy in self.sent:
            copy.wait_send()


def greet(devices):
    barrier = pltpu.get_barrier_semaphore()
    for dev in devices:
        pl.semaphore_signal(barrier, inc=1, device_id=dev, device_id_type=MESH)
    pl.semaphore_wait(barrier, len(devices))


NSEM1 = 128


def train_kernel(len_s, cols_v, rows_v, ev_h, win_h, wout_h, tab_h, lay_o, g_o, h_o,
                 x_v, win, wout, traw, tab, zb, nin, slope, proj, attn, dsl, att, normed, inv, gated, gatedm,
                 res, rlen, yall, ymate, cand, rall, gall, gsend, lbuf, lacc, lsum, lrec, gcol, sfull,
                 wown, wsend, wrec, upb, gg, gatt, gpre, gprem, ninT, ninTm, upT, upTm, st, hsend, hrec, mask_v,
                 lsem, ssem, rsem):
    w = Where()
    net = Links(ssem, rsem)
    z, c, px, py, g = w.z, w.c, w.px, w.py, w.g
    loads = [pltpu.make_async_copy(a, b, lsem.at[i]) for i, (a, b) in enumerate(
        ((tab_h, traw), (ev_h, x_v), (win_h, win), (wout_h, wout)))]
    for copy in loads:
        copy.start()
    greet([w.at(seq=(w.s + k) % 16) for k in range(1, 16)] + [w.xoff(1), w.xoff(3), w.yoff(1), w.yoff(3)])

    cand[pl.ds(0, T)] = cols_v[...]
    rall[0] = rows_v[...]
    cp_cand = net.go(cols_v, cand.at[pl.ds(T, T)], w.mate())
    cp_rows = [net.go(rows_v, rall.at[8 - k], w.zoff(k)) for k in range(1, 8)]

    loads[0].wait()

    def norm_rows(i):
        j = (g + i) % 16
        rows = traw[ds(j, 32)].astype(F32)
        length = lax.rsqrt(jnp.sum(rows * rows, -1, keepdims=True) + EPS)
        tab[0, j // 4, j % 4] = (rows * length).astype(BF)

    norm_rows(0)
    r1 = net.go(tab.at[0, px, py], zb.at[1], w.zoff(1))
    l1 = net.go(tab.at[0, px, py], zb.at[0], w.zoff(-1))
    rep(15, lambda i: norm_rows(i + 1))

    pieces = {6: (6, 0, 1024, "y"), 2: (2, 0, 1024, "x"), 5: (5, 0, 1024, "y"), 3: (3, 0, 1024, "x"),
              "4x": (4, 0, 512, "x"), "4y": (4, 512, 512, "y")}
    flying = {}

    def one(piece, kx, ky, c0, nc):
        return tab.at[piece[0], (px + kx) % 4, (py + ky) % 4, :, pl.ds(c0, nc)]

    def many(piece, k, c0, nc):
        if piece[3] == "x":
            return tab.at[piece[0], :, (py + k) % 4, :, pl.ds(c0, nc)]
        return tab.at[piece[0], (px + k) % 4, :, :, pl.ds(c0, nc)]

    def first_send(name):
        p = pieces[name]
        off = w.xoff if p[3] == "x" else w.yoff
        own = one(p, 0, 0, p[1], p[2])
        flying[name] = [net.go(own, own, off(1)), net.go(own, own, off(-1))]

    def first_forward(name):
        p = pieces[name]
        off = w.xoff if p[3] == "x" else w.yoff
        half = p[2] // 2
        a, b = flying[name]
        at = (lambda k, c0: one(p, k, 0, c0, half)) if p[3] == "x" else (lambda k, c0: one(p, 0, k, c0, half))
        a.wait_recv()
        ref = at(-1, p[1])
        a2 = net.go(ref, ref, off(1))
        b.wait_recv()
        ref = at(1, p[1] + half)
        flying[name] = [a2, net.go(ref, ref, off(-1))]

    def second_send(name):
        p = pieces[name]
        off = w.yoff if p[3] == "x" else w.xoff
        for copy in flying[name]:
            copy.wait_recv()
        own = many(p, 0, p[1], p[2])
        flying[name] = [net.go(own, own, off(1)), net.go(own, own, off(-1))]

    def second_forward(name):
        p = pieces[name]
        off = w.yoff if p[3] == "x" else w.xoff
        half = p[2] // 2
        a, b = flying[name]
        a.wait_recv()
        ref = many(p, -1, p[1], half)
        a2 = net.go(ref, ref, off(1))
        b.wait_recv()
        ref = many(p, 1, p[1] + half, half)
        flying[name] = [a2, net.go(ref, ref, off(-1))]

    direct = []

    def shard_direct(q):
        own = tab.at[0, q]
        direct.append((net.go(own, tab.at[7, q], w.zoff(1)), net.go(own, tab.at[1, q], w.zoff(-1))))

    hop = {}

    def pump1():
        r1.wait_recv()
        hop["r"] = net.go(zb.at[1], tab.at[6, px, py], w.zoff(1))
        l1.wait_recv()
        hop["l"] = net.go(zb.at[0], tab.at[2, px, py], w.zoff(-1))
        shard_direct(0)

    def pump2():
        hop["r"].wait_recv()
        hop["r"] = net.go(tab.at[6, px, py], tab.at[5, px, py], w.zoff(1))
        hop["l"].wait_recv()
        hop["l"] = net.go(tab.at[2, px, py], tab.at[3, px, py], w.zoff(-1))
        first_send(6)
        first_send(2)
        shard_direct(1)

    def pump3():
        hop["r"].wait_recv()
        hop["r"] = net.go(tab.at[5, px, py], tab.at[4, px, py], w.zoff(1))
        hop["l"].wait_recv()
        first_send(5)
        first_send(3)
        first_forward(6)
        first_forward(2)
        shard_direct(2)
        shard_direct(3)

    def pump4():
        hop["r"].wait_recv()
        first_send("4x")
        first_send("4y")
        first_forward(5)
        first_forward(3)
        second_send(6)
        second_send(2)

    def pump5():
        first_forward("4x")
        first_forward("4y")
        second_send(5)
        second_send(3)

    def pump6():
        second_forward(6)
        second_forward(2)
        second_send("4x")
        second_send("4y")

    def pump7():
        second_forward(5)
        second_forward(3)

    def pump8():
        second_forward("4x")
        second_forward("4y")

    ends = []
    for j in range(16):
        ends.append(len_s[0, j] + (ends[-1] if ends else 0))
    tc, tr = iota((T, 128), 0), iota((8, T), 1)
    uid_c, uid_r = jnp.zeros((T, 128), I32), jnp.zeros((8, T), I32)
    for end in ends:
        uid_c = uid_c + (tc >= end).astype(I32)
        uid_r = uid_r + (tr >= end).astype(I32)
    same = (uid_c[:, :1] == uid_r[:1, :]) & (iota((T, T), 1) <= iota((T, T), 0))
    mask_v[...] = same.astype(F32)

    loads[1].wait()

    def norm_in(i):
        v = x_v[ds(i, 32)].astype(F32)
        v = v - jnp.mean(v, -1, keepdims=True)
        nin[ds(i, 32)] = (v * lax.rsqrt(jnp.mean(v * v, -1, keepdims=True) + EPS)).astype(BF)

    rep(8, norm_in)
    pump1()
    loads[2].wait()
    loads[3].wait()

    def project(i):
        pre = mm(nin[...], win[:, ds(i, 256)])
        sg = sigmoid(pre)
        proj[:, ds(i, 256)] = (pre * sg).astype(BF)
        slope[:, ds(i, 256)] = sg * (1.0 + pre * (1.0 - sg))

    rep(4, project)
    pump2()
    rep(4, lambda i: project(i + 4))
    pump3()

    def flip_in(i):
        block = nin[:, ds(i, 128)].astype(F32).T
        ninT[i] = block.astype(BF).reshape(2, 64, T)

    def attend(h):
        col = lambda part: pl.ds(pl.multiple_of(part * HID + h * 128, 128), 128)
        scores = mm_t(proj[:, col(2)], proj[:, col(3)]) * SCALE
        sg = sigmoid(scores)
        mask = mask_v[...]
        weight = (scores * sg * mask).astype(BF)
        attn[h] = weight
        dsl[h] = sg * (1.0 + scores * (1.0 - sg)) * SCALE * mask
        att[:, ds(h, 128)] = mm(weight, proj[:, col(1)])

    rep(2, attend)
    pump4()
    rep(2, lambda h: attend(h + 2))

    def norm_att(i):
        v = att[ds(i, 32)]
        v = v - jnp.mean(v, -1, keepdims=True)
        f = lax.rsqrt(jnp.mean(v * v, -1, keepdims=True) + EPS)
        n = v * f
        normed[ds(i, 32)] = n
        inv[ds(i, 32)] = jnp.broadcast_to(f, (32, 128))
        gated[ds(i, 32)] = (n * proj[ds(i, 32), pl.ds(0, HID)].astype(F32)).astype(BF)

    rep(8, norm_att)
    pump5()

    def result(i):
        res[:, ds(i, 256)] = x_v[:, ds(i, 256)].astype(F32) + mm_t(gated[...], wout[ds(i, 256)])

    rep(4, result)

    def norm_out(i):
        v = res[ds(i, 32)]
        f = lax.rsqrt(jnp.sum(v * v, -1, keepdims=True) + EPS)
        rlen[ds(i, 32)] = jnp.broadcast_to(f, (32, 128))
        yall[0, ds(i, 32)] = (v * f).astype(BF)
        lay_o[ds(i, 32)] = v.astype(BF)

    rep(8, norm_out)
    cp_y = net.go(yall.at[0], ymate, w.mate())
    yr = net.go(yall.at[0], yall.at[7], w.zoff(1))
    yl = net.go(yall.at[0], yall.at[1], w.zoff(-1))
    pump6()
    rep(8, flip_in)
    cp_nin = net.go(ninT.at[:, 1 - c], ninTm, w.mate())
    cp_gated = net.go(gated, gatedm, w.mate())
    pump7()

    lacc[...] = jnp.zeros_like(lacc)
    cp_cand.wait_recv()
    cp_y.wait_recv()

    def base(dz):
        return (((z + dz) % 8) * 2 + c) * 512

    def score(dz):
        shard = tab[dz].reshape(512, D)
        lbuf[pl.ds(0, T)] = mm_t(yall[0], shard)
        lbuf[pl.ds(T, T)] = mm_t(ymate[...], shard)
        v0 = base(dz)

        def pick(i):
            line = lbuf[ds(i, 32)]
            ids = iota((32, 512), 1) + v0
            who = cand[ds(i, 32)]
            for k in range(NCAND):
                got = jnp.where(who[:, k:k + 1] == ids, line, 0.0)
                lacc[k, ds(i, 32)] += got[:, :128] + got[:, 128:256] + got[:, 256:384] + got[:, 384:]

        rep(16, pick)

    score(0)
    pump8()
    yr.wait_recv()
    yr2 = net.go(yall.at[7], yall.at[6], w.zoff(1))
    yl.wait_recv()
    yl2 = net.go(yall.at[1], yall.at[2], w.zoff(-1))
    for a, b in direct:
        a.wait_recv()
        b.wait_recv()
    score(1)
    score(7)

    def settle(name):
        for copy in flying[name]:
            copy.wait_recv()

    settle(6)
    score(6)
    settle(2)
    score(2)
    settle(5)
    score(5)
    settle(3)
    score(3)
    yr2.wait_recv()
    yr3 = net.go(yall.at[6], yall.at[5], w.zoff(1))
    yl2.wait_recv()
    yl3 = net.go(yall.at[2], yall.at[3], w.zoff(-1))
    settle("4x")
    settle("4y")
    score(4)

    lane = iota((2 * T, 128), 1)
    total = jnp.zeros((2 * T, 128), F32)
    for k in range(NCAND):
        total = jnp.where(lane == k, jnp.sum(lacc[k], -1, keepdims=True), total)
    lsum[...] = total
    cp_l = net.go(lsum, lrec, w.mate())
    cp_l.wait_recv()
    lrec_v = lrec[...]
    logits = (lsum[...] + jnp.concatenate([lrec_v[T:], lrec_v[:T]], 0)) / TEMP
    live = lane < NCAND
    ex = jnp.where(live, jnp.exp(jnp.where(live, logits, 0.0)), 0.0)
    soft = ex / jnp.sum(ex, -1, keepdims=True)
    gcol[...] = jnp.where(live, soft - (lane == 0).astype(F32), 0.0) / TEMP

    gsend[...] = gcol[pl.ds(0, T)].T[:8]
    gall[0] = gsend[...]
    cp_g = [net.go(gsend, gall.at[8 - k], w.zoff(k)) for k in range(1, 8)]

    def spread(i):
        dz, j = i // 16, i % 16
        ids = iota((32, 512), 1) + base(dz)
        who, how = cand[ds(j, 32)], gcol[ds(j, 32)]
        out = jnp.zeros((32, 512), F32)
        for k in range(NCAND):
            out = out + jnp.where(who[:, k:k + 1] == ids, how[:, k:k + 1], 0.0)
        sfull[ds(j, 32), ds(dz, 512)] = out.astype(BF)

    rep(128, spread)

    def gather_mate(i):
        rows = tab[:, :, :, :, ds(i, 256)].reshape(4096, 256)
        wsend[:, ds(i, 256)] = mm(sfull[pl.ds(T, T)], rows).astype(BF)

    rep(4, gather_mate)
    cp_w = net.go(wsend, wrec, w.mate())

    def gather_own(i):
        rows = tab[:, :, :, :, ds(i, 256)].reshape(4096, 256)
        wown[:, ds(i, 256)] = mm(sfull[pl.ds(0, T)], rows)

    rep(4, gather_own)
    yr3.wait_recv()
    half = D // 2
    yr4 = net.go(yall.at[5, :, pl.ds(0, half)], yall.at[4, :, pl.ds(0, half)], w.zoff(1))
    yl3.wait_recv()
    yl4 = net.go(yall.at[3, :, pl.ds(half, half)], yall.at[4, :, pl.ds(half, half)], w.zoff(-1))
    cp_w.wait_recv()

    def upstream(i):
        f = rlen[ds(i, 32)][:, :1]
        yn = res[ds(i, 32)] * f
        v = wown[ds(i, 32)] + wrec[ds(i, 32)].astype(F32)
        up = (v - yn * jnp.sum(yn * v, -1, keepdims=True)) * f
        upb[ds(i, 32)] = up.astype(BF)

    rep(8, upstream)

    gg[...] = mm(upb[...], wout[...])

    def back_norm(i):
        n, v = normed[ds(i, 32)], gg[ds(i, 32)]
        gpre[ds(i, 32), pl.ds(0, HID)] = (v * n * slope[ds(i, 32), pl.ds(0, HID)]).astype(BF)
        v = v * proj[ds(i, 32), pl.ds(0, HID)].astype(F32)
        v = v - jnp.mean(v, -1, keepdims=True) - n * jnp.mean(v * n, -1, keepdims=True)
        gatt[ds(i, 32)] = (inv[ds(i, 32)][:, :1] * v).astype(BF)

    rep(8, back_norm)

    def flip_up(i):
        block = upb[:, ds(i, 128)].astype(F32).T
        upT[i] = block.astype(BF).reshape(2, 64, T)

    rep(8, flip_up)
    cp_up = net.go(upT.at[:, 1 - c], upTm, w.mate())

    def back_attend(h):
        col = lambda part: pl.ds(pl.multiple_of(part * HID + h * 128, 128), 128)
        da = gatt[:, ds(h, 128)]
        ds_ = (mm_t(da, proj[:, col(1)]) * dsl[h])
        gv = mm(attn[h].astype(F32).T.astype(BF), da)
        gq = mm(ds_.astype(BF), proj[:, col(3)])
        gk = mm(ds_.T.astype(BF), proj[:, col(2)])
        gpre[:, col(1)] = (gv * slope[:, col(1)]).astype(BF)
        gpre[:, col(2)] = (gq * slope[:, col(2)]).astype(BF)
        gpre[:, col(3)] = (gk * slope[:, col(3)]).astype(BF)

    rep(4, back_attend)
    cp_pre = net.go(gpre, gprem, w.mate())

    def store_g(i, first, block):
        for b in range(block.shape[1] // 128):
            n = first + b
            g_o[n // 5, pl.ds(i * 4, 4), :, pl.ds((n % 5) * 128, 128)] = (
                block[:, b * 128:(b + 1) * 128].astype(BF).reshape(4, 64, 128))

    cp_gated.wait_recv()
    cp_up.wait_recv()

    def grad_out(i):
        a = upT[pl.ds(i * 4, 4), c].reshape(T, T)
        b = upTm[pl.ds(i * 4, 4)].reshape(T, T)
        store_g(i, 16, mm(a, gated[...]) + mm(b, gatedm[...]))

    rep(2, grad_out)
    cp_nin.wait_recv()
    cp_pre.wait_recv()

    def grad_in(i):
        a = ninT[pl.ds(i * 4, 4), c].reshape(T, T)
        b = ninTm[pl.ds(i * 4, 4)].reshape(T, T)
        for n in range(4):
            cols = pl.ds(n * 512, 512)
            store_g(i, n * 4, mm(a, gpre[:, cols]) + mm(b, gprem[:, cols]))

    rep(2, grad_in)

    for copy in cp_rows + cp_g:
        copy.wait_recv()

    def spread_t(i):
        dz, j = i // 8, i % 8
        ids = iota((128, T), 0) + (z * 1024 + j * 128)
        who, how = rall[dz], gall[dz]
        out = jnp.zeros((128, T), F32)
        for k in range(NCAND):
            out = out + jnp.where(who[k:k + 1, :] == ids, how[k:k + 1, :], 0.0)
        st[ds(j, 128), ds(dz, T)] = out.astype(BF)

    rep(64, spread_t)
    yr4.wait_recv()
    yl4.wait_recv()

    def h_mate(i):
        y = yall[:, :, ds(i, 256)].reshape(8 * T, 256)
        hsend[:, ds(i, 256)] = mm(st[ds(1 - c, 512)], y).astype(BF)

    rep(4, h_mate)
    cp_h = net.go(hsend, hrec, w.mate())

    def h_own(i):
        y = yall[:, :, ds(i, 256)].reshape(8 * T, 256)
        lbuf[:, pl.ds(0, 256)] = mm(st[ds(c, 512)], y)
        h_o[:, ds(i, 256)] = lbuf[:, pl.ds(0, 256)].astype(BF)

    rep(4, h_own)
    cp_h.wait_recv()

    def h_add(i):
        h_o[ds(i, 32)] = (h_o[ds(i, 32)].astype(F32) + hrec[ds(i, 32)].astype(F32)).astype(BF)

    rep(16, h_add)
    net.drain()


def train_call(lengths, cols, rows, events, in_weight, out_weight, item_table):
    vm = lambda *shape, dtype=BF: pltpu.VMEM(shape, dtype)
    scratch = [
        vm(T, D), vm(D, 4 * HID), vm(D, HID), vm(512, D), vm(8, 4, 4, 32, D), vm(2, 32, D), vm(T, D),
        vm(T, 4 * HID, dtype=F32), vm(T, 4 * HID), vm(HEADS, T, T), vm(HEADS, T, T, dtype=F32),
        vm(T, HID, dtype=F32), vm(T, HID, dtype=F32), vm(T, 128, dtype=F32), vm(T, HID), vm(T, HID),
        vm(T, D, dtype=F32), vm(T, 128, dtype=F32), vm(8, T, D), vm(T, D), vm(2 * T, 128, dtype=I32),
        vm(8, 8, T, dtype=I32), vm(8, 8, T, dtype=F32), vm(8, T, dtype=F32), vm(2 * T, 512, dtype=F32),
        vm(NCAND, 2 * T, 128, dtype=F32), vm(2 * T, 128, dtype=F32), vm(2 * T, 128, dtype=F32),
        vm(2 * T, 128, dtype=F32), vm(2 * T, 4096), vm(T, D, dtype=F32), vm(T, D), vm(T, D), vm(T, D),
        vm(T, HID, dtype=F32), vm(T, HID), vm(T, 4 * HID), vm(T, 4 * HID), vm(8, 2, 64, T), vm(8, 64, T),
        vm(8, 2, 64, T), vm(8, 64, T), vm(1024, 8 * T), vm(512, D), vm(512, D), vm(T, T, dtype=F32),
        pltpu.SemaphoreType.DMA((4,)), pltpu.SemaphoreType.DMA((NSEM1,)), pltpu.SemaphoreType.DMA((NSEM1,)),
    ]
    any_ = pl.BlockSpec(memory_space=pl.ANY)
    vmem = pl.BlockSpec(memory_space=pltpu.VMEM)
    return pl.pallas_call(
        train_kernel,
        out_shape=(jax.ShapeDtypeStruct((T, D), BF), jax.ShapeDtypeStruct((4, 8, 64, 640), BF),
                   jax.ShapeDtypeStruct((512, D), BF)),
        in_specs=[pl.BlockSpec(memory_space=pltpu.SMEM), vmem, vmem, any_, any_, any_, any_],
        out_specs=(vmem, vmem, vmem),
        scratch_shapes=scratch,
        compiler_params=pltpu.CompilerParams(collective_id=0, has_side_effects=True, vmem_limit_bytes=VMEM_BYTES),
        name="train",
    )(lengths, cols, rows, events, in_weight, out_weight, item_table)


class Ring:
    def __init__(self, net, off, i, src, bufs, out):
        self.net, self.off, self.i, self.src, self.out = net, off, i, src, out
        self.t, self.u, self.v, self.r = bufs

    def start(self):
        far, right, left = (self.i + 2) % 4, (self.i + 1) % 4, (self.i + 3) % 4
        go, off, src = self.net.go, self.off, self.src
        self.ct = [go(src(far, 0), self.t.at[0], off(1)), go(src(far, 1), self.t.at[1], off(-1))]
        self.cu = [go(src(left, 0), self.u.at[0], off(-1)), go(src(right, 1), self.u.at[1], off(1))]

    def relay(self):
        self.cr = []
        for k, j in ((0, (self.i + 1) % 4), (1, (self.i + 3) % 4)):
            self.ct[k].wait_recv()
            self.v[k] = (self.t[k].astype(F32) + self.src(j, k)[...].astype(F32)).astype(BF)
            self.cr.append(self.net.go(self.v.at[k], self.r.at[k], self.off(1 - 2 * k)))

    def finish(self):
        for k in range(2):
            self.cr[k].wait_recv()
            self.cu[k].wait_recv()
            total = self.src(self.i, k)[...].astype(F32) + self.r[k].astype(F32) + self.u[k].astype(F32)
            self.out(k)[...] = total.astype(BF)


NSEM2 = 128


def reduce_kernel(len_s, dst_s, res_v, g_v, h_v, lay_o, w_o, h_o,
                  *refs):
    (ga_b, gb_b, ha_b, hb_b, ga2_b, gb2_b, ha2_b, hb2_b) = [refs[4 * i:4 * i + 4] for i in range(8)]
    (a1, b1, ha1, hb1, piece, zbuf, wpiece, hpiece, wall, hall, slots_s, slots_r, csend, cbuf, ssem, rsem) = refs[32:]
    w = Where()
    net = Links(ssem, rsem)
    z, s, px, py = w.z, w.s, w.px, w.py
    plane = [(i, j) for i in range(4) for j in range(4) if (i, j) != (0, 0)]

    def peer(i, j):
        return w.at(grp=((px + i) % 4) * 4 + (py + j) % 4)

    for k in range(16):
        slots_r[k, pl.ds(24, 8)] = jnp.zeros((8, D), BF)
    lane = iota((8, 128), 1)
    counts = jnp.zeros((8, 128), F32)
    tr = iota((8, T), 1)
    place = jnp.zeros((8, T), I32)
    start = 0
    for j in range(16):
        n, d = len_s[0, j], dst_s[0, j]
        counts = counts + jnp.where(lane == d, n, 0).astype(F32)
        place = jnp.where((tr >= start) & (tr < start + n), d * 32 + tr - start, place)
        start = start + n
    csend[...] = counts
    greet([w.at(seq=(s + k) % 16) for k in range(1, 16)] + [peer(i, j) for i, j in plane])

    two = lambda k: pl.ds(2 * k, 2)
    cut = lambda k: pl.ds(256 * k, 256)
    hicut = lambda k: pl.ds(512 + 256 * k, 256)
    ga = Ring(net, w.xoff, px, lambda j, k: g_v.at[j, two(k)], ga_b, lambda k: a1.at[two(k)])
    gb = Ring(net, w.yoff, py, lambda j, k: g_v.at[:, pl.ds(4 + 2 * k, 2), j], gb_b, lambda k: b1.at[:, two(k)])
    ha = Ring(net, w.xoff, px, lambda j, k: h_v.at[j, :, :, cut(k)], ha_b, lambda k: ha1.at[:, :, cut(k)])
    hb = Ring(net, w.yoff, py, lambda j, k: h_v.at[:, j, :, hicut(k)], hb_b, lambda k: hb1.at[:, :, cut(k)])
    ga2 = Ring(net, w.yoff, py, lambda j, k: a1.at[two(k), j], ga2_b, lambda k: piece.at[two(k)])
    gb2 = Ring(net, w.xoff, px, lambda j, k: b1.at[j, two(k)], gb2_b, lambda k: piece.at[pl.ds(4 + 2 * k, 2)])
    ha2 = Ring(net, w.yoff, py, lambda j, k: ha1.at[j, :, cut(k)], ha2_b, lambda k: hpiece.at[:, cut(k)])
    hb2 = Ring(net, w.xoff, px, lambda j, k: hb1.at[j, :, cut(k)], hb2_b, lambda k: hpiece.at[:, hicut(k)])

    for ring in (ga, gb, ha, hb):
        ring.start()

    cp_count = [net.go(csend, cbuf.at[s], w.at(seq=(s + k) % 16)) for k in range(1, 16)]
    cbuf[s] = csend[...]

    def fill(i):
        pick = jnp.where(iota((128, T), 0) + i * 128 == place[:1, :], 1.0, 0.0).astype(BF)
        slots_s[pl.ds(i * 4, 4)] = mm(pick, res_v[...]).astype(BF).reshape(4, 32, D)

    rep(4, fill)
    used = pl.ds(0, 24)
    cp_slot = [net.go(slots_s.at[(s + k) % 16, used], slots_r.at[s, used], w.at(seq=(s + k) % 16))
               for k in range(1, 16)]
    slots_r[s, used] = slots_s[s, used]

    for ring in (ga, gb, ha, hb):
        ring.relay()
    for ring, after in ((ga, ga2), (gb, gb2), (ha, ha2), (hb, hb2)):
        ring.finish()
        after.start()
    for ring in (ga2, gb2, ha2, hb2):
        ring.relay()
    ga2.finish()
    gb2.finish()
    cp_z = [net.go(piece.at[(z + k) % 8], zbuf.at[k], w.zoff(k)) for k in range(1, 8)]
    ha2.finish()
    hb2.finish()
    cp_h = [net.go(hpiece, hall.at[px, py], peer(i, j)) for i, j in plane]
    hall[px, py] = hpiece[...]
    total = piece[z].astype(F32)
    for k in range(1, 8):
        cp_z[k - 1].wait_recv()
        total = total + zbuf[k].astype(F32)
    wpiece[...] = total.astype(BF)
    cp_w = [net.go(wpiece, wall.at[px, py], peer(i, j)) for i, j in plane]
    wall[px, py] = wpiece[...]

    for copy in cp_count + cp_slot:
        copy.wait_recv()
    cnt = jnp.sum(jnp.where(iota((16, 128), 1) == s, cbuf[:, 0, :], 0.0), -1, keepdims=True)
    row, col = iota((16, 512), 0), iota((16, 512), 1)
    slot = col >> 5
    before = jnp.sum(jnp.where(row < slot, cnt, 0.0), 0, keepdims=True)
    here = jnp.sum(jnp.where(row == slot, cnt, 0.0), 0, keepdims=True)
    inside = (col[:1] & 31).astype(F32)
    goal = jnp.where(inside < here, before + inside, -1.0)
    picks = jnp.where(iota((T, 512), 0).astype(F32) == goal, 1.0, 0.0).astype(BF)

    def land(i):
        lay_o[:, ds(i, 256)] = mm(picks, slots_r[:, :, ds(i, 256)].reshape(512, 256)).astype(BF)

    rep(4, land)
    for copy in cp_w:
        copy.wait_recv()
    w_o[...] = wall[...]
    for copy in cp_h:
        copy.wait_recv()
    h_o[...] = hall[...]
    net.drain()


def reduce_call(lengths, destinations, result, g, h):
    vm = lambda *shape, dtype=BF: pltpu.VMEM(shape, dtype)
    halves = [(2, 4, 16, 640), (4, 2, 16, 640), (4, 32, 256), (4, 32, 256), (2, 16, 640), (2, 16, 640), (32, 256), (32, 256)]
    scratch = [vm(2, *shape) for shape in halves for _ in range(4)] + [
        vm(4, 4, 16, 640), vm(4, 4, 16, 640), vm(4, 32, 512), vm(4, 32, 512), vm(8, 16, 640), vm(8, 16, 640),
        vm(16, 640), vm(32, D), vm(4, 4, 16, 640), vm(4, 4, 32, D), vm(16, 32, D), vm(16, 32, D),
        vm(8, 128, dtype=F32), vm(16, 8, 128, dtype=F32),
        pltpu.SemaphoreType.DMA((NSEM2,)), pltpu.SemaphoreType.DMA((NSEM2,)),
    ]
    vmem = pl.BlockSpec(memory_space=pltpu.VMEM)
    smem = pl.BlockSpec(memory_space=pltpu.SMEM)
    return pl.pallas_call(
        reduce_kernel,
        out_shape=(jax.ShapeDtypeStruct((T, D), BF), jax.ShapeDtypeStruct((4, 4, 16, 640), BF),
                   jax.ShapeDtypeStruct((4, 4, 32, D), BF)),
        in_specs=[smem, smem, vmem, vmem, vmem],
        out_specs=(vmem, vmem, vmem),
        scratch_shapes=scratch,
        compiler_params=pltpu.CompilerParams(collective_id=1, has_side_effects=True, vmem_limit_bytes=VMEM_BYTES),
        name="reduce",
    )(lengths, destinations, result, g.reshape(4, 8, 4, 16, 640), h.reshape(4, 4, 32, D))


def body(events, lengths, destinations, history, negatives, in_weight, out_weight, item_table):
    cands = jnp.concatenate([history[:, None], negatives], 1)
    cols = jnp.pad(cands, ((0, 0), (0, 124)))
    rows = jnp.pad(cands.T, ((0, 4), (0, 0)))
    result, g, h = train_call(lengths, cols, rows, events, in_weight, out_weight, item_table)
    layer_out, wsum, hsum = reduce_call(lengths, destinations, result, g, h)
    wsum = wsum.astype(F32).transpose(1, 2, 0, 3).reshape(64, 2560)
    e = item_table.astype(F32)
    inv = lax.rsqrt(jnp.sum(e * e, -1, keepdims=True) + EPS)
    en = e * inv
    hf = hsum.astype(F32).reshape(512, D)
    table_grad = (hf - en * jnp.sum(en * hf, -1, keepdims=True)) * inv
    return layer_out, wsum[:, :2048], wsum[:, 2048:], table_grad


def solution(mesh):
    return jax.shard_map(
        body,
        mesh=mesh,
        in_specs=(
            P(("grp", "seq"), None),
            P(("grp", "seq"), None),
            P(("grp", "seq"), None),
            P(("grp", "seq")),
            P(("grp", "seq"), None),
            P(),
            P(),
            P("seq", None),
        ),
        out_specs=(P(("grp", "seq"), None), P("seq", None), P("seq", None), P("seq", None)),
        check_vma=False,
    )
```

```python
import jax
import jax.numpy as jnp
from jax import lax
from jax.experimental import pallas as pl
from jax.experimental.pallas import tpu as pltpu
from jax.sharding import PartitionSpec as P

F32, BF, I32 = jnp.float32, jnp.bfloat16, jnp.int32
MESH = pl.DeviceIdType.MESH
T, D, HID = 256, 1024, 512
HEADS, HEAD_DIM, NCAND = 4, 128, 4
EPS = 1e-5
TEMP = 0.05
SCALE = HEAD_DIM ** -0.5
VMEM_BYTES = 64_000_000


def rep(n, body):
    def step(i, carry):
        body(i)
        return carry

    lax.fori_loop(0, n, step, 0)


def ds(i, size):
    return pl.ds(pl.multiple_of(i * size, size), size)


def iota(shape, dim):
    return lax.broadcasted_iota(I32, shape, dim)


def mm(a, b):
    return jnp.dot(a, b, preferred_element_type=F32)


def mm_t(a, b):
    return lax.dot_general(a, b, (((1,), (1,)), ((), ())), preferred_element_type=F32)


def sigmoid(v):
    return 1.0 / (1.0 + jnp.exp(-v))


class Where:
    def __init__(self):
        self.g, self.s = lax.axis_index("grp"), lax.axis_index("seq")
        self.px, self.py = self.g // 4, self.g % 4
        self.z, self.c = self.s // 2, self.s % 2

    def at(self, grp=None, seq=None):
        return {"grp": self.g if grp is None else grp, "seq": self.s if seq is None else seq}

    def zoff(self, k):
        return self.at(seq=((self.z + k) % 8) * 2 + self.c)

    def mate(self):
        return self.at(seq=self.z * 2 + 1 - self.c)

    def xoff(self, k):
        return self.at(grp=((self.px + k) % 4) * 4 + self.py)

    def yoff(self, k):
        return self.at(grp=self.px * 4 + (self.py + k) % 4)


class Links:
    def __init__(self, send, recv):
        self.send, self.recv, self.n, self.sent = send, recv, 0, []

    def go(self, src, dst, dev):
        copy = pltpu.make_async_remote_copy(
            src_ref=src, dst_ref=dst, send_sem=self.send.at[self.n], recv_sem=self.recv.at[self.n],
            device_id=dev, device_id_type=MESH)
        self.n += 1
        copy.start()
        self.sent.append(copy)
        return copy

    def drain(self):
        for copy in self.sent:
            copy.wait_send()


class Ring:
    def __init__(self, net, off, i, src, bufs, out):
        self.net, self.off, self.i, self.src, self.out = net, off, i, src, out
        self.t, self.u, self.v, self.r = bufs

    def start(self):
        far, right, left = (self.i + 2) % 4, (self.i + 1) % 4, (self.i + 3) % 4
        go, off, src = self.net.go, self.off, self.src
        self.ct = [go(src(far, 0), self.t.at[0], off(1)), go(src(far, 1), self.t.at[1], off(-1))]
        self.cu = [go(src(left, 0), self.u.at[0], off(-1)), go(src(right, 1), self.u.at[1], off(1))]

    def relay(self):
        self.cr = []
        for k, j in ((0, (self.i + 1) % 4), (1, (self.i + 3) % 4)):
            self.ct[k].wait_recv()
            self.v[k] = (self.t[k].astype(F32) + self.src(j, k)[...].astype(F32)).astype(BF)
            self.cr.append(self.net.go(self.v.at[k], self.r.at[k], self.off(1 - 2 * k)))

    def finish(self):
        for k in range(2):
            self.cr[k].wait_recv()
            self.cu[k].wait_recv()
            total = self.src(self.i, k)[...].astype(F32) + self.r[k].astype(F32) + self.u[k].astype(F32)
            self.out(k)[...] = total.astype(BF)


def greet(devices):
    barrier = pltpu.get_barrier_semaphore()
    for dev in devices:
        pl.semaphore_signal(barrier, inc=1, device_id=dev, device_id_type=MESH)
    pl.semaphore_wait(barrier, len(devices))


NSEM = 256


def train_kernel(len_s, dst_s, hist_v, neg_v, ev_h, win_h, wout_h, tab_h, lay_o, w_o, h_o, *refs):
    (x_v, win, wout, traw, tab, zb, nin, slope, proj, attn, dsl, att, normed, inv, gated, gatedm,
     res, rlen, yall, ymate, ids_f, cand, rall, gall, gsend, lbuf, lsum, lrec, gcol, whob, sfull,
     wown, wsend, wrec, upb, gg, gatt, gpre, gprem, ninT, ninTm, upT, upTm, hsend, hrec, mask_v, lout,
     g_v, h_v, a1, b1, ha1, hb1, piece, zbuf, wpiece, wall, hall, slots_s, slots_r, csend, cbuf,
     lsem, ssem, rsem) = refs[:len(refs) - 32]
    bufs = refs[len(refs) - 32:]
    (ga_b, gb_b, ha_b, hb_b, ga2_b, gb2_b, ha2_b, hb2_b) = [bufs[4 * i:4 * i + 4] for i in range(8)]
    w = Where()
    net = Links(ssem, rsem)
    s, z, c, px, py, g = w.s, w.z, w.c, w.px, w.py, w.g
    plane = [(i, j) for i in range(4) for j in range(4) if (i, j) != (0, 0)]

    def peer(i, j):
        return w.at(grp=((px + i) % 4) * 4 + (py + j) % 4)

    loads = [pltpu.make_async_copy(a, b, lsem.at[i]) for i, (a, b) in enumerate(
        ((tab_h, traw), (ev_h, x_v), (win_h, win), (wout_h, wout)))]
    for copy in loads:
        copy.start()
    for k in range(16):
        slots_r[k, pl.ds(24, 8)] = jnp.zeros((8, D), BF)
    greet([w.at(seq=(s + k) % 16) for k in range(1, 16)] + [peer(i, j) for i, j in plane])

    loads[0].wait()

    def norm_rows(i):
        j = (g + i) % 16
        rows = traw[ds(j, 32)].astype(F32)
        length = lax.rsqrt(jnp.sum(rows * rows, -1, keepdims=True) + EPS)
        tab[0, j // 4, j % 4] = (rows * length).astype(BF)

    norm_rows(0)
    r1 = net.go(tab.at[0, px, py], zb.at[1], w.zoff(1))
    l1 = net.go(tab.at[0, px, py], zb.at[0], w.zoff(-1))
    rep(15, lambda i: norm_rows(i + 1))

    ids_f[...] = jnp.full((128, T), -1.0, F32)
    ids_f[pl.ds(0, 1)] = hist_v[...].astype(F32)
    ids_f[pl.ds(1, 3)] = neg_v[...].astype(F32)
    rall[0] = ids_f[pl.ds(0, 8)].astype(I32)
    cand[pl.ds(0, T)] = ids_f[...].T.astype(I32)
    cp_cand = net.go(cand.at[pl.ds(0, T)], cand.at[pl.ds(T, T)], w.mate())

    pieces = {6: (6, 0, 1024, "y"), 2: (2, 0, 1024, "x"), 5: (5, 0, 1024, "y"), 3: (3, 0, 1024, "x"),
              "4x": (4, 0, 512, "x"), "4y": (4, 512, 512, "y")}
    flying = {}

    def one(piece, kx, ky, c0, nc):
        return tab.at[piece[0], (px + kx) % 4, (py + ky) % 4, :, pl.ds(c0, nc)]

    def many(piece, k, c0, nc):
        if piece[3] == "x":
            return tab.at[piece[0], :, (py + k) % 4, :, pl.ds(c0, nc)]
        return tab.at[piece[0], (px + k) % 4, :, :, pl.ds(c0, nc)]

    def first_send(name):
        p = pieces[name]
        off = w.xoff if p[3] == "x" else w.yoff
        own = one(p, 0, 0, p[1], p[2])
        flying[name] = [net.go(own, own, off(1)), net.go(own, own, off(-1))]

    def first_forward(name):
        p = pieces[name]
        off = w.xoff if p[3] == "x" else w.yoff
        half = p[2] // 2
        a, b = flying[name]
        at = (lambda k, c0: one(p, k, 0, c0, half)) if p[3] == "x" else (lambda k, c0: one(p, 0, k, c0, half))
        a.wait_recv()
        ref = at(-1, p[1])
        a2 = net.go(ref, ref, off(1))
        b.wait_recv()
        ref = at(1, p[1] + half)
        flying[name] = [a2, net.go(ref, ref, off(-1))]

    def second_send(name):
        p = pieces[name]
        off = w.yoff if p[3] == "x" else w.xoff
        for copy in flying[name]:
            copy.wait_recv()
        own = many(p, 0, p[1], p[2])
        flying[name] = [net.go(own, own, off(1)), net.go(own, own, off(-1))]

    def second_forward(name):
        p = pieces[name]
        off = w.yoff if p[3] == "x" else w.xoff
        half = p[2] // 2
        a, b = flying[name]
        a.wait_recv()
        ref = many(p, -1, p[1], half)
        a2 = net.go(ref, ref, off(1))
        b.wait_recv()
        ref = many(p, 1, p[1] + half, half)
        flying[name] = [a2, net.go(ref, ref, off(-1))]

    direct = []

    def shard_direct(q):
        own = tab.at[0, q]
        direct.append((net.go(own, tab.at[7, q], w.zoff(1)), net.go(own, tab.at[1, q], w.zoff(-1))))

    hop = {}

    def pump1():
        r1.wait_recv()
        hop["r"] = net.go(zb.at[1], tab.at[6, px, py], w.zoff(1))
        l1.wait_recv()
        hop["l"] = net.go(zb.at[0], tab.at[2, px, py], w.zoff(-1))

    def pump2():
        hop["r"].wait_recv()
        hop["r"] = net.go(tab.at[6, px, py], tab.at[5, px, py], w.zoff(1))
        hop["l"].wait_recv()
        hop["l"] = net.go(tab.at[2, px, py], tab.at[3, px, py], w.zoff(-1))
        first_send(6)
        first_send(2)

    def pump3():
        hop["r"].wait_recv()
        hop["r"] = net.go(tab.at[5, px, py], tab.at[4, px, py], w.zoff(1))
        hop["l"].wait_recv()
        first_send(5)
        first_send(3)
        for q in range(4):
            shard_direct(q)

    def pump4():
        first_forward(6)
        first_forward(2)

    def pump5():
        hop["r"].wait_recv()
        first_send("4x")
        first_send("4y")
        first_forward(5)
        first_forward(3)
        second_send(6)
        second_send(2)

    def pump6():
        first_forward("4x")
        first_forward("4y")
        second_send(5)
        second_send(3)

    def pump7():
        second_send("4x")
        second_send("4y")
        second_forward(6)
        second_forward(2)

    def pump8():
        second_forward(5)
        second_forward(3)

    def pump9():
        second_forward("4x")
        second_forward("4y")

    ends = []
    for j in range(16):
        ends.append(len_s[0, j] + (ends[-1] if ends else 0))
    tc, tr = iota((T, 128), 0), iota((8, T), 1)
    uid_c, uid_r = jnp.zeros((T, 128), I32), jnp.zeros((8, T), I32)
    for end in ends:
        uid_c = uid_c + (tc >= end).astype(I32)
        uid_r = uid_r + (tr >= end).astype(I32)
    same = (uid_c[:, :1] == uid_r[:1, :]) & (iota((T, T), 1) <= iota((T, T), 0))
    mask_v[...] = same.astype(F32)

    loads[1].wait()

    def norm_in(i):
        v = x_v[ds(i, 32)].astype(F32)
        v = v - jnp.mean(v, -1, keepdims=True)
        nin[ds(i, 32)] = (v * lax.rsqrt(jnp.mean(v * v, -1, keepdims=True) + EPS)).astype(BF)

    rep(8, norm_in)
    pump1()
    loads[2].wait()
    loads[3].wait()

    def project(i):
        pre = mm(nin[...], win[:, ds(i, 256)])
        sg = sigmoid(pre)
        proj[:, ds(i, 256)] = (pre * sg).astype(BF)
        slope[:, ds(i, 256)] = sg * (1.0 + pre * (1.0 - sg))

    rep(4, project)
    pump2()
    rep(4, lambda i: project(i + 4))
    pump3()

    def flip_in(i):
        block = nin[:, ds(i, 128)].astype(F32).T
        ninT[i] = block.astype(BF).reshape(2, 64, T)

    def attend(h):
        col = lambda part: pl.ds(pl.multiple_of(part * HID + h * 128, 128), 128)
        scores = mm_t(proj[:, col(2)], proj[:, col(3)]) * SCALE
        sg = sigmoid(scores)
        mask = mask_v[...]
        weight = (scores * sg * mask).astype(BF)
        attn[h] = weight
        dsl[h] = sg * (1.0 + scores * (1.0 - sg)) * SCALE * mask
        att[:, ds(h, 128)] = mm(weight, proj[:, col(1)])

    rep(2, attend)
    rep(2, lambda h: attend(h + 2))
    pump4()

    def norm_att(i):
        v = att[ds(i, 32)]
        v = v - jnp.mean(v, -1, keepdims=True)
        f = lax.rsqrt(jnp.mean(v * v, -1, keepdims=True) + EPS)
        n = v * f
        normed[ds(i, 32)] = n
        inv[ds(i, 32)] = jnp.broadcast_to(f, (32, 128))
        gated[ds(i, 32)] = (n * proj[ds(i, 32), pl.ds(0, HID)].astype(F32)).astype(BF)

    rep(8, norm_att)
    pump5()

    def result(i):
        res[:, ds(i, 256)] = x_v[:, ds(i, 256)].astype(F32) + mm_t(gated[...], wout[ds(i, 256)])

    rep(4, result)

    def norm_out(i):
        v = res[ds(i, 32)]
        f = lax.rsqrt(jnp.sum(v * v, -1, keepdims=True) + EPS)
        rlen[ds(i, 32)] = jnp.broadcast_to(f, (32, 128))
        yall[0, ds(i, 32)] = (v * f).astype(BF)
        lout[ds(i, 32)] = v.astype(BF)

    rep(8, norm_out)
    cp_y = net.go(yall.at[0], ymate, w.mate())
    yr = net.go(yall.at[0], yall.at[7], w.zoff(1))
    yl = net.go(yall.at[0], yall.at[1], w.zoff(-1))
    cp_rows = [net.go(rall.at[0], rall.at[8 - k], w.zoff(k)) for k in range(1, 8)]
    pump6()
    rep(8, flip_in)
    cp_nin = net.go(ninT.at[:, 1 - c], ninTm, w.mate())
    cp_gated = net.go(gated, gatedm, w.mate())

    lsum[...] = jnp.zeros_like(lsum)
    cp_cand.wait_recv()

    def owner(dz):
        return ((z + dz) % 8) * 2 + c

    def locate(i):
        dz, j = i // 8, i % 8
        who = cand[ds(j, 64)]
        spot = jnp.where((who >> 9) == owner(dz), (who & 511) + 1, 0).astype(F32)
        whob[dz, ds(j, 64)] = jnp.broadcast_to(jnp.sum(spot, -1, keepdims=True) - 1.0, (64, 128))

    rep(64, locate)
    cp_y.wait_recv()
    lanes = iota((64, 128), 1).astype(F32)

    def score(dz):
        shard = tab[dz].reshape(512, D)
        lbuf[pl.ds(0, T)] = mm_t(yall[0], shard)
        lbuf[pl.ds(T, T)] = mm_t(ymate[...], shard)

        def pick(i):
            who = whob[dz, ds(i, 64)]
            got = jnp.zeros((64, 128), F32)
            for q in range(4):
                got = got + jnp.where(who == lanes + 128.0 * q, lbuf[ds(i, 64), pl.ds(q * 128, 128)], 0.0)
            value = jnp.sum(got, -1, keepdims=True)
            lsum[ds(i, 64)] += jnp.where((cand[ds(i, 64)] >> 9) == owner(dz), value, 0.0)

        rep(8, pick)

    def settle(name):
        for copy in flying[name]:
            copy.wait_recv()

    score(0)
    pump7()
    yr.wait_recv()
    yr2 = net.go(yall.at[7], yall.at[6], w.zoff(1))
    yl.wait_recv()
    yl2 = net.go(yall.at[1], yall.at[2], w.zoff(-1))
    pump8()
    settle(6)
    score(6)
    settle(2)
    score(2)
    pump9()
    for a, b in direct:
        a.wait_recv()
        b.wait_recv()
    score(1)
    score(7)
    settle(5)
    score(5)
    settle(3)
    score(3)
    yr2.wait_recv()
    yr3 = net.go(yall.at[6], yall.at[5], w.zoff(1))
    yl2.wait_recv()
    yl3 = net.go(yall.at[2], yall.at[3], w.zoff(-1))
    settle("4x")
    settle("4y")
    score(4)

    lane = iota((2 * T, 128), 1)
    cp_l = net.go(lsum, lrec, w.mate())
    cp_l.wait_recv()
    lrec_v = lrec[...]
    logits = (lsum[...] + jnp.concatenate([lrec_v[T:], lrec_v[:T]], 0)) / TEMP
    live = lane < NCAND
    ex = jnp.where(live, jnp.exp(jnp.where(live, logits, 0.0)), 0.0)
    soft = ex / jnp.sum(ex, -1, keepdims=True)
    gcol[...] = jnp.where(live, soft - (lane == 0).astype(F32), 0.0) / TEMP

    gsend[...] = gcol[pl.ds(0, T)].T[:8]
    gall[0] = gsend[...]
    cp_g = [net.go(gsend, gall.at[8 - k], w.zoff(k)) for k in range(1, 8)]

    def spread(i):
        dz, j = i // 8, i % 8
        how = jnp.where((cand[ds(j, 64)] >> 9) == owner(dz), gcol[ds(j, 64)], 0.0)
        how = jnp.broadcast_to(jnp.sum(how, -1, keepdims=True), (64, 128))
        who = whob[dz, ds(j, 64)]
        for q in range(4):
            part = jnp.where(who == lanes + 128.0 * q, how, 0.0).astype(BF)
            sfull[ds(j, 64), ds(dz * 4 + q, 128)] = part

    rep(64, spread)

    def gather_mate(i):
        rows = tab[:, :, :, :, ds(i, 256)].reshape(4096, 256)
        wsend[:, ds(i, 256)] = mm(sfull[pl.ds(T, T)], rows).astype(BF)

    rep(4, gather_mate)
    cp_w = net.go(wsend, wrec, w.mate())

    def gather_own(i):
        rows = tab[:, :, :, :, ds(i, 256)].reshape(4096, 256)
        wown[:, ds(i, 256)] = mm(sfull[pl.ds(0, T)], rows)

    rep(4, gather_own)
    yr3.wait_recv()
    half = D // 2
    yr4 = net.go(yall.at[5, :, pl.ds(0, half)], yall.at[4, :, pl.ds(0, half)], w.zoff(1))
    yl3.wait_recv()
    yl4 = net.go(yall.at[3, :, pl.ds(half, half)], yall.at[4, :, pl.ds(half, half)], w.zoff(-1))
    cp_w.wait_recv()

    def upstream(i):
        f = rlen[ds(i, 32)][:, :1]
        yn = res[ds(i, 32)] * f
        v = wown[ds(i, 32)] + wrec[ds(i, 32)].astype(F32)
        up = (v - yn * jnp.sum(yn * v, -1, keepdims=True)) * f
        upb[ds(i, 32)] = up.astype(BF)

    rep(8, upstream)

    gg[...] = mm(upb[...], wout[...])

    def back_norm(i):
        n, v = normed[ds(i, 32)], gg[ds(i, 32)]
        gpre[ds(i, 32), pl.ds(0, HID)] = (v * n * slope[ds(i, 32), pl.ds(0, HID)]).astype(BF)
        v = v * proj[ds(i, 32), pl.ds(0, HID)].astype(F32)
        v = v - jnp.mean(v, -1, keepdims=True) - n * jnp.mean(v * n, -1, keepdims=True)
        gatt[ds(i, 32)] = (inv[ds(i, 32)][:, :1] * v).astype(BF)

    rep(8, back_norm)

    def flip_up(i):
        block = upb[:, ds(i, 128)].astype(F32).T
        upT[i] = block.astype(BF).reshape(2, 64, T)

    rep(8, flip_up)
    cp_up = net.go(upT.at[:, 1 - c], upTm, w.mate())

    def back_attend(h):
        col = lambda part: pl.ds(pl.multiple_of(part * HID + h * 128, 128), 128)
        da = gatt[:, ds(h, 128)]
        ds_ = (mm_t(da, proj[:, col(1)]) * dsl[h])
        gv = mm(attn[h].astype(F32).T.astype(BF), da)
        gq = mm(ds_.astype(BF), proj[:, col(3)])
        gk = mm(ds_.T.astype(BF), proj[:, col(2)])
        gpre[:, col(1)] = (gv * slope[:, col(1)]).astype(BF)
        gpre[:, col(2)] = (gq * slope[:, col(2)]).astype(BF)
        gpre[:, col(3)] = (gk * slope[:, col(3)]).astype(BF)

    rep(4, back_attend)
    cp_pre = net.go(gpre, gprem, w.mate())

    def store_g(i, first, block):
        for b in range(block.shape[1] // 128):
            n = first + b
            g_v[n // 5, pl.ds(i * 4, 4), :, :, pl.ds((n % 5) * 128, 128)] = (
                block[:, b * 128:(b + 1) * 128].astype(BF).reshape(4, 4, 16, 128))

    cp_gated.wait_recv()
    cp_up.wait_recv()

    def grad_out(i):
        a = upT[pl.ds(i * 4, 4), c].reshape(T, T)
        b = upTm[pl.ds(i * 4, 4)].reshape(T, T)
        store_g(i, 16, mm(a, gated[...]) + mm(b, gatedm[...]))

    rep(2, grad_out)
    cp_nin.wait_recv()
    cp_pre.wait_recv()

    def grad_in(i):
        a = ninT[pl.ds(i * 4, 4), c].reshape(T, T)
        b = ninTm[pl.ds(i * 4, 4)].reshape(T, T)
        for n in range(4):
            cols = pl.ds(n * 512, 512)
            store_g(i, n * 4, mm(a, gpre[:, cols]) + mm(b, gprem[:, cols]))

    rep(2, grad_in)

    two = lambda k: pl.ds(2 * k, 2)
    cut = lambda k: pl.ds(256 * k, 256)
    hicut = lambda k: pl.ds(512 + 256 * k, 256)
    ga = Ring(net, w.xoff, px, lambda j, k: g_v.at[j, two(k)], ga_b, lambda k: a1.at[two(k)])
    gb = Ring(net, w.yoff, py, lambda j, k: g_v.at[:, pl.ds(4 + 2 * k, 2), j], gb_b, lambda k: b1.at[:, two(k)])
    ha = Ring(net, w.xoff, px, lambda j, k: h_v.at[j, :, :, cut(k)], ha_b, lambda k: ha1.at[:, :, cut(k)])
    hb = Ring(net, w.yoff, py, lambda j, k: h_v.at[:, j, :, hicut(k)], hb_b, lambda k: hb1.at[:, :, cut(k)])
    ga2 = Ring(net, w.yoff, py, lambda j, k: a1.at[two(k), j], ga2_b, lambda k: piece.at[two(k)])
    gb2 = Ring(net, w.xoff, px, lambda j, k: b1.at[j, two(k)], gb2_b, lambda k: piece.at[pl.ds(4 + 2 * k, 2)])
    mine = hall.at[px, py]
    ha2 = Ring(net, w.yoff, py, lambda j, k: ha1.at[j, :, cut(k)], ha2_b, lambda k: mine.at[:, cut(k)])
    hb2 = Ring(net, w.xoff, px, lambda j, k: hb1.at[j, :, cut(k)], hb2_b, lambda k: mine.at[:, hicut(k)])
    ga.start()
    gb.start()

    for copy in cp_rows + cp_g:
        copy.wait_recv()

    def spread_t(dz):
        who, how = rall[dz], gall[dz]
        for o in range(2):
            hit = (who >> 9) == z * 2 + o
            spot = jnp.sum(jnp.where(hit, (who & 511) + 1, 0).astype(F32), 0, keepdims=True) - 1.0
            much = jnp.sum(jnp.where(hit, how, 0.0), 0, keepdims=True)
            for j in range(4):
                line = (iota((128, T), 0) + j * 128).astype(F32)
                sfull[pl.ds(j * 128, 128), ds(dz + 8 * o, T)] = jnp.where(line == spot, much, 0.0).astype(BF)

    rep(8, spread_t)
    yr4.wait_recv()
    yl4.wait_recv()

    def h_mate(i):
        y = yall[:, :, ds(i, 256)].reshape(8 * T, 256)
        hsend[:, ds(i, 256)] = mm(sfull[:, ds(1 - c, 2048)], y).astype(BF)

    rep(4, h_mate)
    cp_h = net.go(hsend, hrec, w.mate())
    ga.relay()
    gb.relay()

    def h_own(i):
        y = yall[:, :, ds(i, 256)].reshape(8 * T, 256)
        lbuf[:, pl.ds(0, 256)] = mm(sfull[:, ds(c, 2048)], y)
        wown[:, ds(i, 256)] = lbuf[pl.ds(0, T), pl.ds(0, 256)]
        res[:, ds(i, 256)] = lbuf[pl.ds(T, T), pl.ds(0, 256)]

    rep(4, h_own)
    cp_h.wait_recv()
    for part, src in ((0, wown), (1, res)):
        for i in range(8):
            total = src[pl.ds(i * 32, 32)] + hrec[pl.ds(part * T + i * 32, 32)].astype(F32)
            h_v[part * 2 + i // 4, i % 4] = total.astype(BF)
    ha.start()
    hb.start()

    lane8 = iota((8, 128), 1)
    counts = jnp.zeros((8, 128), F32)
    place = jnp.zeros((8, T), I32)
    start = 0
    for j in range(16):
        n, d = len_s[0, j], dst_s[0, j]
        counts = counts + jnp.where(lane8 == d, n, 0).astype(F32)
        place = jnp.where((tr >= start) & (tr < start + n), d * 32 + tr - start, place)
        start = start + n
    csend[...] = counts
    cp_count = [net.go(csend, cbuf.at[s], w.at(seq=(s + k) % 16)) for k in range(1, 16)]
    cbuf[s] = csend[...]

    def fill(i):
        pick = jnp.where(iota((128, T), 0) + i * 128 == place[:1, :], 1.0, 0.0).astype(BF)
        slots_s[pl.ds(i * 4, 4)] = mm(pick, lout[...]).astype(BF).reshape(4, 32, D)

    rep(4, fill)
    used = pl.ds(0, 24)
    cp_slot = [net.go(slots_s.at[(s + k) % 16, used], slots_r.at[s, used], w.at(seq=(s + k) % 16))
               for k in range(1, 16)]
    slots_r[s, used] = slots_s[s, used]

    ga.finish()
    ga2.start()
    gb.finish()
    gb2.start()
    ha.relay()
    hb.relay()
    ga2.relay()
    gb2.relay()
    ha.finish()
    ha2.start()
    hb.finish()
    hb2.start()
    ga2.finish()
    gb2.finish()
    cp_z = [net.go(piece.at[(z + k) % 8], zbuf.at[k], w.zoff(k)) for k in range(1, 8)]
    ha2.relay()
    hb2.relay()
    total = piece[z].astype(F32)
    for k in range(1, 8):
        cp_z[k - 1].wait_recv()
        total = total + zbuf[k].astype(F32)
    wpiece[...] = total.astype(BF)
    cp_w = [net.go(wpiece, wall.at[px, py], peer(i, j)) for i, j in plane]
    wall[px, py] = wpiece[...]
    ha2.finish()
    hb2.finish()
    cp_ha = [net.go(mine, mine, peer(i, j)) for i, j in plane]

    for copy in cp_count + cp_slot:
        copy.wait_recv()
    cnt = jnp.sum(jnp.where(iota((16, 128), 1) == s, cbuf[:, 0, :], 0.0), -1, keepdims=True)
    row, col16 = iota((16, 512), 0), iota((16, 512), 1)
    slot = col16 >> 5
    before = jnp.sum(jnp.where(row < slot, cnt, 0.0), 0, keepdims=True)
    here = jnp.sum(jnp.where(row == slot, cnt, 0.0), 0, keepdims=True)
    inside = (col16[:1] & 31).astype(F32)
    goal = jnp.where(inside < here, before + inside, -1.0)
    picks = jnp.where(iota((T, 512), 0).astype(F32) == goal, 1.0, 0.0).astype(BF)

    def land(i):
        lay_o[:, ds(i, 256)] = mm(picks, slots_r[:, :, ds(i, 256)].reshape(512, 256)).astype(BF)

    rep(4, land)
    for copy in cp_w:
        copy.wait_recv()
    w_o[...] = wall[...]
    for copy in cp_ha:
        copy.wait_recv()
    h_o[...] = hall[...]
    net.drain()


def train_call(lengths, destinations, hist, neg, events, in_weight, out_weight, item_table):
    vm = lambda *shape, dtype=BF: pltpu.VMEM(shape, dtype)
    f32 = dict(dtype=F32)
    halves = [(2, 4, 16, 640), (4, 2, 16, 640), (4, 32, 256), (4, 32, 256), (2, 16, 640), (2, 16, 640), (32, 256), (32, 256)]
    sem = pltpu.SemaphoreType.DMA
    scratch = [
        vm(T, D), vm(D, 4 * HID), vm(D, HID), vm(512, D), vm(8, 4, 4, 32, D), vm(2, 32, D), vm(T, D),
        vm(T, 4 * HID, **f32), vm(T, 4 * HID), vm(HEADS, T, T), vm(HEADS, T, T, **f32),
        vm(T, HID, **f32), vm(T, HID, **f32), vm(T, 128, **f32), vm(T, HID), vm(T, HID),
        vm(T, D, **f32), vm(T, 128, **f32), vm(8, T, D), vm(T, D), vm(128, T, **f32), vm(2 * T, 128, dtype=I32),
        vm(8, 8, T, dtype=I32), vm(8, 8, T, **f32), vm(8, T, **f32), vm(2 * T, 512, **f32),
        vm(2 * T, 128, **f32), vm(2 * T, 128, **f32), vm(2 * T, 128, **f32), vm(8, 2 * T, 128, **f32),
        vm(2 * T, 4096), vm(T, D, **f32), vm(T, D), vm(T, D), vm(T, D),
        vm(T, HID, **f32), vm(T, HID), vm(T, 4 * HID), vm(T, 4 * HID), vm(8, 2, 64, T), vm(8, 64, T),
        vm(8, 2, 64, T), vm(8, 64, T), vm(512, D), vm(512, D), vm(T, T, **f32), vm(T, D),
        vm(4, 8, 4, 16, 640), vm(4, 4, 32, D),
        vm(4, 4, 16, 640), vm(4, 4, 16, 640), vm(4, 32, 512), vm(4, 32, 512), vm(8, 16, 640), vm(8, 16, 640),
        vm(16, 640), vm(4, 4, 16, 640), vm(4, 4, 32, D), vm(16, 32, D), vm(16, 32, D),
        vm(8, 128, **f32), vm(16, 8, 128, **f32),
        sem((4,)), sem((NSEM,)), sem((NSEM,)),
    ] + [vm(2, *shape) for shape in halves for _ in range(4)]
    any_ = pl.BlockSpec(memory_space=pl.ANY)
    vmem = pl.BlockSpec(memory_space=pltpu.VMEM)
    smem = pl.BlockSpec(memory_space=pltpu.SMEM)
    return pl.pallas_call(
        train_kernel,
        out_shape=(jax.ShapeDtypeStruct((T, D), BF), jax.ShapeDtypeStruct((4, 4, 16, 640), BF),
                   jax.ShapeDtypeStruct((4, 4, 32, D), BF)),
        in_specs=[smem, smem, vmem, vmem, any_, any_, any_, any_],
        out_specs=(vmem, vmem, vmem),
        scratch_shapes=scratch,
        compiler_params=pltpu.CompilerParams(collective_id=0, has_side_effects=True, vmem_limit_bytes=VMEM_BYTES),
        name="train",
    )(lengths, destinations, hist, neg, events, in_weight, out_weight, item_table)


def last_kernel(lay, w, h, e, lay_o, in_o, out_o, tab_o):
    lay_o[...] = lay[...]
    rows = jnp.concatenate([w[i, 0] for i in range(4)], 1).astype(F32)
    in_o[...] = rows[:, :4 * HID]
    out_o[...] = rows[:, 4 * HID:]
    item, total = e[...].astype(F32), h[0].reshape(128, D).astype(F32)
    length = lax.rsqrt(jnp.sum(item * item, -1, keepdims=True) + EPS)
    item = item * length
    tab_o[...] = (total - item * jnp.sum(item * total, -1, keepdims=True)) * length


def last_call(lay, w, h, item_table):
    rows = lambda n, m: pl.BlockSpec((n, m), lambda i: (i, 0))
    return pl.pallas_call(
        last_kernel,
        grid=(4,),
        out_shape=(jax.ShapeDtypeStruct((T, D), BF), jax.ShapeDtypeStruct((64, 4 * HID), F32),
                   jax.ShapeDtypeStruct((64, HID), F32), jax.ShapeDtypeStruct((512, D), F32)),
        in_specs=[rows(64, D), pl.BlockSpec((4, 1, 16, 640), lambda i: (0, i, 0, 0)),
                  pl.BlockSpec((1, 4, 32, D), lambda i: (i, 0, 0, 0)), rows(128, D)],
        out_specs=(rows(64, D), rows(16, 4 * HID), rows(16, HID), rows(128, D)),
        name="last",
    )(lay, w, h, item_table)


def body(events, lengths, destinations, history, negatives, in_weight, out_weight, item_table):
    result, wsum, hsum = train_call(lengths, destinations, history.reshape(1, T), negatives.T, events,
                                    in_weight, out_weight, item_table)
    return last_call(result, wsum, hsum, item_table)


def solution(mesh):
    return jax.shard_map(
        body,
        mesh=mesh,
        in_specs=(
            P(("grp", "seq"), None),
            P(("grp", "seq"), None),
            P(("grp", "seq"), None),
            P(("grp", "seq")),
            P(("grp", "seq"), None),
            P(),
            P(),
            P("seq", None),
        ),
        out_specs=(P(("grp", "seq"), None), P("seq", None), P("seq", None), P("seq", None)),
        check_vma=False,
    )
```

```python
import jax
import jax.numpy as jnp
from jax import lax
from jax.experimental import pallas as pl
from jax.experimental.pallas import tpu as pltpu
from jax.sharding import PartitionSpec as P

F32, BF, I32 = jnp.float32, jnp.bfloat16, jnp.int32
MESH = pl.DeviceIdType.MESH
T, D, HID = 256, 1024, 512
HEADS, HEAD_DIM, NCAND = 4, 128, 4
EPS = 1e-5
TEMP = 0.05
SCALE = HEAD_DIM ** -0.5
VMEM_BYTES = 67_000_000


def rep(n, body, unroll=1):
    def step(i, carry):
        body(i)
        return carry

    lax.fori_loop(0, n, step, 0, unroll=unroll)


def ds(i, size):
    return pl.ds(pl.multiple_of(i * size, size), size)


def iota(shape, dim):
    return lax.broadcasted_iota(I32, shape, dim)


def mm(a, b):
    return jnp.dot(a, b, preferred_element_type=F32)


def mm_t(a, b):
    return lax.dot_general(a, b, (((1,), (1,)), ((), ())), preferred_element_type=F32)


def sigmoid(v):
    return 1.0 / (1.0 + jnp.exp(-v))


class Where:
    def __init__(self):
        self.g, self.s = lax.axis_index("grp"), lax.axis_index("seq")
        self.px, self.py = self.g // 4, self.g % 4
        self.z, self.c = self.s // 2, self.s % 2

    def at(self, grp=None, seq=None):
        return {"grp": self.g if grp is None else grp, "seq": self.s if seq is None else seq}

    def zoff(self, k):
        return self.at(seq=((self.z + k) % 8) * 2 + self.c)

    def mate(self):
        return self.at(seq=self.z * 2 + 1 - self.c)

    def xoff(self, k):
        return self.at(grp=((self.px + k) % 4) * 4 + self.py)

    def yoff(self, k):
        return self.at(grp=self.px * 4 + (self.py + k) % 4)


class Links:
    def __init__(self, send, recv):
        self.send, self.recv, self.n, self.sent = send, recv, 0, []

    def describe(self, src, dst, dev):
        return pltpu.make_async_remote_copy(
            src_ref=src, dst_ref=dst, send_sem=self.send.at[self.n], recv_sem=self.recv.at[self.n],
            device_id=dev, device_id_type=MESH)

    def go(self, src, dst, dev):
        return self.bundle(dst, (src, dst, dev))

    def bundle(self, whole, *copies):
        for copy in copies:
            self.describe(*copy).start()
        wait = self.describe(whole, whole, copies[0][2])
        self.n += 1
        self.sent.append(wait)
        return wait

    def drain(self):
        for copy in self.sent:
            copy.wait_send()


class Ring:
    def __init__(self, net, off, i, src, bufs, out):
        self.net, self.off, self.i, self.src, self.out = net, off, i, src, out
        self.t, self.u, self.v, self.r = bufs

    def start(self):
        far, right, left = (self.i + 2) % 4, (self.i + 1) % 4, (self.i + 3) % 4
        off, src, t, u = self.off, self.src, self.t, self.u
        self.ct = self.net.bundle(t, (src(far, 0), t.at[0], off(1)), (src(far, 1), t.at[1], off(-1)))
        self.cu = self.net.bundle(u, (src(left, 0), u.at[0], off(-1)), (src(right, 1), u.at[1], off(1)))

    def relay(self):
        self.ct.wait_recv()
        for k, j in ((0, (self.i + 1) % 4), (1, (self.i + 3) % 4)):
            self.v[k] = (self.t[k].astype(F32) + self.src(j, k)[...].astype(F32)).astype(BF)
        v, r, off = self.v, self.r, self.off
        self.cr = self.net.bundle(r, (v.at[0], r.at[0], off(1)), (v.at[1], r.at[1], off(-1)))

    def finish(self):
        self.cr.wait_recv()
        self.cu.wait_recv()
        for k in range(2):
            total = self.src(self.i, k)[...].astype(F32) + self.r[k].astype(F32) + self.u[k].astype(F32)
            self.out(k)[...] = total.astype(BF)


def call_out(devices):
    barrier = pltpu.get_barrier_semaphore()
    for dev in devices:
        pl.semaphore_signal(barrier, inc=1, device_id=dev, device_id_type=MESH)
    return lambda: pl.semaphore_wait(barrier, len(devices))


NSEM = 88


def train_kernel(len_s, dst_s, hist_v, neg_v, ev_h, win_h, wout_h, tab_h, lay_o, w_o, h_o, *refs):
    (x_v, win, wout, traw, tab, nin, slope, proj, attn, dsl, att, normed, inv, gated, gatedm,
     res, rlen, yall, ymate, ids_f, cand, rall, gall, gsend, lacc, lsum, lrec, gcol, picks, found,
     wown, wsend, wrec, upb, gg, gatt, gpre, gprem, ninT, ninTm, upT, upTm, hsend, hrec, mask_v, lout,
     g_v, h_v, a1, b1, ha1, hb1, piece, zbuf, wpiece, wall, hall, slots_s, slots_r, csend, cbuf,
     lsem, ssem, rsem) = refs[:len(refs) - 32]
    bufs = refs[len(refs) - 32:]
    (ga_b, gb_b, ha_b, hb_b, ga2_b, gb2_b, ha2_b, hb2_b) = [bufs[4 * i:4 * i + 4] for i in range(8)]
    w = Where()
    net = Links(ssem, rsem)
    s, z, c, px, py, g = w.s, w.z, w.c, w.px, w.py, w.g
    plane = [(i, j) for i in range(4) for j in range(4) if (i, j) != (0, 0)]

    def peer(i, j):
        return w.at(grp=((px + i) % 4) * 4 + (py + j) % 4)

    loads = [pltpu.make_async_copy(a, b, lsem.at[i]) for i, (a, b) in enumerate(
        ((tab_h, traw), (ev_h, x_v), (win_h, win), (wout_h, wout)))]
    for copy in loads:
        copy.start()
    for k in range(16):
        slots_r[k, pl.ds(24, 8)] = jnp.zeros((8, D), BF)
    everyone = call_out([w.at(seq=(s + k) % 16) for k in range(1, 16)] + [peer(i, j) for i, j in plane])

    ids_f[...] = jnp.full((128, T), -1.0, F32)
    ids_f[pl.ds(0, 1)] = hist_v[...].astype(F32)
    ids_f[pl.ds(1, 3)] = neg_v[...].astype(F32)
    rall[0] = ids_f[pl.ds(0, 8)].astype(I32)
    cand[pl.ds(0, T)] = ids_f[...].T.astype(I32)

    loads[0].wait()

    def norm_rows(i):
        j = (g + i) % 16
        rows = traw[ds(j, 32)].astype(F32)
        length = lax.rsqrt(jnp.sum(rows * rows, -1, keepdims=True) + EPS)
        tab[0, j // 4, j % 4] = (rows * length).astype(BF)

    norm_rows(0)
    everyone()
    low, high = pl.ds(0, 512), pl.ds(512, 512)
    mine_at = lambda dz, cols: tab.at[dz, px, py, :, cols]
    slice_in = {(1, 7): net.bundle(
        tab.at[0, 0, pl.ds(0, 2), :, high],
        *[(mine_at(0, high), mine_at(8 - k, high), w.zoff(k)) for k in (1, 7)])}
    for a, b in ((2, 6), (3, 5)):
        slice_in[a, b] = net.bundle(
            tab.at[0, 0, pl.ds(0, 2)],
            *[(tab.at[0, px, py], tab.at[8 - k, px, py], w.zoff(k)) for k in (a, b)])
    rep(15, lambda i: norm_rows(i + 1))
    cp_cand = net.go(cand.at[pl.ds(0, T)], cand.at[pl.ds(T, T)], w.mate())

    pieces = {7: (tab.at[7], 512, 512, "y"), 1: (tab.at[1], 512, 512, "x"),
              6: (tab.at[6], 0, 1024, "y"), 2: (tab.at[2], 0, 1024, "x"),
              5: (tab.at[5], 0, 1024, "y"), 3: (tab.at[3], 0, 1024, "x"),
              "4x": (tab.at[4], 0, 512, "x"), "4y": (tab.at[4], 512, 512, "y"),
              "hx": (hall, 0, 512, "x"), "hy": (hall, 512, 512, "y")}
    flying = {}

    def one(piece, kx, ky, c0, nc):
        return piece[0].at[(px + kx) % 4, (py + ky) % 4, :, pl.ds(c0, nc)]

    def many(piece, k, c0, nc):
        if piece[3] == "x":
            return piece[0].at[:, (py + k) % 4, :, pl.ds(c0, nc)]
        return piece[0].at[(px + k) % 4, :, :, pl.ds(c0, nc)]

    def pair(name, whole, right, left, off):
        flying[name] = net.bundle(whole, (right, right, off(1)), (left, left, off(-1)))

    def first_send(name):
        p = pieces[name]
        own = one(p, 0, 0, p[1], p[2])
        pair(name, p[0].at[0, pl.ds(0, 2), :, pl.ds(p[1], p[2])], own, own, w.xoff if p[3] == "x" else w.yoff)

    def first_forward(name):
        p = pieces[name]
        half = p[2] // 2
        at = (lambda k, c0: one(p, k, 0, c0, half)) if p[3] == "x" else (lambda k, c0: one(p, 0, k, c0, half))
        flying[name].wait_recv()
        pair(name, one(p, 0, 0, p[1], p[2]), at(-1, p[1]), at(1, p[1] + half), w.xoff if p[3] == "x" else w.yoff)

    def second_send(name):
        p = pieces[name]
        flying[name].wait_recv()
        own = many(p, 0, p[1], p[2])
        pair(name, p[0].at[pl.ds(0, 2), :, :, pl.ds(p[1], p[2])], own, own, w.yoff if p[3] == "x" else w.xoff)

    def second_forward(name):
        p = pieces[name]
        half = p[2] // 2
        flying[name].wait_recv()
        pair(name, many(p, 0, p[1], p[2]), many(p, -1, p[1], half), many(p, 1, p[1] + half, half),
             w.yoff if p[3] == "x" else w.xoff)

    def step(stage, *names):
        for name in names:
            stage(name)

    def slices(a, b):
        slice_in[a, b].wait_recv()

    ends = []
    for j in range(16):
        ends.append(len_s[0, j] + (ends[-1] if ends else 0))
    tc, tr = iota((T, 128), 0), iota((8, T), 1)
    uid_c, uid_r = jnp.zeros((T, 128), I32), jnp.zeros((8, T), I32)
    for end in ends:
        uid_c = uid_c + (tc >= end).astype(I32)
        uid_r = uid_r + (tr >= end).astype(I32)
    same = (uid_c[:, :1] == uid_r[:1, :]) & (iota((T, T), 1) <= iota((T, T), 0))
    mask_v[...] = same.astype(F32)

    loads[1].wait()

    def norm_in(i):
        v = x_v[ds(i, 32)].astype(F32)
        v = v - jnp.mean(v, -1, keepdims=True)
        nin[ds(i, 32)] = (v * lax.rsqrt(jnp.mean(v * v, -1, keepdims=True) + EPS)).astype(BF)

    rep(8, norm_in, 2)
    loads[2].wait()
    loads[3].wait()

    def project(i):
        pre = mm(nin[...], win[:, ds(i, 256)])
        sg = sigmoid(pre)
        proj[:, ds(i, 256)] = (pre * sg).astype(BF)
        slope[:, ds(i, 256)] = sg * (1.0 + pre * (1.0 - sg))

    rep(2, project)
    slices(1, 7)
    step(first_send, 1, 7)
    rep(3, lambda i: project(i + 2))
    slices(2, 6)
    step(first_send, 2, 6)
    rep(3, lambda i: project(i + 5))
    step(first_forward, 1, 7)

    def flip_in(i):
        block = nin[:, ds(i, 128)].astype(F32).T
        ninT[i] = block.astype(BF).reshape(2, 64, T)

    def attend(h):
        col = lambda part: pl.ds(pl.multiple_of(part * HID + h * 128, 128), 128)
        scores = mm_t(proj[:, col(2)], proj[:, col(3)]) * SCALE
        sg = sigmoid(scores)
        mask = mask_v[...]
        weight = (scores * sg * mask).astype(BF)
        attn[h] = weight
        dsl[h] = sg * (1.0 + scores * (1.0 - sg)) * SCALE * mask
        att[:, ds(h, 128)] = mm(weight, proj[:, col(1)])

    rep(2, attend)
    slices(3, 5)
    slice_in["4r", "4l"] = net.bundle(
        tab.at[0, 0, 0], (mine_at(5, low), mine_at(4, low), w.zoff(1)), (mine_at(3, high), mine_at(4, high), w.zoff(-1)))
    direct = net.bundle(
        tab.at[pl.ds(0, 2), :, :, :, low], (tab.at[0, :, :, :, low], tab.at[7, :, :, :, low], w.zoff(1)),
        (tab.at[0, :, :, :, low], tab.at[1, :, :, :, low], w.zoff(-1)))
    step(first_send, 3, 5)
    step(first_forward, 2, 6)
    rep(2, lambda h: attend(h + 2))
    step(second_send, 1, 7)

    def norm_att(i):
        v = att[ds(i, 32)]
        v = v - jnp.mean(v, -1, keepdims=True)
        f = lax.rsqrt(jnp.mean(v * v, -1, keepdims=True) + EPS)
        n = v * f
        normed[ds(i, 32)] = n
        inv[ds(i, 32)] = jnp.broadcast_to(f, (32, 128))
        gated[ds(i, 32)] = (n * proj[ds(i, 32), pl.ds(0, HID)].astype(F32)).astype(BF)

    rep(8, norm_att, 2)
    slices("4r", "4l")
    step(first_send, "4x", "4y")
    step(first_forward, 3, 5)
    step(second_send, 2, 6)

    def result(i):
        res[:, ds(i, 256)] = x_v[:, ds(i, 256)].astype(F32) + mm_t(gated[...], wout[ds(i, 256)])

    rep(4, result)

    def norm_out(i):
        v = res[ds(i, 32)]
        f = lax.rsqrt(jnp.sum(v * v, -1, keepdims=True) + EPS)
        rlen[ds(i, 32)] = jnp.broadcast_to(f, (32, 128))
        yall[0, ds(i, 32)] = (v * f).astype(BF)
        lout[ds(i, 32)] = v.astype(BF)

    rep(8, norm_out, 2)
    cp_y = net.go(yall.at[0], ymate, w.mate())
    two_y = yall.at[pl.ds(0, 2)]
    hop = net.bundle(two_y, (yall.at[0], yall.at[7], w.zoff(1)), (yall.at[0], yall.at[1], w.zoff(-1)))
    cp_rows = net.bundle(rall.at[pl.ds(0, 7)], *[(rall.at[0], rall.at[8 - k], w.zoff(k)) for k in range(1, 8)])
    step(first_forward, "4x", "4y")
    rep(8, flip_in)
    step(second_forward, 1, 7)
    step(second_send, 3, 5)
    cp_nin = net.go(ninT.at[:, 1 - c], ninTm, w.mate())
    cp_gated = net.go(gated, gatedm, w.mate())

    lsum[...] = jnp.zeros_like(lsum)
    lanes = iota((256, 128), 1).astype(F32)
    cp_cand.wait_recv()

    def owner(dz):
        return ((z + dz) % 8) * 2 + c

    def aim(dz):
        def part(i):
            who = cand[ds(i, 256)]
            spot = jnp.where((who >> 9) == owner(dz), (who & 511) + 1, 0).astype(F32)
            spot = jnp.broadcast_to(jnp.sum(spot, -1, keepdims=True) - 1.0, (256, 128))
            for q in range(4):
                picks[ds(i, 256), pl.ds(q * 128, 128)] = jnp.where(spot == lanes + 128.0 * q, 1.0, 0.0).astype(BF)
            lacc[ds(i, 256)] = jnp.zeros((256, 128), F32)

        rep(2, part)

    def score(dz):
        def part(i):
            rows = mm(picks[...], tab[dz, :, :, :, ds(i, 256)].reshape(512, 256))
            found[dz, :, ds(i, 256)] = rows.astype(BF)
            for first, y in ((0, yall[0, :, ds(i, 256)]), (T, ymate[:, ds(i, 256)])):
                got = rows[first:first + T] * y.astype(F32)
                lacc[pl.ds(first, T)] += got[:, :128] + got[:, 128:]

        rep(4, part)

        def close(i):
            value = jnp.sum(lacc[ds(i, 256)], -1, keepdims=True)
            lsum[ds(i, 256)] += jnp.where((cand[ds(i, 256)] >> 9) == owner(dz), value, 0.0)

        rep(2, close)

    def settle(*names):
        for name in names:
            flying[name].wait_recv()

    aim(0)
    cp_y.wait_recv()
    score(0)
    step(second_send, "4x", "4y")
    aim(1)
    direct.wait_recv()
    settle(1, 7)
    step(second_forward, 2, 6)
    score(1)
    aim(7)
    score(7)
    hop.wait_recv()
    hop = net.bundle(two_y, (yall.at[7], yall.at[6], w.zoff(1)), (yall.at[1], yall.at[2], w.zoff(-1)))
    aim(2)
    settle(2, 6)
    step(second_forward, 3, 5)
    score(2)
    aim(6)
    score(6)
    step(second_forward, "4x", "4y")
    aim(3)
    settle(3, 5)
    score(3)
    aim(5)
    score(5)
    aim(4)
    settle("4x", "4y")
    score(4)
    lane = iota((2 * T, 128), 1)
    cp_l = net.go(lsum, lrec, w.mate())
    hop.wait_recv()
    hop = net.bundle(two_y, (yall.at[6], yall.at[5], w.zoff(1)), (yall.at[2], yall.at[3], w.zoff(-1)))
    cp_l.wait_recv()
    lrec_v = lrec[...]
    logits = (lsum[...] + jnp.concatenate([lrec_v[T:], lrec_v[:T]], 0)) / TEMP
    live = lane < NCAND
    ex = jnp.where(live, jnp.exp(jnp.where(live, logits, 0.0)), 0.0)
    soft = ex / jnp.sum(ex, -1, keepdims=True)
    gcol[...] = jnp.where(live, soft - (lane == 0).astype(F32), 0.0) / TEMP

    gsend[...] = gcol[pl.ds(0, T)].T[:8]
    gall[0] = gsend[...]
    cp_g = net.bundle(gall.at[pl.ds(0, 7)], *[(gsend, gall.at[8 - k], w.zoff(k)) for k in range(1, 8)])

    def blend(at):
        who, how = cand[at] >> 9, gcol[at]
        total = jnp.zeros((32, D), F32)
        for dz in range(8):
            much = jnp.sum(jnp.where(who == owner(dz), how, 0.0), -1, keepdims=True)
            total = total + much * found[dz, at].astype(F32)
        return total

    def gather_mate(i):
        wsend[ds(i, 32)] = blend(ds(i + 8, 32)).astype(BF)

    rep(8, gather_mate)
    cp_w = net.go(wsend, wrec, w.mate())

    def gather_own(i):
        wown[ds(i, 32)] = blend(ds(i, 32))

    rep(8, gather_own)
    cp_w.wait_recv()

    def upstream(i):
        f = rlen[ds(i, 32)][:, :1]
        yn = res[ds(i, 32)] * f
        v = wown[ds(i, 32)] + wrec[ds(i, 32)].astype(F32)
        up = (v - yn * jnp.sum(yn * v, -1, keepdims=True)) * f
        upb[ds(i, 32)] = up.astype(BF)

    rep(8, upstream, 2)

    gg[...] = mm(upb[...], wout[...])

    def back_norm(i):
        n, v = normed[ds(i, 32)], gg[ds(i, 32)]
        gpre[ds(i, 32), pl.ds(0, HID)] = (v * n * slope[ds(i, 32), pl.ds(0, HID)]).astype(BF)
        v = v * proj[ds(i, 32), pl.ds(0, HID)].astype(F32)
        v = v - jnp.mean(v, -1, keepdims=True) - n * jnp.mean(v * n, -1, keepdims=True)
        gatt[ds(i, 32)] = (inv[ds(i, 32)][:, :1] * v).astype(BF)

    rep(8, back_norm, 2)

    def flip_up(i):
        block = upb[:, ds(i, 128)].astype(F32).T
        upT[i] = block.astype(BF).reshape(2, 64, T)

    rep(8, flip_up)
    cp_up = net.go(upT.at[:, 1 - c], upTm, w.mate())

    def back_attend(h):
        col = lambda part: pl.ds(pl.multiple_of(part * HID + h * 128, 128), 128)
        da = gatt[:, ds(h, 128)]
        ds_ = (mm_t(da, proj[:, col(1)]) * dsl[h])
        gv = mm(attn[h].astype(F32).T.astype(BF), da)
        gq = mm(ds_.astype(BF), proj[:, col(3)])
        gk = mm(ds_.T.astype(BF), proj[:, col(2)])
        gpre[:, col(1)] = (gv * slope[:, col(1)]).astype(BF)
        gpre[:, col(2)] = (gq * slope[:, col(2)]).astype(BF)
        gpre[:, col(3)] = (gk * slope[:, col(3)]).astype(BF)

    rep(4, back_attend)
    cp_pre = net.go(gpre, gprem, w.mate())
    hop.wait_recv()
    a, b = pl.ds(0, 512), pl.ds(512, 512)
    hop = net.bundle(yall.at[0], (yall.at[5, :, a], yall.at[4, :, a], w.zoff(1)),
                     (yall.at[3, :, b], yall.at[4, :, b], w.zoff(-1)))

    def store_g(i, first, block):
        for b in range(block.shape[1] // 128):
            n = first + b
            g_v[n // 5, pl.ds(i * 4, 4), :, :, pl.ds((n % 5) * 128, 128)] = (
                block[:, b * 128:(b + 1) * 128].astype(BF).reshape(4, 4, 16, 128))

    cp_gated.wait_recv()
    cp_up.wait_recv()

    def grad_out(i):
        a = upT[pl.ds(i * 4, 4), c].reshape(T, T)
        b = upTm[pl.ds(i * 4, 4)].reshape(T, T)
        store_g(i, 16, mm(a, gated[...]) + mm(b, gatedm[...]))

    rep(2, grad_out)
    cp_nin.wait_recv()
    cp_pre.wait_recv()

    def grad_in(i):
        a = ninT[pl.ds(i * 4, 4), c].reshape(T, T)
        b = ninTm[pl.ds(i * 4, 4)].reshape(T, T)
        for n in range(4):
            cols = pl.ds(n * 512, 512)
            store_g(i, n * 4, mm(a, gpre[:, cols]) + mm(b, gprem[:, cols]))

    rep(2, grad_in)

    two = lambda k: pl.ds(2 * k, 2)
    cut = lambda k: pl.ds(256 * k, 256)
    hicut = lambda k: pl.ds(512 + 256 * k, 256)
    ga = Ring(net, w.xoff, px, lambda j, k: g_v.at[j, two(k)], ga_b, lambda k: a1.at[two(k)])
    gb = Ring(net, w.yoff, py, lambda j, k: g_v.at[:, pl.ds(4 + 2 * k, 2), j], gb_b, lambda k: b1.at[:, two(k)])
    ha = Ring(net, w.xoff, px, lambda j, k: h_v.at[j, :, :, cut(k)], ha_b, lambda k: ha1.at[:, :, cut(k)])
    hb = Ring(net, w.yoff, py, lambda j, k: h_v.at[:, j, :, hicut(k)], hb_b, lambda k: hb1.at[:, :, cut(k)])
    ga2 = Ring(net, w.yoff, py, lambda j, k: a1.at[two(k), j], ga2_b, lambda k: piece.at[two(k)])
    gb2 = Ring(net, w.xoff, px, lambda j, k: b1.at[j, two(k)], gb2_b, lambda k: piece.at[pl.ds(4 + 2 * k, 2)])
    mine = hall.at[px, py]
    ha2 = Ring(net, w.yoff, py, lambda j, k: ha1.at[j, :, cut(k)], ha2_b, lambda k: mine.at[:, cut(k)])
    hb2 = Ring(net, w.xoff, px, lambda j, k: hb1.at[j, :, cut(k)], hb2_b, lambda k: mine.at[:, hicut(k)])
    ga.start()
    gb.start()

    lane8 = iota((8, 128), 1)
    counts = jnp.zeros((8, 128), F32)
    place = jnp.zeros((8, T), I32)
    start = 0
    for j in range(16):
        n, d = len_s[0, j], dst_s[0, j]
        counts = counts + jnp.where(lane8 == d, n, 0).astype(F32)
        place = jnp.where((tr >= start) & (tr < start + n), d * 32 + tr - start, place)
        start = start + n
    csend[...] = counts
    cp_count = net.bundle(cbuf.at[pl.ds(0, 15)], *[(csend, cbuf.at[s], w.at(seq=(s + k) % 16)) for k in range(1, 16)])
    cbuf[s] = csend[...]

    def fill(i):
        pick = jnp.where(iota((128, T), 0) + i * 128 == place[:1, :], 1.0, 0.0).astype(BF)
        slots_s[pl.ds(i * 4, 4)] = mm(pick, lout[...]).astype(BF).reshape(4, 32, D)

    rep(4, fill)
    used = pl.ds(0, 24)
    cp_slot = net.bundle(
        slots_r.at[pl.ds(0, 15), used],
        *[(slots_s.at[(s + k) % 16, used], slots_r.at[s, used], w.at(seq=(s + k) % 16)) for k in range(1, 16)])
    slots_r[s, used] = slots_s[s, used]

    cp_rows.wait_recv()
    cp_g.wait_recv()

    def spread_t(dz):
        who, how = rall[dz], gall[dz]
        for o in range(2):
            hit = (who >> 9) == z * 2 + o
            spot = jnp.sum(jnp.where(hit, (who & 511) + 1, 0).astype(F32), 0, keepdims=True) - 1.0
            much = jnp.sum(jnp.where(hit, how, 0.0), 0, keepdims=True)
            for j in range(4):
                line = (iota((128, T), 0) + j * 128).astype(F32)
                found[dz // 4 + 2 * o, pl.ds(j * 128, 128), ds(dz % 4, T)] = jnp.where(line == spot, much, 0.0).astype(BF)

    rep(8, spread_t)

    def h_part(o, i):
        y = [yall[pl.ds(4 * k, 4), :, ds(i, 256)].reshape(4 * T, 256) for k in range(2)]
        return mm(found[2 * o], y[0]) + mm(found[2 * o + 1], y[1])

    def h_mate(i):
        hsend[:, ds(i, 256)] = h_part(1 - c, i).astype(BF)

    hop.wait_recv()
    rep(4, h_mate)
    cp_h = net.go(hsend, hrec, w.mate())
    ga.relay()
    gb.relay()

    def h_own(i):
        part = h_part(c, i)
        wown[:, ds(i, 256)] = part[:T]
        res[:, ds(i, 256)] = part[T:]

    rep(4, h_own)
    cp_h.wait_recv()
    for part, src in ((0, wown), (1, res)):
        for i in range(8):
            total = src[pl.ds(i * 32, 32)] + hrec[pl.ds(part * T + i * 32, 32)].astype(F32)
            h_v[part * 2 + i // 4, i % 4] = total.astype(BF)
    ha.start()
    hb.start()

    ga.finish()
    ga2.start()
    gb.finish()
    gb2.start()
    ha.relay()
    hb.relay()
    ga2.relay()
    gb2.relay()
    ha.finish()
    ha2.start()
    hb.finish()
    hb2.start()
    ga2.finish()
    gb2.finish()
    cp_z = net.bundle(zbuf.at[pl.ds(0, 7)], *[(piece.at[(z + k) % 8], zbuf.at[k], w.zoff(k)) for k in range(1, 8)])
    ha2.relay()
    hb2.relay()
    ha2.finish()
    first_send("hx")
    hb2.finish()
    first_send("hy")
    total = piece[z].astype(F32)
    cp_z.wait_recv()
    for k in range(1, 8):
        total = total + zbuf[k].astype(F32)
    wpiece[...] = total.astype(BF)
    cp_sum = net.bundle(wall.at[pl.ds(0, 15)], *[(wpiece, wall.at[g], peer(i, j)) for i, j in plane])
    wall[g] = wpiece[...]
    step(first_forward, "hx", "hy")
    step(second_send, "hx", "hy")

    cp_count.wait_recv()
    cp_slot.wait_recv()
    cnt = jnp.sum(jnp.where(iota((16, 128), 1) == s, cbuf[:, 0, :], 0.0), -1, keepdims=True)
    row, col16 = iota((16, 512), 0), iota((16, 512), 1)
    slot = col16 >> 5
    before = jnp.sum(jnp.where(row < slot, cnt, 0.0), 0, keepdims=True)
    here = jnp.sum(jnp.where(row == slot, cnt, 0.0), 0, keepdims=True)
    inside = (col16[:1] & 31).astype(F32)
    goal = jnp.where(inside < here, before + inside, -1.0)
    chosen = jnp.where(iota((T, 512), 0).astype(F32) == goal, 1.0, 0.0).astype(BF)

    def land(i):
        lay_o[:, ds(i, 256)] = mm(chosen, slots_r[:, :, ds(i, 256)].reshape(512, 256)).astype(BF)

    rep(4, land)
    step(second_forward, "hx", "hy")
    cp_sum.wait_recv()
    w_o[...] = wall[...]
    settle("hx", "hy")
    h_o[...] = hall[...]
    assert net.n == NSEM, net.n
    net.drain()


def train_call(lengths, destinations, hist, neg, events, in_weight, out_weight, item_table):
    vm = lambda *shape, dtype=BF: pltpu.VMEM(shape, dtype)
    f32 = dict(dtype=F32)
    halves = [(2, 4, 16, 640), (4, 2, 16, 640), (4, 32, 256), (4, 32, 256), (2, 16, 640), (2, 16, 640), (32, 256), (32, 256)]
    sem = pltpu.SemaphoreType.DMA
    scratch = [
        vm(T, D), vm(D, 4 * HID), vm(D, HID), vm(512, D), vm(8, 4, 4, 32, D), vm(T, D),
        vm(T, 4 * HID, **f32), vm(T, 4 * HID), vm(HEADS, T, T), vm(HEADS, T, T, **f32),
        vm(T, HID, **f32), vm(T, HID, **f32), vm(T, 128, **f32), vm(T, HID), vm(T, HID),
        vm(T, D, **f32), vm(T, 128, **f32), vm(8, T, D), vm(T, D), vm(128, T, **f32), vm(2 * T, 128, dtype=I32),
        vm(8, 8, T, dtype=I32), vm(8, 8, T, **f32), vm(8, T, **f32), vm(2 * T, 128, **f32),
        vm(2 * T, 128, **f32), vm(2 * T, 128, **f32), vm(2 * T, 128, **f32), vm(2 * T, 512),
        vm(8, 2 * T, D), vm(T, D, **f32), vm(T, D), vm(T, D), vm(T, D),
        vm(T, HID, **f32), vm(T, HID), vm(T, 4 * HID), vm(T, 4 * HID), vm(8, 2, 64, T), vm(8, 64, T),
        vm(8, 2, 64, T), vm(8, 64, T), vm(512, D), vm(512, D), vm(T, T, **f32), vm(T, D),
        vm(4, 8, 4, 16, 640), vm(4, 4, 32, D),
        vm(4, 4, 16, 640), vm(4, 4, 16, 640), vm(4, 32, 512), vm(4, 32, 512), vm(8, 16, 640), vm(8, 16, 640),
        vm(16, 640), vm(16, 16, 640), vm(4, 4, 32, D), vm(16, 32, D), vm(16, 32, D),
        vm(8, 128, **f32), vm(16, 8, 128, **f32),
        sem((4,)), sem((NSEM,)), sem((NSEM,)),
    ] + [vm(2, *shape) for shape in halves for _ in range(4)]
    any_ = pl.BlockSpec(memory_space=pl.ANY)
    vmem = pl.BlockSpec(memory_space=pltpu.VMEM)
    smem = pl.BlockSpec(memory_space=pltpu.SMEM)
    return pl.pallas_call(
        train_kernel,
        out_shape=(jax.ShapeDtypeStruct((T, D), BF), jax.ShapeDtypeStruct((16, 16, 640), BF),
                   jax.ShapeDtypeStruct((4, 4, 32, D), BF)),
        in_specs=[smem, smem, vmem, vmem, any_, any_, any_, any_],
        out_specs=(vmem, vmem, vmem),
        scratch_shapes=scratch,
        compiler_params=pltpu.CompilerParams(collective_id=0, has_side_effects=True, vmem_limit_bytes=VMEM_BYTES),
        name="train",
    )(lengths, destinations, hist, neg, events, in_weight, out_weight, item_table)


def last_kernel(lay, w, h, e, lay_o, in_o, out_o, tab_o):
    lay_o[...] = lay[...]
    rows = jnp.concatenate([w[i, 0] for i in range(4)], 1).astype(F32)
    in_o[...] = rows[:, :4 * HID]
    out_o[...] = rows[:, 4 * HID:]
    item, total = e[...].astype(F32), h[0].reshape(128, D).astype(F32)
    length = lax.rsqrt(jnp.sum(item * item, -1, keepdims=True) + EPS)
    item = item * length
    tab_o[...] = (total - item * jnp.sum(item * total, -1, keepdims=True)) * length


def last_call(lay, w, h, item_table):
    rows = lambda n, m: pl.BlockSpec((n, m), lambda i: (i, 0))
    return pl.pallas_call(
        last_kernel,
        grid=(4,),
        out_shape=(jax.ShapeDtypeStruct((T, D), BF), jax.ShapeDtypeStruct((64, 4 * HID), F32),
                   jax.ShapeDtypeStruct((64, HID), F32), jax.ShapeDtypeStruct((512, D), F32)),
        in_specs=[rows(64, D), pl.BlockSpec((4, 1, 16, 640), lambda i: (0, i, 0, 0)),
                  pl.BlockSpec((1, 4, 32, D), lambda i: (i, 0, 0, 0)), rows(128, D)],
        out_specs=(rows(64, D), rows(16, 4 * HID), rows(16, HID), rows(128, D)),
        name="last",
    )(lay, w, h, item_table)


def body(events, lengths, destinations, history, negatives, in_weight, out_weight, item_table):
    result, wsum, hsum = train_call(lengths, destinations, history.reshape(1, T), negatives.T, events,
                                    in_weight, out_weight, item_table)
    return last_call(result, wsum.reshape(4, 4, 16, 640), hsum, item_table)


def solution(mesh):
    return jax.shard_map(
        body,
        mesh=mesh,
        in_specs=(
            P(("grp", "seq"), None),
            P(("grp", "seq"), None),
            P(("grp", "seq"), None),
            P(("grp", "seq")),
            P(("grp", "seq"), None),
            P(),
            P(),
            P("seq", None),
        ),
        out_specs=(P(("grp", "seq"), None), P("seq", None), P("seq", None), P("seq", None)),
        check_vma=False,
    )
```

```python
import jax
import jax.numpy as jnp
from jax import lax
from jax.experimental import pallas as pl
from jax.experimental.pallas import tpu as pltpu
from jax.sharding import PartitionSpec as P

F32, BF, I32 = jnp.float32, jnp.bfloat16, jnp.int32
MESH = pl.DeviceIdType.MESH
T, D, HID = 256, 1024, 512
HEADS, HEAD_DIM, NCAND = 4, 128, 4
EPS = 1e-5
TEMP = 0.05
SCALE = HEAD_DIM ** -0.5
VMEM_BYTES = 67_000_000


def rep(n, body, unroll=1):
    def step(i, carry):
        body(i)
        return carry

    lax.fori_loop(0, n, step, 0, unroll=unroll)


def ds(i, size):
    return pl.ds(pl.multiple_of(i * size, size), size)


def iota(shape, dim):
    return lax.broadcasted_iota(I32, shape, dim)


def mm(a, b):
    return jnp.dot(a, b, preferred_element_type=F32)


def mm_t(a, b):
    return lax.dot_general(a, b, (((1,), (1,)), ((), ())), preferred_element_type=F32)


def sigmoid(v):
    return 1.0 / (1.0 + jnp.exp(-v))


class Where:
    def __init__(self):
        self.g, self.s = lax.axis_index("grp"), lax.axis_index("seq")
        self.px, self.py = self.g // 4, self.g % 4
        self.z, self.c = self.s // 2, self.s % 2

    def at(self, grp=None, seq=None):
        return {"grp": self.g if grp is None else grp, "seq": self.s if seq is None else seq}

    def zoff(self, k):
        return self.at(seq=((self.z + k) % 8) * 2 + self.c)

    def mate(self):
        return self.at(seq=self.z * 2 + 1 - self.c)

    def xoff(self, k):
        return self.at(grp=((self.px + k) % 4) * 4 + self.py)

    def yoff(self, k):
        return self.at(grp=self.px * 4 + (self.py + k) % 4)


class Links:
    def __init__(self, send, recv):
        self.send, self.recv, self.n, self.sent = send, recv, 0, []

    def describe(self, src, dst, dev):
        return pltpu.make_async_remote_copy(
            src_ref=src, dst_ref=dst, send_sem=self.send.at[self.n], recv_sem=self.recv.at[self.n],
            device_id=dev, device_id_type=MESH)

    def go(self, src, dst, dev):
        return self.bundle(dst, (src, dst, dev))

    def bundle(self, whole, *copies):
        for copy in copies:
            self.describe(*copy).start()
        wait = self.describe(whole, whole, copies[0][2])
        self.n += 1
        self.sent.append(wait)
        return wait

    def drain(self):
        for copy in self.sent:
            copy.wait_send()


class Ring:
    def __init__(self, net, off, i, src, bufs, out):
        self.net, self.off, self.i, self.src, self.out = net, off, i, src, out
        self.t, self.u, self.v, self.r = bufs

    def start(self):
        far, right, left = (self.i + 2) % 4, (self.i + 1) % 4, (self.i + 3) % 4
        off, src, t, u = self.off, self.src, self.t, self.u
        self.ct = self.net.bundle(t, (src(far, 0), t.at[0], off(1)), (src(far, 1), t.at[1], off(-1)))
        self.cu = self.net.bundle(u, (src(left, 0), u.at[0], off(-1)), (src(right, 1), u.at[1], off(1)))

    def relay(self):
        self.ct.wait_recv()
        for k, j in ((0, (self.i + 1) % 4), (1, (self.i + 3) % 4)):
            self.v[k] = (self.t[k].astype(F32) + self.src(j, k)[...].astype(F32)).astype(BF)
        v, r, off = self.v, self.r, self.off
        self.cr = self.net.bundle(r, (v.at[0], r.at[0], off(1)), (v.at[1], r.at[1], off(-1)))

    def finish(self):
        self.cr.wait_recv()
        self.cu.wait_recv()
        for k in range(2):
            total = self.src(self.i, k)[...].astype(F32) + self.r[k].astype(F32) + self.u[k].astype(F32)
            self.out(k)[...] = total.astype(BF)


class Swap:
    def __init__(self, net, off, i, src, buf, out):
        self.net, self.off, self.i, self.src, self.buf, self.out = net, off, i, src, buf, out

    def start(self):
        buf = self.buf
        self.got = self.net.bundle(
            buf.at[pl.ds(1, 3)], *[(self.src((self.i + k) % 4), buf.at[k], self.off(k)) for k in (2, 1, 3)])

    def finish(self):
        self.got.wait_recv()
        total = self.src(self.i)[...].astype(F32)
        for k in range(1, 4):
            total = total + self.buf[k].astype(F32)
        self.out[...] = total.astype(BF)


def call_out(devices):
    barrier = pltpu.get_barrier_semaphore()
    for dev in devices:
        pl.semaphore_signal(barrier, inc=1, device_id=dev, device_id_type=MESH)
    return lambda: pl.semaphore_wait(barrier, len(devices))


NSEM = 84


def train_kernel(len_s, dst_s, hist_v, neg_v, ev_h, win_h, wout_h, tab_h, lay_o, w_o, h_o, *refs):
    (x_v, win, wout, traw, tab, nin, slope, proj, attn, dsl, att, normed, inv, gated, gatedm,
     res, rlen, yall, ymate, ids_f, cand, rall, gall, gsend, lacc, lsum, lrec, gcol, picks, found,
     wown, wsend, wrec, upb, gg, gatt, gpre, gprem, ninT, ninTm, upT, upTm, hsend, hrec, mask_v, lout,
     g_v, h_v, a1, b1, ha1, hb1, piece, zbuf, wpiece, wall, hall, slots_s, slots_r, csend, cbuf,
     lsem, ssem, rsem) = refs[:len(refs) - 20]
    bufs = refs[len(refs) - 20:]
    (ga_b, gb_b, ha_b, hb_b) = [bufs[4 * i:4 * i + 4] for i in range(4)]
    ga2_b, gb2_b, ha2_b, hb2_b = bufs[16:]
    w = Where()
    net = Links(ssem, rsem)
    s, z, c, px, py, g = w.s, w.z, w.c, w.px, w.py, w.g
    plane = [(i, j) for i in range(4) for j in range(4) if (i, j) != (0, 0)]

    def peer(i, j):
        return w.at(grp=((px + i) % 4) * 4 + (py + j) % 4)

    loads = [pltpu.make_async_copy(a, b, lsem.at[i]) for i, (a, b) in enumerate(
        ((tab_h, traw), (ev_h, x_v), (win_h, win), (wout_h, wout)))]
    for copy in loads:
        copy.start()
    for k in range(16):
        slots_r[k, pl.ds(24, 8)] = jnp.zeros((8, D), BF)
    everyone = call_out([w.at(seq=(s + k) % 16) for k in range(1, 16)] + [peer(i, j) for i, j in plane])

    ids_f[...] = jnp.full((128, T), -1.0, F32)
    ids_f[pl.ds(0, 1)] = hist_v[...].astype(F32)
    ids_f[pl.ds(1, 3)] = neg_v[...].astype(F32)
    rall[0] = ids_f[pl.ds(0, 8)].astype(I32)
    cand[pl.ds(0, T)] = ids_f[...].T.astype(I32)

    loads[0].wait()

    def norm_rows(i):
        j = (g + i) % 16
        rows = traw[ds(j, 32)].astype(F32)
        length = lax.rsqrt(jnp.sum(rows * rows, -1, keepdims=True) + EPS)
        tab[0, j // 4, j % 4] = (rows * length).astype(BF)

    norm_rows(0)
    everyone()
    low, high = pl.ds(0, 512), pl.ds(512, 512)
    mine_at = lambda dz, cols: tab.at[dz, px, py, :, cols]
    slice_in = {}
    for a, b in ((1, 7), (2, 6), (3, 5)):
        slice_in[a, b] = net.bundle(
            tab.at[0, 0, pl.ds(0, 2)],
            *[(tab.at[0, px, py], tab.at[8 - k, px, py], w.zoff(k)) for k in (a, b)])
    rep(15, lambda i: norm_rows(i + 1))
    cp_cand = net.go(cand.at[pl.ds(0, T)], cand.at[pl.ds(T, T)], w.mate())

    pieces = {7: (tab.at[7], 0, 1024, "y"), 1: (tab.at[1], 0, 1024, "x"),
              6: (tab.at[6], 0, 1024, "y"), 2: (tab.at[2], 0, 1024, "x"),
              5: (tab.at[5], 0, 1024, "y"), 3: (tab.at[3], 0, 1024, "x"),
              "4x": (tab.at[4], 0, 512, "x"), "4y": (tab.at[4], 512, 512, "y")}
    flying, early = {}, {}

    def one(piece, kx, ky, c0, nc):
        return piece[0].at[(px + kx) % 4, (py + ky) % 4, :, pl.ds(c0, nc)]

    def many(piece, k, c0, nc):
        if piece[3] == "x":
            return piece[0].at[:, (py + k) % 4, :, pl.ds(c0, nc)]
        return piece[0].at[(px + k) % 4, :, :, pl.ds(c0, nc)]

    def pair(name, whole, right, left, off):
        flying[name] = net.bundle(whole, (right, right, off(1)), (left, left, off(-1)))

    def first_send(name):
        p = pieces[name]
        own = one(p, 0, 0, p[1], p[2])
        whole = p[0].at[0, pl.ds(0, 2), :, pl.ds(p[1], p[2])]
        across = w.yoff if p[3] == "x" else w.xoff
        pair(name, whole, own, own, w.xoff if p[3] == "x" else w.yoff)
        early[name] = net.bundle(whole, (own, own, across(1)), (own, own, across(-1)))

    def first_forward(name):
        p = pieces[name]
        half = p[2] // 2
        at = (lambda k, c0: one(p, k, 0, c0, half)) if p[3] == "x" else (lambda k, c0: one(p, 0, k, c0, half))
        flying[name].wait_recv()
        pair(name, one(p, 0, 0, p[1], p[2]), at(-1, p[1]), at(1, p[1] + half), w.xoff if p[3] == "x" else w.yoff)

    def second_send(name):
        p = pieces[name]
        flying[name].wait_recv()
        across = w.yoff if p[3] == "x" else w.xoff
        others = [one(p, k, 0, p[1], p[2]) if p[3] == "x" else one(p, 0, k, p[1], p[2]) for k in (1, 3, 2)]
        flying[name] = net.bundle(
            p[0].at[pl.ds(0, 2), pl.ds(0, 3), :, pl.ds(p[1], p[2])],
            *[(ref, ref, across(d)) for ref in others for d in (1, -1)])

    def second_forward(name):
        p = pieces[name]
        half = p[2] // 2
        early[name].wait_recv()
        flying[name].wait_recv()
        pair(name, many(p, 0, p[1], p[2]), many(p, -1, p[1], half), many(p, 1, p[1] + half, half),
             w.yoff if p[3] == "x" else w.xoff)

    def step(stage, *names):
        for name in names:
            stage(name)

    def slices(a, b):
        slice_in[a, b].wait_recv()

    ends = []
    for j in range(16):
        ends.append(len_s[0, j] + (ends[-1] if ends else 0))
    tc, tr = iota((T, 128), 0), iota((8, T), 1)
    uid_c, uid_r = jnp.zeros((T, 128), I32), jnp.zeros((8, T), I32)
    for end in ends:
        uid_c = uid_c + (tc >= end).astype(I32)
        uid_r = uid_r + (tr >= end).astype(I32)
    same = (uid_c[:, :1] == uid_r[:1, :]) & (iota((T, T), 1) <= iota((T, T), 0))
    mask_v[...] = same.astype(F32)

    loads[1].wait()

    def norm_in(i):
        v = x_v[ds(i, 32)].astype(F32)
        v = v - jnp.mean(v, -1, keepdims=True)
        nin[ds(i, 32)] = (v * lax.rsqrt(jnp.mean(v * v, -1, keepdims=True) + EPS)).astype(BF)

    rep(8, norm_in, 2)
    loads[2].wait()
    loads[3].wait()

    def project(i):
        pre = mm(nin[...], win[:, ds(i, 256)])
        sg = sigmoid(pre)
        proj[:, ds(i, 256)] = (pre * sg).astype(BF)
        slope[:, ds(i, 256)] = sg * (1.0 + pre * (1.0 - sg))

    rep(2, project)
    slices(1, 7)
    step(first_send, 1, 7)
    rep(3, lambda i: project(i + 2))
    slices(2, 6)
    step(first_send, 2, 6)
    rep(3, lambda i: project(i + 5))
    step(first_forward, 1, 7)

    def flip_in(i):
        block = nin[:, ds(i, 128)].astype(F32).T
        ninT[i] = block.astype(BF).reshape(2, 64, T)

    def attend(h):
        col = lambda part: pl.ds(pl.multiple_of(part * HID + h * 128, 128), 128)
        scores = mm_t(proj[:, col(2)], proj[:, col(3)]) * SCALE
        sg = sigmoid(scores)
        mask = mask_v[...]
        weight = (scores * sg * mask).astype(BF)
        attn[h] = weight
        dsl[h] = sg * (1.0 + scores * (1.0 - sg)) * SCALE * mask
        att[:, ds(h, 128)] = mm(weight, proj[:, col(1)])

    rep(2, attend)
    slices(3, 5)
    slice_in["4r", "4l"] = net.bundle(
        tab.at[0, 0, 0], (mine_at(5, low), mine_at(4, low), w.zoff(1)), (mine_at(3, high), mine_at(4, high), w.zoff(-1)))
    step(first_send, 3, 5)
    step(first_forward, 2, 6)
    rep(2, lambda h: attend(h + 2))
    step(second_send, 1, 7)

    def norm_att(i):
        v = att[ds(i, 32)]
        v = v - jnp.mean(v, -1, keepdims=True)
        f = lax.rsqrt(jnp.mean(v * v, -1, keepdims=True) + EPS)
        n = v * f
        normed[ds(i, 32)] = n
        inv[ds(i, 32)] = jnp.broadcast_to(f, (32, 128))
        gated[ds(i, 32)] = (n * proj[ds(i, 32), pl.ds(0, HID)].astype(F32)).astype(BF)

    rep(8, norm_att, 2)
    slices("4r", "4l")
    step(first_send, "4x", "4y")
    step(first_forward, 3, 5)
    step(second_send, 2, 6)

    def result(i):
        res[:, ds(i, 256)] = x_v[:, ds(i, 256)].astype(F32) + mm_t(gated[...], wout[ds(i, 256)])

    rep(4, result)

    def norm_out(i):
        v = res[ds(i, 32)]
        f = lax.rsqrt(jnp.sum(v * v, -1, keepdims=True) + EPS)
        rlen[ds(i, 32)] = jnp.broadcast_to(f, (32, 128))
        yall[0, ds(i, 32)] = (v * f).astype(BF)
        lout[ds(i, 32)] = v.astype(BF)

    rep(8, norm_out, 2)
    cp_y = net.go(yall.at[0], ymate, w.mate())
    two_y = yall.at[pl.ds(0, 2)]
    hop = net.bundle(two_y, (yall.at[0], yall.at[7], w.zoff(1)), (yall.at[0], yall.at[1], w.zoff(-1)))
    cp_rows = net.bundle(rall.at[pl.ds(0, 7)], *[(rall.at[0], rall.at[8 - k], w.zoff(k)) for k in range(1, 8)])
    lane8 = iota((8, 128), 1)
    counts = jnp.zeros((8, 128), F32)
    place = jnp.zeros((8, T), I32)
    start = 0
    for j in range(16):
        n, d = len_s[0, j], dst_s[0, j]
        counts = counts + jnp.where(lane8 == d, n, 0).astype(F32)
        place = jnp.where((tr >= start) & (tr < start + n), d * 32 + tr - start, place)
        start = start + n
    csend[...] = counts
    cbuf[s] = csend[...]

    def fill(i):
        pick = jnp.where(iota((128, T), 0) + i * 128 == place[:1, :], 1.0, 0.0).astype(BF)
        slots_s[pl.ds(i * 4, 4)] = mm(pick, lout[...]).astype(BF).reshape(4, 32, D)

    used = pl.ds(0, 24)
    rep(4, fill)
    slots_r[s, used] = slots_s[s, used]
    cp_count = net.bundle(cbuf.at[pl.ds(0, 15)], *[(csend, cbuf.at[s], w.at(seq=(s + k) % 16)) for k in range(1, 16)])

    def slots(*ks):
        return net.bundle(
            slots_r.at[pl.ds(0, len(ks)), used],
            *[(slots_s.at[(s + k) % 16, used], slots_r.at[s, used], w.at(seq=(s + k) % 16)) for k in ks])

    cp_slot = [slots(8, 1, 15, 2, 14)]

    step(first_forward, "4x", "4y")
    rep(8, flip_in)
    step(second_forward, 1, 7)
    step(second_send, 3, 5)
    cp_nin = net.go(ninT.at[:, 1 - c], ninTm, w.mate())
    cp_gated = net.go(gated, gatedm, w.mate())

    lsum[...] = jnp.zeros_like(lsum)
    lanes = iota((256, 128), 1).astype(F32)
    cp_cand.wait_recv()

    def owner(dz):
        return ((z + dz) % 8) * 2 + c

    def aim(dz):
        def part(i):
            who = cand[ds(i, 256)]
            spot = jnp.where((who >> 9) == owner(dz), (who & 511) + 1, 0).astype(F32)
            spot = jnp.broadcast_to(jnp.sum(spot, -1, keepdims=True) - 1.0, (256, 128))
            for q in range(4):
                picks[ds(i, 256), pl.ds(q * 128, 128)] = jnp.where(spot == lanes + 128.0 * q, 1.0, 0.0).astype(BF)
            lacc[ds(i, 256)] = jnp.zeros((256, 128), F32)

        rep(2, part)

    def score(dz):
        def part(i):
            rows = mm(picks[...], tab[dz, :, :, :, ds(i, 256)].reshape(512, 256))
            found[dz, :, ds(i, 256)] = rows.astype(BF)
            for first, y in ((0, yall[0, :, ds(i, 256)]), (T, ymate[:, ds(i, 256)])):
                got = rows[first:first + T] * y.astype(F32)
                lacc[pl.ds(first, T)] += got[:, :128] + got[:, 128:]

        rep(4, part)

        def close(i):
            value = jnp.sum(lacc[ds(i, 256)], -1, keepdims=True)
            lsum[ds(i, 256)] += jnp.where((cand[ds(i, 256)] >> 9) == owner(dz), value, 0.0)

        rep(2, close)

    def settle(*names):
        for name in names:
            flying[name].wait_recv()

    aim(0)
    cp_y.wait_recv()
    score(0)
    step(second_send, "4x", "4y")
    aim(1)
    settle(1, 7)
    step(second_forward, 2, 6)
    score(1)
    aim(7)
    score(7)
    hop.wait_recv()
    hop = net.bundle(two_y, (yall.at[7], yall.at[6], w.zoff(1)), (yall.at[1], yall.at[2], w.zoff(-1)))
    aim(2)
    settle(2, 6)
    step(second_forward, 3, 5)
    score(2)
    aim(6)
    score(6)
    step(second_forward, "4x", "4y")
    aim(3)
    settle(3, 5)
    score(3)
    hop.wait_recv()
    hop = net.bundle(two_y, (yall.at[6], yall.at[5], w.zoff(1)), (yall.at[2], yall.at[3], w.zoff(-1)))
    aim(5)
    score(5)
    aim(4)
    settle("4x", "4y")
    score(4)
    lane = iota((2 * T, 128), 1)
    cp_l = net.go(lsum, lrec, w.mate())
    cp_l.wait_recv()
    lrec_v = lrec[...]
    logits = (lsum[...] + jnp.concatenate([lrec_v[T:], lrec_v[:T]], 0)) / TEMP
    live = lane < NCAND
    ex = jnp.where(live, jnp.exp(jnp.where(live, logits, 0.0)), 0.0)
    soft = ex / jnp.sum(ex, -1, keepdims=True)
    gcol[...] = jnp.where(live, soft - (lane == 0).astype(F32), 0.0) / TEMP

    gsend[...] = gcol[pl.ds(0, T)].T[:8]
    gall[0] = gsend[...]
    cp_g = net.bundle(gall.at[pl.ds(0, 7)], *[(gsend, gall.at[8 - k], w.zoff(k)) for k in range(1, 8)])

    def blend(at):
        who, how = cand[at] >> 9, gcol[at]
        total = jnp.zeros((32, D), F32)
        for dz in range(8):
            much = jnp.sum(jnp.where(who == owner(dz), how, 0.0), -1, keepdims=True)
            total = total + much * found[dz, at].astype(F32)
        return total

    def gather_mate(i):
        wsend[ds(i, 32)] = blend(ds(i + 8, 32)).astype(BF)

    rep(8, gather_mate)
    cp_w = net.go(wsend, wrec, w.mate())

    def gather_own(i):
        wown[ds(i, 32)] = blend(ds(i, 32))

    rep(8, gather_own)
    cp_w.wait_recv()

    def upstream(i):
        f = rlen[ds(i, 32)][:, :1]
        yn = res[ds(i, 32)] * f
        v = wown[ds(i, 32)] + wrec[ds(i, 32)].astype(F32)
        up = (v - yn * jnp.sum(yn * v, -1, keepdims=True)) * f
        upb[ds(i, 32)] = up.astype(BF)

    rep(8, upstream, 2)

    gg[...] = mm(upb[...], wout[...])

    def back_norm(i):
        n, v = normed[ds(i, 32)], gg[ds(i, 32)]
        gpre[ds(i, 32), pl.ds(0, HID)] = (v * n * slope[ds(i, 32), pl.ds(0, HID)]).astype(BF)
        v = v * proj[ds(i, 32), pl.ds(0, HID)].astype(F32)
        v = v - jnp.mean(v, -1, keepdims=True) - n * jnp.mean(v * n, -1, keepdims=True)
        gatt[ds(i, 32)] = (inv[ds(i, 32)][:, :1] * v).astype(BF)

    rep(8, back_norm, 2)

    def flip_up(i):
        block = upb[:, ds(i, 128)].astype(F32).T
        upT[i] = block.astype(BF).reshape(2, 64, T)

    rep(8, flip_up)
    cp_up = net.go(upT.at[:, 1 - c], upTm, w.mate())

    def back_attend(h):
        col = lambda part: pl.ds(pl.multiple_of(part * HID + h * 128, 128), 128)
        da = gatt[:, ds(h, 128)]
        ds_ = (mm_t(da, proj[:, col(1)]) * dsl[h])
        gv = mm(attn[h].astype(F32).T.astype(BF), da)
        gq = mm(ds_.astype(BF), proj[:, col(3)])
        gk = mm(ds_.T.astype(BF), proj[:, col(2)])
        gpre[:, col(1)] = (gv * slope[:, col(1)]).astype(BF)
        gpre[:, col(2)] = (gq * slope[:, col(2)]).astype(BF)
        gpre[:, col(3)] = (gk * slope[:, col(3)]).astype(BF)

    rep(4, back_attend)
    cp_pre = net.go(gpre, gprem, w.mate())

    def store_g(i, first, block):
        for b in range(block.shape[1] // 128):
            n = first + b
            g_v[n // 5, pl.ds(i * 4, 4), :, :, pl.ds((n % 5) * 128, 128)] = (
                block[:, b * 128:(b + 1) * 128].astype(BF).reshape(4, 4, 16, 128))

    cp_gated.wait_recv()
    cp_up.wait_recv()

    def grad_out(i):
        a = upT[pl.ds(i * 4, 4), c].reshape(T, T)
        b = upTm[pl.ds(i * 4, 4)].reshape(T, T)
        store_g(i, 16, mm(a, gated[...]) + mm(b, gatedm[...]))

    rep(2, grad_out)
    cp_nin.wait_recv()
    cp_pre.wait_recv()
    hop.wait_recv()
    a, b = pl.ds(0, 512), pl.ds(512, 512)
    hop = net.bundle(yall.at[0], (yall.at[5, :, a], yall.at[4, :, a], w.zoff(1)),
                     (yall.at[3, :, b], yall.at[4, :, b], w.zoff(-1)))

    def grad_in(i):
        a = ninT[pl.ds(i * 4, 4), c].reshape(T, T)
        b = ninTm[pl.ds(i * 4, 4)].reshape(T, T)
        for n in range(4):
            cols = pl.ds(n * 512, 512)
            store_g(i, n * 4, mm(a, gpre[:, cols]) + mm(b, gprem[:, cols]))

    rep(2, grad_in)

    two = lambda k: pl.ds(2 * k, 2)
    cut = lambda k: pl.ds(256 * k, 256)
    hicut = lambda k: pl.ds(512 + 256 * k, 256)
    ga = Ring(net, w.xoff, px, lambda j, k: g_v.at[j, two(k)], ga_b, lambda k: a1.at[two(k)])
    gb = Ring(net, w.yoff, py, lambda j, k: g_v.at[:, pl.ds(4 + 2 * k, 2), j], gb_b, lambda k: b1.at[:, two(k)])
    ha = Ring(net, w.xoff, px, lambda j, k: h_v.at[j, :, :, cut(k)], ha_b, lambda k: ha1.at[:, :, cut(k)])
    hb = Ring(net, w.yoff, py, lambda j, k: h_v.at[:, j, :, hicut(k)], hb_b, lambda k: hb1.at[:, :, cut(k)])
    ga2 = Swap(net, w.yoff, py, lambda j: a1.at[:, j], ga2_b, piece.at[pl.ds(0, 4)])
    gb2 = Swap(net, w.xoff, px, lambda j: b1.at[j], gb2_b, piece.at[pl.ds(4, 4)])
    mine = hall.at[px, py]
    ha2 = Swap(net, w.yoff, py, lambda j: ha1.at[j], ha2_b, mine.at[:, low])
    hb2 = Swap(net, w.xoff, px, lambda j: hb1.at[j], hb2_b, mine.at[:, high])
    ga.start()
    gb.start()
    cp_rows.wait_recv()
    cp_g.wait_recv()

    def spread_t(dz):
        who, how = rall[dz], gall[dz]
        for o in range(2):
            hit = (who >> 9) == z * 2 + o
            spot = jnp.sum(jnp.where(hit, (who & 511) + 1, 0).astype(F32), 0, keepdims=True) - 1.0
            much = jnp.sum(jnp.where(hit, how, 0.0), 0, keepdims=True)
            for j in range(4):
                line = (iota((128, T), 0) + j * 128).astype(F32)
                found[dz // 4 + 2 * o, pl.ds(j * 128, 128), ds(dz % 4, T)] = jnp.where(line == spot, much, 0.0).astype(BF)

    rep(8, spread_t)

    def h_part(o, i):
        y = [yall[pl.ds(4 * k, 4), :, ds(i, 256)].reshape(4 * T, 256) for k in range(2)]
        return mm(found[2 * o], y[0]) + mm(found[2 * o + 1], y[1])

    def h_mate(i):
        hsend[:, ds(i, 256)] = h_part(1 - c, i).astype(BF)

    hop.wait_recv()
    cp_slot.append(slots(7, 9, 6, 10, 5, 11, 4, 12, 3, 13))
    ga.relay()
    gb.relay()
    rep(4, h_mate)
    cp_h = net.go(hsend, hrec, w.mate())
    ga.finish()
    ga2.start()
    gb.finish()
    gb2.start()

    def h_own(i):
        part = h_part(c, i)
        wown[:, ds(i, 256)] = part[:T]
        res[:, ds(i, 256)] = part[T:]

    rep(4, h_own)
    cp_h.wait_recv()
    for part, src in ((0, wown), (1, res)):
        for i in range(8):
            total = src[pl.ds(i * 32, 32)] + hrec[pl.ds(part * T + i * 32, 32)].astype(F32)
            h_v[part * 2 + i // 4, i % 4] = total.astype(BF)
    ha.start()
    hb.start()

    ga2.finish()
    gb2.finish()
    cp_z = net.bundle(zbuf.at[pl.ds(0, 7)], *[(piece.at[(z + k) % 8], zbuf.at[k], w.zoff(k)) for k in range(1, 8)])
    ha.relay()
    hb.relay()
    ha.finish()
    ha2.start()
    hb.finish()
    hb2.start()
    total = piece[z].astype(F32)
    cp_z.wait_recv()
    for k in range(1, 8):
        total = total + zbuf[k].astype(F32)
    wpiece[...] = total.astype(BF)
    cp_sum = net.bundle(wall.at[pl.ds(0, 15)], *[(wpiece, wall.at[g], peer(i, j)) for i, j in plane])
    wall[g] = wpiece[...]
    ha2.finish()
    spread_x = net.bundle(hall.at[0, pl.ds(0, 3), :, low], *[(mine.at[:, low], mine.at[:, low], w.xoff(k)) for k in (2, 1, 3)])
    hb2.finish()
    spread_y = net.bundle(hall.at[0, pl.ds(0, 3), :, high], *[(mine.at[:, high], mine.at[:, high], w.yoff(k)) for k in (2, 1, 3)])
    line_x, line_y = hall.at[:, py, :, low], hall.at[px, :, :, high]
    spread_x.wait_recv()
    cover_x = net.bundle(hall.at[pl.ds(0, 3), :, :, low], *[(line_x, line_x, w.yoff(k)) for k in (2, 1, 3)])
    spread_y.wait_recv()
    cover_y = net.bundle(hall.at[pl.ds(0, 3), :, :, high], *[(line_y, line_y, w.xoff(k)) for k in (2, 1, 3)])

    cp_count.wait_recv()
    for copy in cp_slot:
        copy.wait_recv()
    cnt = jnp.sum(jnp.where(iota((16, 128), 1) == s, cbuf[:, 0, :], 0.0), -1, keepdims=True)
    row, col16 = iota((16, 512), 0), iota((16, 512), 1)
    slot = col16 >> 5
    before = jnp.sum(jnp.where(row < slot, cnt, 0.0), 0, keepdims=True)
    here = jnp.sum(jnp.where(row == slot, cnt, 0.0), 0, keepdims=True)
    inside = (col16[:1] & 31).astype(F32)
    goal = jnp.where(inside < here, before + inside, -1.0)
    chosen = jnp.where(iota((T, 512), 0).astype(F32) == goal, 1.0, 0.0).astype(BF)

    def land(i):
        lay_o[:, ds(i, 256)] = mm(chosen, slots_r[:, :, ds(i, 256)].reshape(512, 256)).astype(BF)

    rep(4, land)
    cp_sum.wait_recv()
    w_o[...] = wall[...]
    cover_x.wait_recv()
    cover_y.wait_recv()
    h_o[...] = hall[...]
    assert net.n == NSEM, net.n
    net.drain()


def train_call(lengths, destinations, hist, neg, events, in_weight, out_weight, item_table):
    vm = lambda *shape, dtype=BF: pltpu.VMEM(shape, dtype)
    f32 = dict(dtype=F32)
    halves = [(2, 4, 16, 640), (4, 2, 16, 640), (4, 32, 256), (4, 32, 256)]
    wholes = [(4, 16, 640), (4, 16, 640), (32, 512), (32, 512)]
    sem = pltpu.SemaphoreType.DMA
    scratch = [
        vm(T, D), vm(D, 4 * HID), vm(D, HID), vm(512, D), vm(8, 4, 4, 32, D), vm(T, D),
        vm(T, 4 * HID, **f32), vm(T, 4 * HID), vm(HEADS, T, T), vm(HEADS, T, T, **f32),
        vm(T, HID, **f32), vm(T, HID, **f32), vm(T, 128, **f32), vm(T, HID), vm(T, HID),
        vm(T, D, **f32), vm(T, 128, **f32), vm(8, T, D), vm(T, D), vm(128, T, **f32), vm(2 * T, 128, dtype=I32),
        vm(8, 8, T, dtype=I32), vm(8, 8, T, **f32), vm(8, T, **f32), vm(2 * T, 128, **f32),
        vm(2 * T, 128, **f32), vm(2 * T, 128, **f32), vm(2 * T, 128, **f32), vm(2 * T, 512),
        vm(8, 2 * T, D), vm(T, D, **f32), vm(T, D), vm(T, D), vm(T, D),
        vm(T, HID, **f32), vm(T, HID), vm(T, 4 * HID), vm(T, 4 * HID), vm(8, 2, 64, T), vm(8, 64, T),
        vm(8, 2, 64, T), vm(8, 64, T), vm(512, D), vm(512, D), vm(T, T, **f32), vm(T, D),
        vm(4, 8, 4, 16, 640), vm(4, 4, 32, D),
        vm(4, 4, 16, 640), vm(4, 4, 16, 640), vm(4, 32, 512), vm(4, 32, 512), vm(8, 16, 640), vm(8, 16, 640),
        vm(16, 640), vm(16, 16, 640), vm(4, 4, 32, D), vm(16, 32, D), vm(16, 32, D),
        vm(8, 128, **f32), vm(16, 8, 128, **f32),
        sem((4,)), sem((NSEM,)), sem((NSEM,)),
    ] + [vm(2, *shape) for shape in halves for _ in range(4)] + [vm(4, *shape) for shape in wholes]
    any_ = pl.BlockSpec(memory_space=pl.ANY)
    vmem = pl.BlockSpec(memory_space=pltpu.VMEM)
    smem = pl.BlockSpec(memory_space=pltpu.SMEM)
    return pl.pallas_call(
        train_kernel,
        out_shape=(jax.ShapeDtypeStruct((T, D), BF), jax.ShapeDtypeStruct((16, 16, 640), BF),
                   jax.ShapeDtypeStruct((4, 4, 32, D), BF)),
        in_specs=[smem, smem, vmem, vmem, any_, any_, any_, any_],
        out_specs=(vmem, vmem, vmem),
        scratch_shapes=scratch,
        compiler_params=pltpu.CompilerParams(collective_id=0, has_side_effects=True, vmem_limit_bytes=VMEM_BYTES),
        name="train",
    )(lengths, destinations, hist, neg, events, in_weight, out_weight, item_table)


def last_kernel(lay, w, h, e, lay_o, in_o, out_o, tab_o):
    lay_o[...] = lay[...]
    rows = jnp.concatenate([w[i, 0] for i in range(4)], 1).astype(F32)
    in_o[...] = rows[:, :4 * HID]
    out_o[...] = rows[:, 4 * HID:]
    item, total = e[...].astype(F32), h[0].reshape(128, D).astype(F32)
    length = lax.rsqrt(jnp.sum(item * item, -1, keepdims=True) + EPS)
    item = item * length
    tab_o[...] = (total - item * jnp.sum(item * total, -1, keepdims=True)) * length


def last_call(lay, w, h, item_table):
    rows = lambda n, m: pl.BlockSpec((n, m), lambda i: (i, 0))
    return pl.pallas_call(
        last_kernel,
        grid=(4,),
        out_shape=(jax.ShapeDtypeStruct((T, D), BF), jax.ShapeDtypeStruct((64, 4 * HID), F32),
                   jax.ShapeDtypeStruct((64, HID), F32), jax.ShapeDtypeStruct((512, D), F32)),
        in_specs=[rows(64, D), pl.BlockSpec((4, 1, 16, 640), lambda i: (0, i, 0, 0)),
                  pl.BlockSpec((1, 4, 32, D), lambda i: (i, 0, 0, 0)), rows(128, D)],
        out_specs=(rows(64, D), rows(16, 4 * HID), rows(16, HID), rows(128, D)),
        name="last",
    )(lay, w, h, item_table)


def body(events, lengths, destinations, history, negatives, in_weight, out_weight, item_table):
    result, wsum, hsum = train_call(lengths, destinations, history.reshape(1, T), negatives.T, events,
                                    in_weight, out_weight, item_table)
    return last_call(result, wsum.reshape(4, 4, 16, 640), hsum, item_table)


def solution(mesh):
    return jax.shard_map(
        body,
        mesh=mesh,
        in_specs=(
            P(("grp", "seq"), None),
            P(("grp", "seq"), None),
            P(("grp", "seq"), None),
            P(("grp", "seq")),
            P(("grp", "seq"), None),
            P(),
            P(),
            P("seq", None),
        ),
        out_specs=(P(("grp", "seq"), None), P("seq", None), P("seq", None), P("seq", None)),
        check_vma=False,
    )
```

```python
import jax
import jax.numpy as jnp
from jax import lax
from jax.experimental import pallas as pl
from jax.experimental.pallas import tpu as pltpu
from jax.sharding import PartitionSpec as P

F32, BF, I32 = jnp.float32, jnp.bfloat16, jnp.int32
MESH = pl.DeviceIdType.MESH
T, D, HID = 256, 1024, 512
HEADS, HEAD_DIM, NCAND = 4, 128, 4
EPS = 1e-5
TEMP = 0.05
SCALE = HEAD_DIM ** -0.5
VMEM_BYTES = 67_000_000


def rep(n, body, unroll=1):
    def step(i, carry):
        body(i)
        return carry

    lax.fori_loop(0, n, step, 0, unroll=unroll)


def ds(i, size):
    return pl.ds(pl.multiple_of(i * size, size), size)


def iota(shape, dim):
    return lax.broadcasted_iota(I32, shape, dim)


def mm(a, b):
    return jnp.dot(a, b, preferred_element_type=F32)


def mm_t(a, b):
    return lax.dot_general(a, b, (((1,), (1,)), ((), ())), preferred_element_type=F32)


def sigmoid(v):
    return 1.0 / (1.0 + jnp.exp(-v))


class Where:
    def __init__(self):
        self.g, self.s = lax.axis_index("grp"), lax.axis_index("seq")
        self.px, self.py = self.g // 4, self.g % 4
        self.z, self.c = self.s // 2, self.s % 2

    def at(self, grp=None, seq=None):
        return {"grp": self.g if grp is None else grp, "seq": self.s if seq is None else seq}

    def zoff(self, k):
        return self.at(seq=((self.z + k) % 8) * 2 + self.c)

    def mate(self):
        return self.at(seq=self.z * 2 + 1 - self.c)

    def xoff(self, k):
        return self.at(grp=((self.px + k) % 4) * 4 + self.py)

    def yoff(self, k):
        return self.at(grp=self.px * 4 + (self.py + k) % 4)


class Links:
    def __init__(self, send, recv):
        self.send, self.recv, self.n, self.sent = send, recv, 0, []

    def describe(self, src, dst, dev):
        return pltpu.make_async_remote_copy(
            src_ref=src, dst_ref=dst, send_sem=self.send.at[self.n], recv_sem=self.recv.at[self.n],
            device_id=dev, device_id_type=MESH)

    def go(self, src, dst, dev):
        return self.bundle(dst, (src, dst, dev))

    def bundle(self, whole, *copies):
        for copy in copies:
            self.describe(*copy).start()
        wait = self.describe(whole, whole, copies[0][2])
        self.n += 1
        self.sent.append(wait)
        return wait

    def drain(self):
        for copy in self.sent:
            copy.wait_send()


class Ring:
    def __init__(self, net, off, i, src, bufs, out):
        self.net, self.off, self.i, self.src, self.out = net, off, i, src, out
        self.t, self.u, self.v, self.r = bufs

    def start(self):
        far, right, left = (self.i + 2) % 4, (self.i + 1) % 4, (self.i + 3) % 4
        off, src, t, u = self.off, self.src, self.t, self.u
        self.ct = self.net.bundle(t, (src(far, 0), t.at[0], off(1)), (src(far, 1), t.at[1], off(-1)))
        self.cu = self.net.bundle(u, (src(left, 0), u.at[0], off(-1)), (src(right, 1), u.at[1], off(1)))

    def relay(self):
        self.ct.wait_recv()
        for k, j in ((0, (self.i + 1) % 4), (1, (self.i + 3) % 4)):
            self.v[k] = (self.t[k].astype(F32) + self.src(j, k)[...].astype(F32)).astype(BF)
        v, r, off = self.v, self.r, self.off
        self.cr = self.net.bundle(r, (v.at[0], r.at[0], off(1)), (v.at[1], r.at[1], off(-1)))

    def finish(self):
        self.cr.wait_recv()
        self.cu.wait_recv()
        for k in range(2):
            total = self.src(self.i, k)[...].astype(F32) + self.r[k].astype(F32) + self.u[k].astype(F32)
            self.out(k)[...] = total.astype(BF)


class Swap:
    def __init__(self, net, off, i, src, buf, out):
        self.net, self.off, self.i, self.src, self.buf, self.out = net, off, i, src, buf, out

    def start(self):
        buf = self.buf
        self.got = self.net.bundle(
            buf.at[pl.ds(1, 3)], *[(self.src((self.i + k) % 4), buf.at[k], self.off(k)) for k in (2, 1, 3)])

    def finish(self):
        self.got.wait_recv()
        total = self.src(self.i)[...].astype(F32)
        for k in range(1, 4):
            total = total + self.buf[k].astype(F32)
        self.out[...] = total.astype(BF)


def call_out(devices):
    barrier = pltpu.get_barrier_semaphore()
    for dev in devices:
        pl.semaphore_signal(barrier, inc=1, device_id=dev, device_id_type=MESH)
    return lambda: pl.semaphore_wait(barrier, len(devices))


NSEM = 93


def train_kernel(len_s, dst_s, hist_v, neg_v, ev_h, win_h, wout_h, tab_h, lay_o, w_o, h_o, *refs):
    (x_v, win, wout, traw, tab, nin, slope, proj, attn, dsl, att, normed, inv, gated, gatedm,
     res, rlen, yall, ymate, ids_f, cand, rall, gall, gsend, lacc, lsum, lsend, lrec, gcol, picks, found,
     wown, wsend, wrec, upb, gg, gatt, gpre, gprem, ninT, ninTm, upT, upTm, hsend, hrec, mask_v, lout,
     g_v, h_v, a1, b1, ha1, hb1, piece, zbuf, wpiece, hpiece, wall, hall, slots_s, slots_r, csend, cbuf,
     lsem, ssem, rsem) = refs[:len(refs) - 20]
    bufs = refs[len(refs) - 20:]
    (ga_b, gb_b, ha_b, hb_b) = [bufs[4 * i:4 * i + 4] for i in range(4)]
    ga2_b, gb2_b, ha2_b, hb2_b = bufs[16:]
    w = Where()
    net = Links(ssem, rsem)
    s, z, c, px, py, g = w.s, w.z, w.c, w.px, w.py, w.g
    plane = [(i, j) for i in range(4) for j in range(4) if (i, j) != (0, 0)]

    def peer(i, j):
        return w.at(grp=((px + i) % 4) * 4 + (py + j) % 4)

    loads = [pltpu.make_async_copy(a, b, lsem.at[i]) for i, (a, b) in enumerate(
        ((tab_h, traw), (ev_h, x_v), (win_h, win), (wout_h, wout)))]
    for copy in loads:
        copy.start()
    for k in range(16):
        slots_r[k, pl.ds(24, 8)] = jnp.zeros((8, D), BF)
    everyone = call_out([w.at(seq=(s + k) % 16) for k in range(1, 16)] + [peer(i, j) for i, j in plane])

    ids_f[...] = jnp.full((128, T), -1.0, F32)
    ids_f[pl.ds(0, 1)] = hist_v[...].astype(F32)
    ids_f[pl.ds(1, 3)] = neg_v[...].astype(F32)
    rall[0] = ids_f[pl.ds(0, 8)].astype(I32)
    cand[pl.ds(0, T)] = ids_f[...].T.astype(I32)

    loads[0].wait()

    def norm_rows(i):
        j = (g + i) % 16
        rows = traw[ds(j, 32)].astype(F32)
        length = lax.rsqrt(jnp.sum(rows * rows, -1, keepdims=True) + EPS)
        tab[0, j // 4, j % 4] = (rows * length).astype(BF)

    norm_rows(0)
    everyone()
    low, high = pl.ds(0, 512), pl.ds(512, 512)
    mine_at = lambda dz, cols: tab.at[dz, px, py, :, cols]
    slice_in = {}
    for a, b in ((1, 7), (2, 6), (3, 5)):
        slice_in[a, b] = net.bundle(
            tab.at[0, 0, pl.ds(0, 2)],
            *[(tab.at[0, px, py], tab.at[8 - k, px, py], w.zoff(k)) for k in (a, b)])
    rep(15, lambda i: norm_rows(i + 1))
    cp_cand = net.go(cand.at[pl.ds(0, T)], cand.at[pl.ds(T, T)], w.mate())

    pieces = {7: (tab.at[7], 0, 1024, "y"), 1: (tab.at[1], 0, 1024, "x"),
              6: (tab.at[6], 0, 1024, "y"), 2: (tab.at[2], 0, 1024, "x"),
              5: (tab.at[5], 0, 1024, "y"), 3: (tab.at[3], 0, 1024, "x"),
              "4x": (tab.at[4], 0, 512, "x"), "4y": (tab.at[4], 512, 512, "y")}
    flying, early = {}, {}

    def one(piece, kx, ky, c0, nc):
        return piece[0].at[(px + kx) % 4, (py + ky) % 4, :, pl.ds(c0, nc)]

    def many(piece, k, c0, nc):
        if piece[3] == "x":
            return piece[0].at[:, (py + k) % 4, :, pl.ds(c0, nc)]
        return piece[0].at[(px + k) % 4, :, :, pl.ds(c0, nc)]

    def pair(name, whole, right, left, off):
        flying[name] = net.bundle(whole, (right, right, off(1)), (left, left, off(-1)))

    def first_send(name):
        p = pieces[name]
        own = one(p, 0, 0, p[1], p[2])
        whole = p[0].at[0, pl.ds(0, 2), :, pl.ds(p[1], p[2])]
        across = w.yoff if p[3] == "x" else w.xoff
        pair(name, whole, own, own, w.xoff if p[3] == "x" else w.yoff)
        early[name] = net.bundle(whole, (own, own, across(1)), (own, own, across(-1)))

    def first_forward(name):
        p = pieces[name]
        half = p[2] // 2
        at = (lambda k, c0: one(p, k, 0, c0, half)) if p[3] == "x" else (lambda k, c0: one(p, 0, k, c0, half))
        flying[name].wait_recv()
        pair(name, one(p, 0, 0, p[1], p[2]), at(-1, p[1]), at(1, p[1] + half), w.xoff if p[3] == "x" else w.yoff)

    def second_send(name):
        p = pieces[name]
        flying[name].wait_recv()
        across = w.yoff if p[3] == "x" else w.xoff
        others = [one(p, k, 0, p[1], p[2]) if p[3] == "x" else one(p, 0, k, p[1], p[2]) for k in (1, 3, 2)]
        flying[name] = net.bundle(
            p[0].at[pl.ds(0, 2), pl.ds(0, 3), :, pl.ds(p[1], p[2])],
            *[(ref, ref, across(d)) for ref in others for d in (1, -1)])

    def second_forward(name):
        p = pieces[name]
        half = p[2] // 2
        early[name].wait_recv()
        flying[name].wait_recv()
        pair(name, many(p, 0, p[1], p[2]), many(p, -1, p[1], half), many(p, 1, p[1] + half, half),
             w.yoff if p[3] == "x" else w.xoff)

    def step(stage, *names):
        for name in names:
            stage(name)

    def slices(a, b):
        slice_in[a, b].wait_recv()

    ends = []
    for j in range(16):
        ends.append(len_s[0, j] + (ends[-1] if ends else 0))
    tc, tr = iota((T, 128), 0), iota((8, T), 1)
    uid_c, uid_r = jnp.zeros((T, 128), I32), jnp.zeros((8, T), I32)
    for end in ends:
        uid_c = uid_c + (tc >= end).astype(I32)
        uid_r = uid_r + (tr >= end).astype(I32)
    same = (uid_c[:, :1] == uid_r[:1, :]) & (iota((T, T), 1) <= iota((T, T), 0))
    mask_v[...] = same.astype(F32)

    loads[1].wait()

    def norm_in(i):
        v = x_v[ds(i, 32)].astype(F32)
        v = v - jnp.mean(v, -1, keepdims=True)
        nin[ds(i, 32)] = (v * lax.rsqrt(jnp.mean(v * v, -1, keepdims=True) + EPS)).astype(BF)

    rep(8, norm_in, 2)
    loads[2].wait()
    loads[3].wait()

    def project(i):
        pre = mm(nin[...], win[:, ds(i, 256)])
        sg = sigmoid(pre)
        proj[:, ds(i, 256)] = (pre * sg).astype(BF)
        slope[:, ds(i, 256)] = sg * (1.0 + pre * (1.0 - sg))

    rep(2, project)
    slices(1, 7)
    step(first_send, 1, 7)
    rep(3, lambda i: project(i + 2))
    slices(2, 6)
    step(first_send, 2, 6)
    rep(3, lambda i: project(i + 5))
    step(first_forward, 1, 7)

    def flip_in(i):
        block = nin[:, ds(i, 128)].astype(F32).T
        ninT[i] = block.astype(BF).reshape(2, 64, T)

    def attend(h):
        col = lambda part: pl.ds(pl.multiple_of(part * HID + h * 128, 128), 128)
        scores = mm_t(proj[:, col(2)], proj[:, col(3)]) * SCALE
        sg = sigmoid(scores)
        mask = mask_v[...]
        weight = (scores * sg * mask).astype(BF)
        attn[h] = weight
        dsl[h] = sg * (1.0 + scores * (1.0 - sg)) * SCALE * mask
        att[:, ds(h, 128)] = mm(weight, proj[:, col(1)])

    rep(2, attend)
    slices(3, 5)
    slice_in["4r", "4l"] = net.bundle(
        tab.at[0, 0, 0], (mine_at(5, low), mine_at(4, low), w.zoff(1)), (mine_at(3, high), mine_at(4, high), w.zoff(-1)))
    step(first_send, 3, 5)
    step(first_forward, 2, 6)
    rep(2, lambda h: attend(h + 2))
    step(second_send, 1, 7)

    def norm_att(i):
        v = att[ds(i, 32)]
        v = v - jnp.mean(v, -1, keepdims=True)
        f = lax.rsqrt(jnp.mean(v * v, -1, keepdims=True) + EPS)
        n = v * f
        normed[ds(i, 32)] = n
        inv[ds(i, 32)] = jnp.broadcast_to(f, (32, 128))
        gated[ds(i, 32)] = (n * proj[ds(i, 32), pl.ds(0, HID)].astype(F32)).astype(BF)

    rep(8, norm_att, 2)
    slices("4r", "4l")
    step(first_send, "4x", "4y")
    step(first_forward, 3, 5)
    step(second_send, 2, 6)

    def result(i):
        res[:, ds(i, 256)] = x_v[:, ds(i, 256)].astype(F32) + mm_t(gated[...], wout[ds(i, 256)])

    rep(4, result)

    def norm_out(i):
        v = res[ds(i, 32)]
        f = lax.rsqrt(jnp.sum(v * v, -1, keepdims=True) + EPS)
        rlen[ds(i, 32)] = jnp.broadcast_to(f, (32, 128))
        yall[0, ds(i, 32)] = (v * f).astype(BF)
        lout[ds(i, 32)] = v.astype(BF)

    rep(8, norm_out, 2)
    cp_y = net.go(yall.at[0], ymate, w.mate())
    two_y = yall.at[pl.ds(0, 2)]
    hop = net.bundle(two_y, (yall.at[0], yall.at[7], w.zoff(1)), (yall.at[0], yall.at[1], w.zoff(-1)))
    cp_rows = net.bundle(rall.at[pl.ds(0, 7)], *[(rall.at[0], rall.at[8 - k], w.zoff(k)) for k in range(1, 8)])
    lane8 = iota((8, 128), 1)
    counts = jnp.zeros((8, 128), F32)
    place = jnp.zeros((8, T), I32)
    start = 0
    for j in range(16):
        n, d = len_s[0, j], dst_s[0, j]
        counts = counts + jnp.where(lane8 == d, n, 0).astype(F32)
        place = jnp.where((tr >= start) & (tr < start + n), d * 32 + tr - start, place)
        start = start + n
    csend[...] = counts
    cbuf[s] = csend[...]

    def fill(i):
        pick = jnp.where(iota((128, T), 0) + i * 128 == place[:1, :], 1.0, 0.0).astype(BF)
        slots_s[pl.ds(i * 4, 4)] = mm(pick, lout[...]).astype(BF).reshape(4, 32, D)

    used = pl.ds(0, 24)
    rep(4, fill)
    slots_r[s, used] = slots_s[s, used]
    cp_count = net.bundle(cbuf.at[pl.ds(0, 15)], *[(csend, cbuf.at[s], w.at(seq=(s + k) % 16)) for k in range(1, 16)])

    def slots(*ks):
        return net.bundle(
            slots_r.at[pl.ds(0, len(ks)), used],
            *[(slots_s.at[(s + k) % 16, used], slots_r.at[s, used], w.at(seq=(s + k) % 16)) for k in ks])

    cp_slot = [slots(8, 1, 15, 2, 14)]

    step(first_forward, "4x", "4y")
    rep(8, flip_in)
    step(second_forward, 1, 7)
    step(second_send, 3, 5)
    cp_nin = net.go(ninT.at[:, 1 - c], ninTm, w.mate())
    cp_gated = net.go(gated, gatedm, w.mate())

    lsum[...] = jnp.zeros_like(lsum)
    lanes = iota((256, 128), 1).astype(F32)
    cp_cand.wait_recv()

    def owner(dz):
        return ((z + dz) % 8) * 2 + c

    def aim(dz):
        def part(i):
            who = cand[ds(i, 256)]
            spot = jnp.where((who >> 9) == owner(dz), (who & 511) + 1, 0).astype(F32)
            spot = jnp.broadcast_to(jnp.sum(spot, -1, keepdims=True) - 1.0, (256, 128))
            for q in range(4):
                picks[ds(i, 256), pl.ds(q * 128, 128)] = jnp.where(spot == lanes + 128.0 * q, 1.0, 0.0).astype(BF)
            lacc[ds(i, 256)] = jnp.zeros((256, 128), F32)

        rep(2, part)

    def score(dz):
        def part(i):
            rows = mm(picks[...], tab[dz, :, :, :, ds(i, 256)].reshape(512, 256))
            found[dz, :, ds(i, 256)] = rows.astype(BF)
            for first, y in ((0, yall[0, :, ds(i, 256)]), (T, ymate[:, ds(i, 256)])):
                got = rows[first:first + T] * y.astype(F32)
                lacc[pl.ds(first, T)] += got[:, :128] + got[:, 128:]

        rep(4, part)

        def close(i):
            value = jnp.sum(lacc[ds(i, 256)], -1, keepdims=True)
            lsum[ds(i, 256)] += jnp.where((cand[ds(i, 256)] >> 9) == owner(dz), value, 0.0)

        rep(2, close)

    def settle(*names):
        for name in names:
            flying[name].wait_recv()

    aim(0)
    cp_y.wait_recv()
    score(0)
    step(second_send, "4x", "4y")
    aim(1)
    settle(1, 7)
    step(second_forward, 2, 6)
    score(1)
    aim(7)
    score(7)
    hop.wait_recv()
    hop = net.bundle(two_y, (yall.at[7], yall.at[6], w.zoff(1)), (yall.at[1], yall.at[2], w.zoff(-1)))
    aim(2)
    settle(2, 6)
    step(second_forward, 3, 5)
    score(2)
    aim(6)
    score(6)
    step(second_forward, "4x", "4y")
    aim(3)
    settle(3, 5)
    score(3)
    aim(5)
    score(5)
    aim(4)
    settle("4x", "4y")
    score(4)
    lsend[...] = lsum[...].T[:8]
    cp_l = net.go(lsend, lrec, w.mate())
    cp_l.wait_recv()
    other = lrec[...]
    logits = (lsend[...] + jnp.concatenate([other[:, T:], other[:, :T]], 1)) / TEMP
    cand_no = iota((8, 2 * T), 0)
    live = cand_no < NCAND
    ex = jnp.where(live, jnp.exp(jnp.where(live, logits, 0.0)), 0.0)
    soft = ex / jnp.sum(ex, 0, keepdims=True)
    coef = jnp.where(live, soft - (cand_no == 0).astype(F32), 0.0) / TEMP
    gsend[...] = coef[:, :T]
    gall[0] = coef[:, :T]
    gcol[...] = jnp.concatenate([coef, jnp.zeros((120, 2 * T), F32)], 0).T

    cp_g = net.bundle(gall.at[pl.ds(0, 7)], *[(gsend, gall.at[8 - k], w.zoff(k)) for k in range(1, 8)])

    hop.wait_recv()
    hop = net.bundle(two_y, (yall.at[6], yall.at[5], w.zoff(1)), (yall.at[2], yall.at[3], w.zoff(-1)))

    def blend(at):
        who, how = cand[at] >> 9, gcol[at]
        total = jnp.zeros((32, D), F32)
        for dz in range(8):
            much = jnp.sum(jnp.where(who == owner(dz), how, 0.0), -1, keepdims=True)
            total = total + much * found[dz, at].astype(F32)
        return total

    def gather_mate(i):
        wsend[ds(i, 32)] = blend(ds(i + 8, 32)).astype(BF)

    rep(8, gather_mate)
    cp_w = net.go(wsend, wrec, w.mate())

    def gather_own(i):
        wown[ds(i, 32)] = blend(ds(i, 32))

    rep(8, gather_own)
    cp_w.wait_recv()

    def upstream(i):
        f = rlen[ds(i, 32)][:, :1]
        yn = res[ds(i, 32)] * f
        v = wown[ds(i, 32)] + wrec[ds(i, 32)].astype(F32)
        up = (v - yn * jnp.sum(yn * v, -1, keepdims=True)) * f
        upb[ds(i, 32)] = up.astype(BF)

    rep(8, upstream, 2)

    gg[...] = mm(upb[...], wout[...])

    def back_norm(i):
        n, v = normed[ds(i, 32)], gg[ds(i, 32)]
        gpre[ds(i, 32), pl.ds(0, HID)] = (v * n * slope[ds(i, 32), pl.ds(0, HID)]).astype(BF)
        v = v * proj[ds(i, 32), pl.ds(0, HID)].astype(F32)
        v = v - jnp.mean(v, -1, keepdims=True) - n * jnp.mean(v * n, -1, keepdims=True)
        gatt[ds(i, 32)] = (inv[ds(i, 32)][:, :1] * v).astype(BF)

    rep(8, back_norm, 2)

    def flip_up(i):
        block = upb[:, ds(i, 128)].astype(F32).T
        upT[i] = block.astype(BF).reshape(2, 64, T)

    cp_pre = net.go(gpre.at[:, pl.ds(0, HID)], gprem.at[:, pl.ds(0, HID)], w.mate())
    rep(8, flip_up)
    cp_up = net.go(upT.at[:, 1 - c], upTm, w.mate())

    def back_attend(h):
        col = lambda part: pl.ds(pl.multiple_of(part * HID + h * 128, 128), 128)
        da = gatt[:, ds(h, 128)]
        ds_ = (mm_t(da, proj[:, col(1)]) * dsl[h])
        gv = mm(attn[h].astype(F32).T.astype(BF), da)
        gq = mm(ds_.astype(BF), proj[:, col(3)])
        gk = mm(ds_.T.astype(BF), proj[:, col(2)])
        gpre[:, col(1)] = (gv * slope[:, col(1)]).astype(BF)
        gpre[:, col(2)] = (gq * slope[:, col(2)]).astype(BF)
        gpre[:, col(3)] = (gk * slope[:, col(3)]).astype(BF)

    rep(4, back_attend)
    rest = pl.ds(HID, 3 * HID)
    cp_rest = net.go(gpre.at[:, rest], gprem.at[:, rest], w.mate())

    def store_g(i, first, block):
        for b in range(block.shape[1] // 128):
            n = first + b
            if n < 4:
                group, at = n // 2, n % 2
            elif n < 16:
                group, at = (n - 4) // 3, 2 + (n - 4) % 3
            else:
                group, at = 2 + (n - 16) // 2, n % 2
            g_v[group, pl.ds(i * 4, 4), :, :, pl.ds(at * 128, 128)] = (
                block[:, b * 128:(b + 1) * 128].astype(BF).reshape(4, 4, 16, 128))

    two = lambda k: pl.ds(2 * k, 2)
    cut = lambda k: pl.ds(256 * k, 256)
    hicut = lambda k: pl.ds(512 + 256 * k, 256)

    def g_rings(cols):
        cut = lambda bufs: [buf.at[:, :, :, :, cols] for buf in bufs]
        return (
            Ring(net, w.xoff, px, lambda j, k: g_v.at[j, two(k), :, :, cols], cut(ga_b),
                 lambda k: a1.at[two(k), :, :, cols]),
            Ring(net, w.yoff, py, lambda j, k: g_v.at[:, pl.ds(4 + 2 * k, 2), j, :, cols], cut(gb_b),
                 lambda k: b1.at[:, two(k), :, cols]))

    ga, gb = g_rings(pl.ds(0, 256))
    gc, gd = g_rings(pl.ds(256, 384))
    ha = Ring(net, w.xoff, px, lambda j, k: h_v.at[j, :, :, cut(k)], ha_b, lambda k: ha1.at[:, :, cut(k)])
    hb = Ring(net, w.yoff, py, lambda j, k: h_v.at[:, j, :, hicut(k)], hb_b, lambda k: hb1.at[:, :, cut(k)])
    ga2 = Swap(net, w.yoff, py, lambda j: a1.at[:, j], ga2_b, piece.at[pl.ds(0, 4)])
    gb2 = Swap(net, w.xoff, px, lambda j: b1.at[j], gb2_b, piece.at[pl.ds(4, 4)])
    mine = hall.at[px, py]
    ha2 = Swap(net, w.yoff, py, lambda j: ha1.at[j], ha2_b, hpiece.at[:, low])
    hb2 = Swap(net, w.xoff, px, lambda j: hb1.at[j], hb2_b, hpiece.at[:, high])
    cp_gated.wait_recv()
    cp_up.wait_recv()
    cp_nin.wait_recv()
    cp_pre.wait_recv()

    def grad_out(i):
        a = upT[pl.ds(i * 4, 4), c].reshape(T, T)
        b = upTm[pl.ds(i * 4, 4)].reshape(T, T)
        store_g(i, 16, mm(a, gated[...]) + mm(b, gatedm[...]))

    def grad_in(i, blocks):
        a = ninT[pl.ds(i * 4, 4), c].reshape(T, T)
        b = ninTm[pl.ds(i * 4, 4)].reshape(T, T)
        for n in blocks:
            cols = pl.ds(n * 512, 512)
            store_g(i, n * 4, mm(a, gpre[:, cols]) + mm(b, gprem[:, cols]))

    def grad_first(i):
        grad_out(i)
        grad_in(i, (0,))

    rep(2, grad_first)
    ga.start()
    gb.start()
    cp_rows.wait_recv()
    cp_g.wait_recv()

    def spread_t(dz):
        who, how = rall[dz], gall[dz]
        for o in range(2):
            hit = (who >> 9) == z * 2 + o
            spot = jnp.sum(jnp.where(hit, (who & 511) + 1, 0).astype(F32), 0, keepdims=True) - 1.0
            much = jnp.sum(jnp.where(hit, how, 0.0), 0, keepdims=True)
            for j in range(4):
                line = (iota((128, T), 0) + j * 128).astype(F32)
                found[dz // 4 + 2 * o, pl.ds(j * 128, 128), ds(dz % 4, T)] = jnp.where(line == spot, much, 0.0).astype(BF)

    rep(8, spread_t)

    cp_rest.wait_recv()
    rep(2, lambda i: grad_in(i, (1, 2, 3)))
    gc.start()
    gd.start()

    def h_part(o, k, i):
        total = jnp.zeros((2 * T, 256), F32)
        for plane_no, first, n in ((0, 0, 3), (1, 2, 2)) if k == 0 else ((0, 3, 1), (1, 0, 2)):
            y = yall[pl.ds(plane_no * 4 + first, n), :, ds(i, 256)].reshape(n * T, 256)
            total = total + mm(found[2 * o + plane_no, :, pl.ds(first * T, n * T)], y)
        return total

    def h_first(i):
        part = h_part(1 - c, 0, i)
        slope[:, ds(i, 256)] = part[:T]
        slope[:, ds(i + 4, 256)] = part[T:]
        part = h_part(c, 0, i)
        wown[:, ds(i, 256)] = part[:T]
        res[:, ds(i, 256)] = part[T:]

    def h_mate(i):
        part = h_part(1 - c, 1, i)
        hsend[pl.ds(0, T), ds(i, 256)] = (part[:T] + slope[:, ds(i, 256)]).astype(BF)
        hsend[pl.ds(T, T), ds(i, 256)] = (part[T:] + slope[:, ds(i + 4, 256)]).astype(BF)

    def h_own(i):
        part = h_part(c, 1, i)
        wown[:, ds(i, 256)] += part[:T]
        res[:, ds(i, 256)] += part[T:]

    rep(4, h_first)
    hop.wait_recv()
    a, b = pl.ds(0, 512), pl.ds(512, 512)
    hop = net.bundle(yall.at[0], (yall.at[5, :, a], yall.at[4, :, a], w.zoff(1)),
                     (yall.at[3, :, b], yall.at[4, :, b], w.zoff(-1)))
    for ring in (ga, gb, gc, gd):
        ring.relay()
    for ring in (ga, gb, gc, gd):
        ring.finish()
    ga2.start()
    gb2.start()
    hop.wait_recv()
    rep(4, h_mate)
    cp_h = net.go(hsend, hrec, w.mate())
    rep(4, h_own)
    cp_h.wait_recv()
    for part, src in ((0, wown), (1, res)):
        for i in range(8):
            total = src[pl.ds(i * 32, 32)] + hrec[pl.ds(part * T + i * 32, 32)].astype(F32)
            h_v[part * 2 + i // 4, i % 4] = total.astype(BF)
    ha.start()
    hb.start()
    ga2.finish()
    gb2.finish()
    cp_z = net.bundle(zbuf.at[pl.ds(0, 7)], *[(piece.at[(z + k) % 8], zbuf.at[k], w.zoff(k)) for k in range(1, 8)])
    ha.relay()
    hb.relay()
    total = piece[z].astype(F32)
    cp_z.wait_recv()
    cp_slot.append(slots(7, 9, 6, 10, 5, 11, 4, 12, 3, 13))
    for k in range(1, 8):
        total = total + zbuf[k].astype(F32)
    wpiece[...] = total.astype(BF)
    ha.finish()
    ha2.start()
    hb.finish()
    hb2.start()
    cp_sum = net.bundle(wall.at[pl.ds(0, 15)], *[(wpiece, wall.at[g], peer(i, j)) for i, j in plane])
    wall[g] = wpiece[...]
    ha2.finish()
    hb2.finish()
    rows = traw[ds(g, 32)].astype(F32)
    length = lax.rsqrt(jnp.sum(rows * rows, -1, keepdims=True) + EPS)
    rows, total = rows * length, hpiece[...].astype(F32)
    mine[...] = ((total - rows * jnp.sum(rows * total, -1, keepdims=True)) * length).astype(BF)
    hops = (2, 1, 3)
    plans = (("x", low, w.xoff, w.yoff), ("y", high, w.yoff, w.xoff))
    spread, cross = {}, {}
    for name, cols, along, over in plans:
        part, whole = mine.at[:, cols], hall.at[0, pl.ds(0, 3), :, cols]
        spread[name] = net.bundle(whole, *[(part, part, along(k)) for k in hops])
        cross[name] = net.bundle(whole, *[(part, part, over(k)) for k in hops])
    cover = []
    for name, cols, along, over in plans:
        parts = [hall.at[(px + k) % 4, py, :, cols] if name == "x" else hall.at[px, (py + k) % 4, :, cols] for k in hops]
        spread[name].wait_recv()
        cover.append(net.bundle(hall.at[pl.ds(0, 3), pl.ds(0, 3), :, cols],
                                *[(part, part, over(k)) for k in hops for part in parts]))

    cp_count.wait_recv()
    for copy in cp_slot:
        copy.wait_recv()
    cnt = jnp.sum(jnp.where(iota((16, 128), 1) == s, cbuf[:, 0, :], 0.0), -1, keepdims=True)
    row, col16 = iota((16, 512), 0), iota((16, 512), 1)
    slot = col16 >> 5
    before = jnp.sum(jnp.where(row < slot, cnt, 0.0), 0, keepdims=True)
    here = jnp.sum(jnp.where(row == slot, cnt, 0.0), 0, keepdims=True)
    inside = (col16[:1] & 31).astype(F32)
    goal = jnp.where(inside < here, before + inside, -1.0)
    chosen = jnp.where(iota((T, 512), 0).astype(F32) == goal, 1.0, 0.0).astype(BF)

    def land(i):
        lay_o[:, ds(i, 256)] = mm(chosen, slots_r[:, :, ds(i, 256)].reshape(512, 256)).astype(BF)

    rep(4, land)
    cp_sum.wait_recv()
    w_o[...] = wall[...]
    for copy in cover + [cross["x"], cross["y"]]:
        copy.wait_recv()
    h_o[...] = hall[...]
    assert net.n == NSEM, net.n
    net.drain()


def train_call(lengths, destinations, hist, neg, events, in_weight, out_weight, item_table):
    vm = lambda *shape, dtype=BF: pltpu.VMEM(shape, dtype)
    f32 = dict(dtype=F32)
    halves = [(2, 4, 16, 640), (4, 2, 16, 640), (4, 32, 256), (4, 32, 256)]
    wholes = [(4, 16, 640), (4, 16, 640), (32, 512), (32, 512)]
    sem = pltpu.SemaphoreType.DMA
    scratch = [
        vm(T, D), vm(D, 4 * HID), vm(D, HID), vm(512, D), vm(8, 4, 4, 32, D), vm(T, D),
        vm(T, 4 * HID, **f32), vm(T, 4 * HID), vm(HEADS, T, T), vm(HEADS, T, T, **f32),
        vm(T, HID, **f32), vm(T, HID, **f32), vm(T, 128, **f32), vm(T, HID), vm(T, HID),
        vm(T, D, **f32), vm(T, 128, **f32), vm(8, T, D), vm(T, D), vm(128, T, **f32), vm(2 * T, 128, dtype=I32),
        vm(8, 8, T, dtype=I32), vm(8, 8, T, **f32), vm(8, T, **f32), vm(2 * T, 128, **f32),
        vm(2 * T, 128, **f32), vm(8, 2 * T, **f32), vm(8, 2 * T, **f32), vm(2 * T, 128, **f32), vm(2 * T, 512),
        vm(8, 2 * T, D), vm(T, D, **f32), vm(T, D), vm(T, D), vm(T, D),
        vm(T, HID, **f32), vm(T, HID), vm(T, 4 * HID), vm(T, 4 * HID), vm(8, 2, 64, T), vm(8, 64, T),
        vm(8, 2, 64, T), vm(8, 64, T), vm(512, D), vm(512, D), vm(T, T, **f32), vm(T, D),
        vm(4, 8, 4, 16, 640), vm(4, 4, 32, D),
        vm(4, 4, 16, 640), vm(4, 4, 16, 640), vm(4, 32, 512), vm(4, 32, 512), vm(8, 16, 640), vm(8, 16, 640),
        vm(16, 640), vm(32, D), vm(16, 16, 640), vm(4, 4, 32, D), vm(16, 32, D), vm(16, 32, D),
        vm(8, 128, **f32), vm(16, 8, 128, **f32),
        sem((4,)), sem((NSEM,)), sem((NSEM,)),
    ] + [vm(2, *shape) for shape in halves for _ in range(4)] + [vm(4, *shape) for shape in wholes]
    any_ = pl.BlockSpec(memory_space=pl.ANY)
    vmem = pl.BlockSpec(memory_space=pltpu.VMEM)
    smem = pl.BlockSpec(memory_space=pltpu.SMEM)
    return pl.pallas_call(
        train_kernel,
        out_shape=(jax.ShapeDtypeStruct((T, D), BF), jax.ShapeDtypeStruct((16, 16, 640), BF),
                   jax.ShapeDtypeStruct((4, 4, 32, D), BF)),
        in_specs=[smem, smem, vmem, vmem, any_, any_, any_, any_],
        out_specs=(vmem, vmem, vmem),
        scratch_shapes=scratch,
        compiler_params=pltpu.CompilerParams(collective_id=0, has_side_effects=True, vmem_limit_bytes=VMEM_BYTES),
        name="train",
    )(lengths, destinations, hist, neg, events, in_weight, out_weight, item_table)


def last_kernel(lay, w, h, lay_o, in_o, out_o, tab_o):
    lay_o[...] = lay[...]
    part = lambda i, a, b: w[i, 0][:, a:b].astype(F32)
    in_o[...] = jnp.concatenate([part(0, 0, 256), part(1, 0, 256)] + [part(i, 256, 640) for i in range(4)], 1)
    out_o[...] = jnp.concatenate([part(2, 0, 256), part(3, 0, 256)], 1)
    tab_o[...] = h[0].reshape(128, D).astype(F32)


def last_call(lay, w, h):
    rows = lambda n, m: pl.BlockSpec((n, m), lambda i: (i, 0))
    return pl.pallas_call(
        last_kernel,
        grid=(4,),
        out_shape=(jax.ShapeDtypeStruct((T, D), BF), jax.ShapeDtypeStruct((64, 4 * HID), F32),
                   jax.ShapeDtypeStruct((64, HID), F32), jax.ShapeDtypeStruct((512, D), F32)),
        in_specs=[rows(64, D), pl.BlockSpec((4, 1, 16, 640), lambda i: (0, i, 0, 0)),
                  pl.BlockSpec((1, 4, 32, D), lambda i: (i, 0, 0, 0))],
        out_specs=(rows(64, D), rows(16, 4 * HID), rows(16, HID), rows(128, D)),
        name="last",
    )(lay, w, h)


def body(events, lengths, destinations, history, negatives, in_weight, out_weight, item_table):
    result, wsum, hsum = train_call(lengths, destinations, history.reshape(1, T), negatives.T, events,
                                    in_weight, out_weight, item_table)
    return last_call(result, wsum.reshape(4, 4, 16, 640), hsum)


def solution(mesh):
    return jax.shard_map(
        body,
        mesh=mesh,
        in_specs=(
            P(("grp", "seq"), None),
            P(("grp", "seq"), None),
            P(("grp", "seq"), None),
            P(("grp", "seq")),
            P(("grp", "seq"), None),
            P(),
            P(),
            P("seq", None),
        ),
        out_specs=(P(("grp", "seq"), None), P("seq", None), P("seq", None), P("seq", None)),
        check_vma=False,
    )
```

```python
import jax
import jax.numpy as jnp
from jax import lax
from jax.experimental import pallas as pl
from jax.experimental.pallas import tpu as pltpu
from jax.sharding import PartitionSpec as P

F32, BF, I32 = jnp.float32, jnp.bfloat16, jnp.int32
MESH = pl.DeviceIdType.MESH
T, D, HID = 256, 1024, 512
HEADS, HEAD_DIM, NCAND = 4, 128, 4
EPS = 1e-5
TEMP = 0.05
SCALE = HEAD_DIM ** -0.5
VMEM_BYTES = 67_000_000


def rep(n, body, unroll=1):
    def step(i, carry):
        body(i)
        return carry

    lax.fori_loop(0, n, step, 0, unroll=unroll)


def ds(i, size):
    return pl.ds(pl.multiple_of(i * size, size), size)


def iota(shape, dim):
    return lax.broadcasted_iota(I32, shape, dim)


def mm(a, b):
    return jnp.dot(a, b, preferred_element_type=F32)


def mm_t(a, b):
    return lax.dot_general(a, b, (((1,), (1,)), ((), ())), preferred_element_type=F32)


def sigmoid(v):
    return 1.0 / (1.0 + jnp.exp(-v))


class Where:
    def __init__(self):
        self.g, self.s = lax.axis_index("grp"), lax.axis_index("seq")
        self.px, self.py = self.g // 4, self.g % 4
        self.z, self.c = self.s // 2, self.s % 2

    def at(self, grp=None, seq=None):
        return {"grp": self.g if grp is None else grp, "seq": self.s if seq is None else seq}

    def zoff(self, k):
        return self.at(seq=((self.z + k) % 8) * 2 + self.c)

    def mate(self):
        return self.at(seq=self.z * 2 + 1 - self.c)

    def xoff(self, k):
        return self.at(grp=((self.px + k) % 4) * 4 + self.py)

    def yoff(self, k):
        return self.at(grp=self.px * 4 + (self.py + k) % 4)


class Links:
    def __init__(self, send, recv):
        self.send, self.recv, self.n, self.sent = send, recv, 0, []

    def describe(self, src, dst, dev):
        return pltpu.make_async_remote_copy(
            src_ref=src, dst_ref=dst, send_sem=self.send.at[self.n], recv_sem=self.recv.at[self.n],
            device_id=dev, device_id_type=MESH)

    def go(self, src, dst, dev):
        return self.bundle(dst, (src, dst, dev))

    def bundle(self, whole, *copies):
        for copy in copies:
            self.describe(*copy).start()
        wait = self.describe(whole, whole, copies[0][2])
        self.n += 1
        self.sent.append(wait)
        return wait

    def drain(self):
        for copy in self.sent:
            copy.wait_send()


class Ring:
    def __init__(self, net, off, i, src, bufs, out):
        self.net, self.off, self.i, self.src, self.out = net, off, i, src, out
        self.t, self.u, self.v, self.r = bufs

    def start(self):
        far, right, left = (self.i + 2) % 4, (self.i + 1) % 4, (self.i + 3) % 4
        off, src, t, u = self.off, self.src, self.t, self.u
        self.ct = self.net.bundle(t, (src(far, 0), t.at[0], off(1)), (src(far, 1), t.at[1], off(-1)))
        self.cu = self.net.bundle(u, (src(left, 0), u.at[0], off(-1)), (src(right, 1), u.at[1], off(1)))

    def relay(self):
        self.ct.wait_recv()
        for k, j in ((0, (self.i + 1) % 4), (1, (self.i + 3) % 4)):
            self.v[k] = (self.t[k].astype(F32) + self.src(j, k)[...].astype(F32)).astype(BF)
        v, r, off = self.v, self.r, self.off
        self.cr = self.net.bundle(r, (v.at[0], r.at[0], off(1)), (v.at[1], r.at[1], off(-1)))

    def finish(self):
        self.cr.wait_recv()
        self.cu.wait_recv()
        for k in range(2):
            total = self.src(self.i, k)[...].astype(F32) + self.r[k].astype(F32) + self.u[k].astype(F32)
            self.out(k)[...] = total.astype(BF)


class Swap:
    def __init__(self, net, off, i, src, buf, out):
        self.net, self.off, self.i, self.src, self.buf, self.out = net, off, i, src, buf, out

    def start(self):
        buf = self.buf
        self.got = self.net.bundle(
            buf.at[pl.ds(1, 3)], *[(self.src((self.i + k) % 4), buf.at[k], self.off(k)) for k in (2, 1, 3)])

    def finish(self):
        self.got.wait_recv()
        total = self.src(self.i)[...].astype(F32)
        for k in range(1, 4):
            total = total + self.buf[k].astype(F32)
        self.out[...] = total.astype(BF)


def call_out(devices):
    barrier = pltpu.get_barrier_semaphore()
    for dev in devices:
        pl.semaphore_signal(barrier, inc=1, device_id=dev, device_id_type=MESH)
    return lambda: pl.semaphore_wait(barrier, len(devices))


NSEM = 93


def train_kernel(len_s, dst_s, hist_v, neg_v, ev_h, win_h, wout_h, tab_h, lay_o, w_o, h_o, *refs):
    (x_v, win, wout, traw, tab, nin, slope, proj, attn, dsl, att, normed, inv, gated, gatedm,
     res, rlen, yall, ymate, ids_f, cand, rall, gall, gsend, lacc, lsum, lsend, lrec, gcol, picks, found,
     wown, wsend, wrec, upb, gg, gatt, gpre, gprem, ninT, ninTm, upT, upTm, hsend, hrec, mask_v, lout,
     g_v, h_v, a1, b1, ha1, hb1, piece, zbuf, wpiece, hpiece, wall, hall, slots_s, slots_r, csend, cbuf,
     lsem, ssem, rsem) = refs[:len(refs) - 20]
    bufs = refs[len(refs) - 20:]
    (ga_b, gb_b, ha_b, hb_b) = [bufs[4 * i:4 * i + 4] for i in range(4)]
    ga2_b, gb2_b, ha2_b, hb2_b = bufs[16:]
    w = Where()
    net = Links(ssem, rsem)
    s, z, c, px, py, g = w.s, w.z, w.c, w.px, w.py, w.g
    plane = [(i, j) for i in range(4) for j in range(4) if (i, j) != (0, 0)]

    def peer(i, j):
        return w.at(grp=((px + i) % 4) * 4 + (py + j) % 4)

    loads = [pltpu.make_async_copy(a, b, lsem.at[i]) for i, (a, b) in enumerate(
        ((tab_h, traw), (ev_h, x_v), (win_h, win), (wout_h, wout)))]
    for copy in loads:
        copy.start()
    everyone = call_out([w.at(seq=(s + k) % 16) for k in range(1, 16)] + [peer(i, j) for i, j in plane])

    ids_f[...] = jnp.full((128, T), -1.0, F32)
    ids_f[pl.ds(0, 1)] = hist_v[...].astype(F32)
    ids_f[pl.ds(1, 3)] = neg_v[...].astype(F32)
    rall[0] = ids_f[pl.ds(0, 8)].astype(I32)
    cand[pl.ds(0, T)] = ids_f[...].T.astype(I32)

    loads[0].wait()

    def norm_rows(i):
        j = (g + i) % 16
        rows = traw[ds(j, 32)].astype(F32)
        length = lax.rsqrt(jnp.sum(rows * rows, -1, keepdims=True) + EPS)
        tab[0, j // 4, j % 4] = (rows * length).astype(BF)

    norm_rows(0)
    everyone()
    low, high = pl.ds(0, 512), pl.ds(512, 512)
    mine_at = lambda dz, cols: tab.at[dz, px, py, :, cols]
    slice_in = {}
    for a, b in ((1, 7), (2, 6), (3, 5)):
        slice_in[a, b] = net.bundle(
            tab.at[0, 0, pl.ds(0, 2)],
            *[(tab.at[0, px, py], tab.at[8 - k, px, py], w.zoff(k)) for k in (a, b)])
    rep(15, lambda i: norm_rows(i + 1))
    cp_cand = net.go(cand.at[pl.ds(0, T)], cand.at[pl.ds(T, T)], w.mate())

    pieces = {7: (tab.at[7], 0, 1024, "y"), 1: (tab.at[1], 0, 1024, "x"),
              6: (tab.at[6], 0, 1024, "y"), 2: (tab.at[2], 0, 1024, "x"),
              5: (tab.at[5], 0, 1024, "y"), 3: (tab.at[3], 0, 1024, "x"),
              "4x": (tab.at[4], 0, 512, "x"), "4y": (tab.at[4], 512, 512, "y")}
    flying, early = {}, {}

    def one(piece, kx, ky, c0, nc):
        return piece[0].at[(px + kx) % 4, (py + ky) % 4, :, pl.ds(c0, nc)]

    def many(piece, k, c0, nc):
        if piece[3] == "x":
            return piece[0].at[:, (py + k) % 4, :, pl.ds(c0, nc)]
        return piece[0].at[(px + k) % 4, :, :, pl.ds(c0, nc)]

    def pair(name, whole, right, left, off):
        flying[name] = net.bundle(whole, (right, right, off(1)), (left, left, off(-1)))

    def first_send(name):
        p = pieces[name]
        own = one(p, 0, 0, p[1], p[2])
        whole = p[0].at[0, pl.ds(0, 2), :, pl.ds(p[1], p[2])]
        across = w.yoff if p[3] == "x" else w.xoff
        pair(name, whole, own, own, w.xoff if p[3] == "x" else w.yoff)
        early[name] = net.bundle(whole, (own, own, across(1)), (own, own, across(-1)))

    def first_forward(name):
        p = pieces[name]
        half = p[2] // 2
        at = (lambda k, c0: one(p, k, 0, c0, half)) if p[3] == "x" else (lambda k, c0: one(p, 0, k, c0, half))
        flying[name].wait_recv()
        pair(name, one(p, 0, 0, p[1], p[2]), at(-1, p[1]), at(1, p[1] + half), w.xoff if p[3] == "x" else w.yoff)

    def second_send(name):
        p = pieces[name]
        flying[name].wait_recv()
        across = w.yoff if p[3] == "x" else w.xoff
        others = [one(p, k, 0, p[1], p[2]) if p[3] == "x" else one(p, 0, k, p[1], p[2]) for k in (1, 3, 2)]
        flying[name] = net.bundle(
            p[0].at[pl.ds(0, 2), pl.ds(0, 3), :, pl.ds(p[1], p[2])],
            *[(ref, ref, across(d)) for ref in others for d in (1, -1)])

    def second_forward(name):
        p = pieces[name]
        half = p[2] // 2
        early[name].wait_recv()
        flying[name].wait_recv()
        pair(name, many(p, 0, p[1], p[2]), many(p, -1, p[1], half), many(p, 1, p[1] + half, half),
             w.yoff if p[3] == "x" else w.xoff)

    def step(stage, *names):
        for name in names:
            stage(name)

    def slices(a, b):
        slice_in[a, b].wait_recv()

    ends = []
    for j in range(16):
        ends.append(len_s[0, j] + (ends[-1] if ends else 0))
    tc, tr = iota((T, 128), 0), iota((8, T), 1)
    uid_c, uid_r = jnp.zeros((T, 128), I32), jnp.zeros((8, T), I32)
    for end in ends:
        uid_c = uid_c + (tc >= end).astype(I32)
        uid_r = uid_r + (tr >= end).astype(I32)
    same = (uid_c[:, :1] == uid_r[:1, :]) & (iota((T, T), 1) <= iota((T, T), 0))
    mask_v[...] = same.astype(F32)

    loads[1].wait()

    def norm_in(i):
        v = x_v[ds(i, 32)].astype(F32)
        v = v - jnp.mean(v, -1, keepdims=True)
        nin[ds(i, 32)] = (v * lax.rsqrt(jnp.mean(v * v, -1, keepdims=True) + EPS)).astype(BF)

    rep(8, norm_in, 2)
    loads[2].wait()
    loads[3].wait()

    def project(i):
        pre = mm(nin[...], win[:, ds(i, 256)])
        sg = sigmoid(pre)
        proj[:, ds(i, 256)] = (pre * sg).astype(BF)
        slope[:, ds(i, 256)] = sg * (1.0 + pre * (1.0 - sg))

    rep(2, project)
    slices(1, 7)
    step(first_send, 1, 7)
    rep(3, lambda i: project(i + 2))
    slices(2, 6)
    step(first_send, 2, 6)
    rep(3, lambda i: project(i + 5))
    step(first_forward, 1, 7)

    def flip_in(i):
        block = nin[:, ds(i, 128)].astype(F32).T
        ninT[i] = block.astype(BF).reshape(2, 64, T)

    def attend(h):
        col = lambda part: pl.ds(pl.multiple_of(part * HID + h * 128, 128), 128)
        scores = mm_t(proj[:, col(2)], proj[:, col(3)]) * SCALE
        sg = sigmoid(scores)
        mask = mask_v[...]
        weight = (scores * sg * mask).astype(BF)
        attn[h] = weight
        dsl[h] = sg * (1.0 + scores * (1.0 - sg)) * SCALE * mask
        att[:, ds(h, 128)] = mm(weight, proj[:, col(1)])

    rep(2, attend, 2)
    slices(3, 5)
    slice_in["4r", "4l"] = net.bundle(
        tab.at[0, 0, 0], (mine_at(5, low), mine_at(4, low), w.zoff(1)), (mine_at(3, high), mine_at(4, high), w.zoff(-1)))
    step(first_send, 3, 5)
    step(first_forward, 2, 6)
    rep(2, lambda h: attend(h + 2), 2)
    step(second_send, 1, 7)

    def norm_att(i):
        v = att[ds(i, 32)]
        v = v - jnp.mean(v, -1, keepdims=True)
        f = lax.rsqrt(jnp.mean(v * v, -1, keepdims=True) + EPS)
        n = v * f
        normed[ds(i, 32)] = n
        inv[ds(i, 32)] = jnp.broadcast_to(f, (32, 128))
        gated[ds(i, 32)] = (n * proj[ds(i, 32), pl.ds(0, HID)].astype(F32)).astype(BF)

    rep(8, norm_att, 2)
    slices("4r", "4l")
    step(first_send, "4x", "4y")
    step(first_forward, 3, 5)
    step(second_send, 2, 6)

    def result(i):
        res[:, ds(i, 256)] = x_v[:, ds(i, 256)].astype(F32) + mm_t(gated[...], wout[ds(i, 256)])

    rep(4, result)

    def norm_out(i):
        v = res[ds(i, 32)]
        f = lax.rsqrt(jnp.sum(v * v, -1, keepdims=True) + EPS)
        rlen[ds(i, 32)] = jnp.broadcast_to(f, (32, 128))
        yall[0, ds(i, 32)] = (v * f).astype(BF)
        lout[ds(i, 32)] = v.astype(BF)

    rep(8, norm_out, 2)
    cp_y = net.go(yall.at[0], ymate, w.mate())
    two_y = yall.at[pl.ds(0, 2)]
    hop = net.bundle(two_y, (yall.at[0], yall.at[7], w.zoff(1)), (yall.at[0], yall.at[1], w.zoff(-1)))
    cp_rows = net.bundle(rall.at[pl.ds(0, 7)], *[(rall.at[0], rall.at[8 - k], w.zoff(k)) for k in range(1, 8)])
    lane8 = iota((8, 128), 1)
    counts = jnp.zeros((8, 128), F32)
    place = jnp.zeros((8, T), I32)
    start = 0
    for j in range(16):
        n, d = len_s[0, j], dst_s[0, j]
        counts = counts + jnp.where(lane8 == d, n, 0).astype(F32)
        place = jnp.where((tr >= start) & (tr < start + n), d * 32 + tr - start, place)
        start = start + n
    csend[...] = counts
    cbuf[s] = csend[...]

    def fill(i):
        pick = jnp.where(iota((128, T), 0) + i * 128 == place[:1, :], 1.0, 0.0).astype(BF)
        slots_s[pl.ds(i * 4, 4)] = mm(pick, lout[...]).astype(BF).reshape(4, 32, D)

    used = pl.ds(0, 24)
    rep(4, fill)
    for k in range(16):
        slots_r[k, pl.ds(24, 8)] = jnp.zeros((8, D), BF)
    slots_r[s, used] = slots_s[s, used]
    cp_count = net.bundle(cbuf.at[pl.ds(0, 15)], *[(csend, cbuf.at[s], w.at(seq=(s + k) % 16)) for k in range(1, 16)])

    def slots(*ks):
        return net.bundle(
            slots_r.at[pl.ds(0, len(ks)), used],
            *[(slots_s.at[(s + k) % 16, used], slots_r.at[s, used], w.at(seq=(s + k) % 16)) for k in ks])

    cp_slot = [slots(8, 1, 15, 2, 14)]

    step(first_forward, "4x", "4y")
    rep(8, flip_in, 2)
    step(second_forward, 1, 7)
    step(second_send, 3, 5)
    cp_nin = net.go(ninT.at[:, 1 - c], ninTm, w.mate())
    cp_gated = net.go(gated, gatedm, w.mate())

    lsum[...] = jnp.zeros_like(lsum)
    lanes = iota((256, 128), 1).astype(F32)
    cp_cand.wait_recv()

    def owner(dz):
        return ((z + dz) % 8) * 2 + c

    def aim(dz):
        def part(i):
            who = cand[ds(i, 256)]
            spot = jnp.where((who >> 9) == owner(dz), (who & 511) + 1, 0).astype(F32)
            spot = jnp.broadcast_to(jnp.sum(spot, -1, keepdims=True) - 1.0, (256, 128))
            for q in range(4):
                picks[ds(i, 256), pl.ds(q * 128, 128)] = jnp.where(spot == lanes + 128.0 * q, 1.0, 0.0).astype(BF)
            lacc[ds(i, 256)] = jnp.zeros((256, 128), F32)

        rep(2, part)

    def score(dz):
        def part(i):
            rows = mm(picks[...], tab[dz, :, :, :, ds(i, 256)].reshape(512, 256))
            found[dz, :, ds(i, 256)] = rows.astype(BF)
            for first, y in ((0, yall[0, :, ds(i, 256)]), (T, ymate[:, ds(i, 256)])):
                got = rows[first:first + T] * y.astype(F32)
                lacc[pl.ds(first, T)] += got[:, :128] + got[:, 128:]

        rep(4, part, 2)

        def close(i):
            value = jnp.sum(lacc[ds(i, 256)], -1, keepdims=True)
            lsum[ds(i, 256)] += jnp.where((cand[ds(i, 256)] >> 9) == owner(dz), value, 0.0)

        rep(2, close)

    def settle(*names):
        for name in names:
            flying[name].wait_recv()

    aim(0)
    cp_y.wait_recv()
    score(0)
    step(second_send, "4x", "4y")
    aim(1)
    settle(1, 7)
    step(second_forward, 2, 6)
    score(1)
    aim(7)
    score(7)
    hop.wait_recv()
    hop = net.bundle(two_y, (yall.at[7], yall.at[6], w.zoff(1)), (yall.at[1], yall.at[2], w.zoff(-1)))
    aim(2)
    settle(2, 6)
    step(second_forward, 3, 5)
    score(2)
    aim(6)
    score(6)
    step(second_forward, "4x", "4y")
    aim(3)
    settle(3, 5)
    score(3)
    aim(5)
    score(5)
    aim(4)
    settle("4x", "4y")
    score(4)
    lsend[...] = lsum[...].T[:8]
    cp_l = net.go(lsend, lrec, w.mate())
    cp_l.wait_recv()
    other = lrec[...]
    logits = (lsend[...] + jnp.concatenate([other[:, T:], other[:, :T]], 1)) / TEMP
    cand_no = iota((8, 2 * T), 0)
    live = cand_no < NCAND
    ex = jnp.where(live, jnp.exp(jnp.where(live, logits, 0.0)), 0.0)
    soft = ex / jnp.sum(ex, 0, keepdims=True)
    coef = jnp.where(live, soft - (cand_no == 0).astype(F32), 0.0) / TEMP
    gsend[...] = coef[:, :T]
    gall[0] = coef[:, :T]
    gcol[...] = jnp.concatenate([coef, jnp.zeros((120, 2 * T), F32)], 0).T

    cp_g = net.bundle(gall.at[pl.ds(0, 7)], *[(gsend, gall.at[8 - k], w.zoff(k)) for k in range(1, 8)])


    hop.wait_recv()
    hop = net.bundle(two_y, (yall.at[6], yall.at[5], w.zoff(1)), (yall.at[2], yall.at[3], w.zoff(-1)))

    def blend(at):
        who, how = cand[at] >> 9, gcol[at]
        total = jnp.zeros((32, D), F32)
        for dz in range(8):
            much = jnp.sum(jnp.where(who == owner(dz), how, 0.0), -1, keepdims=True)
            total = total + much * found[dz, at].astype(F32)
        return total

    def gather_mate(i):
        wsend[ds(i, 32)] = blend(ds(i + 8, 32)).astype(BF)

    rep(8, gather_mate, 2)
    cp_w = net.go(wsend, wrec, w.mate())

    def gather_own(i):
        wown[ds(i, 32)] = blend(ds(i, 32))

    rep(8, gather_own, 2)
    cp_w.wait_recv()

    def upstream(i):
        f = rlen[ds(i, 32)][:, :1]
        yn = res[ds(i, 32)] * f
        v = wown[ds(i, 32)] + wrec[ds(i, 32)].astype(F32)
        up = (v - yn * jnp.sum(yn * v, -1, keepdims=True)) * f
        upb[ds(i, 32)] = up.astype(BF)

    rep(8, upstream, 2)

    gg[...] = mm(upb[...], wout[...])

    def back_norm(i):
        n, v = normed[ds(i, 32)], gg[ds(i, 32)]
        gpre[ds(i, 32), pl.ds(0, HID)] = (v * n * slope[ds(i, 32), pl.ds(0, HID)]).astype(BF)
        v = v * proj[ds(i, 32), pl.ds(0, HID)].astype(F32)
        v = v - jnp.mean(v, -1, keepdims=True) - n * jnp.mean(v * n, -1, keepdims=True)
        gatt[ds(i, 32)] = (inv[ds(i, 32)][:, :1] * v).astype(BF)

    rep(8, back_norm, 2)

    def flip_up(i):
        block = upb[:, ds(i, 128)].astype(F32).T
        upT[i] = block.astype(BF).reshape(2, 64, T)

    cp_pre = net.go(gpre.at[:, pl.ds(0, HID)], gprem.at[:, pl.ds(0, HID)], w.mate())
    rep(8, flip_up, 2)
    cp_up = net.go(upT.at[:, 1 - c], upTm, w.mate())

    def back_attend(h):
        col = lambda part: pl.ds(pl.multiple_of(part * HID + h * 128, 128), 128)
        da = gatt[:, ds(h, 128)]
        ds_ = (mm_t(da, proj[:, col(1)]) * dsl[h])
        gv = mm(attn[h].astype(F32).T.astype(BF), da)
        gq = mm(ds_.astype(BF), proj[:, col(3)])
        gk = mm(ds_.T.astype(BF), proj[:, col(2)])
        gpre[:, col(1)] = (gv * slope[:, col(1)]).astype(BF)
        gpre[:, col(2)] = (gq * slope[:, col(2)]).astype(BF)
        gpre[:, col(3)] = (gk * slope[:, col(3)]).astype(BF)

    rep(4, back_attend, 2)
    rest = pl.ds(HID, 3 * HID)
    cp_rest = net.go(gpre.at[:, rest], gprem.at[:, rest], w.mate())

    def store_g(i, first, block):
        for b in range(block.shape[1] // 128):
            n = first + b
            if n < 4:
                group, at = n // 2, n % 2
            elif n < 16:
                group, at = (n - 4) // 3, 2 + (n - 4) % 3
            else:
                group, at = 2 + (n - 16) // 2, n % 2
            g_v[group, pl.ds(i * 4, 4), :, :, pl.ds(at * 128, 128)] = (
                block[:, b * 128:(b + 1) * 128].astype(BF).reshape(4, 4, 16, 128))

    two = lambda k: pl.ds(2 * k, 2)
    cut = lambda k: pl.ds(256 * k, 256)
    hicut = lambda k: pl.ds(512 + 256 * k, 256)

    def g_rings(cols):
        cut = lambda bufs: [buf.at[:, :, :, :, cols] for buf in bufs]
        return (
            Ring(net, w.xoff, px, lambda j, k: g_v.at[j, two(k), :, :, cols], cut(ga_b),
                 lambda k: a1.at[two(k), :, :, cols]),
            Ring(net, w.yoff, py, lambda j, k: g_v.at[:, pl.ds(4 + 2 * k, 2), j, :, cols], cut(gb_b),
                 lambda k: b1.at[:, two(k), :, cols]))

    ga, gb = g_rings(pl.ds(0, 256))
    gc, gd = g_rings(pl.ds(256, 384))
    ha = Ring(net, w.xoff, px, lambda j, k: h_v.at[j, :, :, cut(k)], ha_b, lambda k: ha1.at[:, :, cut(k)])
    hb = Ring(net, w.yoff, py, lambda j, k: h_v.at[:, j, :, hicut(k)], hb_b, lambda k: hb1.at[:, :, cut(k)])
    ga2 = Swap(net, w.yoff, py, lambda j: a1.at[:, j], ga2_b, piece.at[pl.ds(0, 4)])
    gb2 = Swap(net, w.xoff, px, lambda j: b1.at[j], gb2_b, piece.at[pl.ds(4, 4)])
    mine = hall.at[px, py]
    ha2 = Swap(net, w.yoff, py, lambda j: ha1.at[j], ha2_b, hpiece.at[:, low])
    hb2 = Swap(net, w.xoff, px, lambda j: hb1.at[j], hb2_b, hpiece.at[:, high])
    cp_gated.wait_recv()
    cp_up.wait_recv()
    cp_nin.wait_recv()
    cp_pre.wait_recv()

    def grad_out(i):
        a = upT[pl.ds(i * 4, 4), c].reshape(T, T)
        b = upTm[pl.ds(i * 4, 4)].reshape(T, T)
        store_g(i, 16, mm(a, gated[...]) + mm(b, gatedm[...]))

    def grad_in(i, blocks):
        a = ninT[pl.ds(i * 4, 4), c].reshape(T, T)
        b = ninTm[pl.ds(i * 4, 4)].reshape(T, T)
        for n in blocks:
            cols = pl.ds(n * 512, 512)
            store_g(i, n * 4, mm(a, gpre[:, cols]) + mm(b, gprem[:, cols]))

    def grad_first(i):
        grad_out(i)
        grad_in(i, (0,))

    rep(2, grad_first)
    ga.start()
    gb.start()
    cp_rows.wait_recv()
    cp_g.wait_recv()

    def spread_t(dz):
        who, how = rall[dz], gall[dz]
        for o in range(2):
            hit = (who >> 9) == z * 2 + o
            spot = jnp.sum(jnp.where(hit, (who & 511) + 1, 0).astype(F32), 0, keepdims=True) - 1.0
            much = jnp.sum(jnp.where(hit, how, 0.0), 0, keepdims=True)
            for j in range(4):
                line = (iota((128, T), 0) + j * 128).astype(F32)
                found[dz // 4 + 2 * o, pl.ds(j * 128, 128), ds(dz % 4, T)] = jnp.where(line == spot, much, 0.0).astype(BF)

    rep(8, spread_t)

    cp_rest.wait_recv()
    rep(2, lambda i: grad_in(i, (1, 2, 3)))
    gc.start()
    gd.start()

    def h_part(o, k, i):
        total = jnp.zeros((2 * T, 256), F32)
        for plane_no, first, n in ((0, 0, 3), (1, 2, 2)) if k == 0 else ((0, 3, 1), (1, 0, 2)):
            y = yall[pl.ds(plane_no * 4 + first, n), :, ds(i, 256)].reshape(n * T, 256)
            total = total + mm(found[2 * o + plane_no, :, pl.ds(first * T, n * T)], y)
        return total

    def h_first(i):
        part = h_part(1 - c, 0, i)
        slope[:, ds(i, 256)] = part[:T]
        slope[:, ds(i + 4, 256)] = part[T:]
        part = h_part(c, 0, i)
        wown[:, ds(i, 256)] = part[:T]
        res[:, ds(i, 256)] = part[T:]

    def h_mate(i):
        part = h_part(1 - c, 1, i)
        hsend[pl.ds(0, T), ds(i, 256)] = (part[:T] + slope[:, ds(i, 256)]).astype(BF)
        hsend[pl.ds(T, T), ds(i, 256)] = (part[T:] + slope[:, ds(i + 4, 256)]).astype(BF)

    def h_own(i):
        part = h_part(c, 1, i)
        wown[:, ds(i, 256)] += part[:T]
        res[:, ds(i, 256)] += part[T:]

    rep(4, h_first)
    for ring in (ga, gb):
        ring.relay()
    hop.wait_recv()
    a, b = pl.ds(0, 512), pl.ds(512, 512)
    hop = net.bundle(yall.at[0], (yall.at[5, :, a], yall.at[4, :, a], w.zoff(1)),
                     (yall.at[3, :, b], yall.at[4, :, b], w.zoff(-1)))
    for ring in (gc, gd):
        ring.relay()
    for ring in (ga, gb, gc, gd):
        ring.finish()
    ga2.start()
    gb2.start()
    hop.wait_recv()
    rep(4, h_mate)
    cp_h = net.go(hsend, hrec, w.mate())
    rep(4, h_own)
    cp_h.wait_recv()
    for part, src in ((0, wown), (1, res)):
        for i in range(8):
            total = src[pl.ds(i * 32, 32)] + hrec[pl.ds(part * T + i * 32, 32)].astype(F32)
            h_v[part * 2 + i // 4, i % 4] = total.astype(BF)
    ha.start()
    hb.start()
    ga2.finish()
    gb2.finish()
    cp_z = net.bundle(zbuf.at[pl.ds(0, 7)], *[(piece.at[(z + k) % 8], zbuf.at[k], w.zoff(k)) for k in range(1, 8)])
    cp_slot.append(slots(7, 9, 6, 10, 5, 11, 4, 12, 3, 13))
    ha.relay()
    hb.relay()
    ha.finish()
    ha2.start()
    hb.finish()
    hb2.start()
    total = piece[z].astype(F32)
    cp_z.wait_recv()
    for k in range(1, 8):
        total = total + zbuf[k].astype(F32)
    wpiece[...] = total.astype(BF)
    ha2.finish()
    hb2.finish()
    rows = traw[ds(g, 32)].astype(F32)
    length = lax.rsqrt(jnp.sum(rows * rows, -1, keepdims=True) + EPS)
    rows, total = rows * length, hpiece[...].astype(F32)
    mine[...] = ((total - rows * jnp.sum(rows * total, -1, keepdims=True)) * length).astype(BF)
    hops = (2, 1, 3)
    plans = (("x", low, w.xoff, w.yoff), ("y", high, w.yoff, w.xoff))
    spread, cross = {}, {}
    for name, cols, along, over in plans:
        part, whole = mine.at[:, cols], hall.at[0, pl.ds(0, 3), :, cols]
        spread[name] = net.bundle(whole, *[(part, part, along(k)) for k in hops])
        cross[name] = net.bundle(whole, *[(part, part, over(k)) for k in hops])
    cp_sum = net.bundle(wall.at[pl.ds(0, 15)], *[(wpiece, wall.at[g], peer(i, j)) for i, j in plane])
    wall[g] = wpiece[...]
    cover = []
    for name, cols, along, over in plans:
        parts = [hall.at[(px + k) % 4, py, :, cols] if name == "x" else hall.at[px, (py + k) % 4, :, cols] for k in hops]
        spread[name].wait_recv()
        cover.append(net.bundle(hall.at[pl.ds(0, 3), pl.ds(0, 3), :, cols],
                                *[(part, part, over(k)) for k in hops for part in parts]))

    cp_count.wait_recv()
    for copy in cp_slot:
        copy.wait_recv()
    cnt = jnp.sum(jnp.where(iota((16, 128), 1) == s, cbuf[:, 0, :], 0.0), -1, keepdims=True)
    row, col16 = iota((16, 512), 0), iota((16, 512), 1)
    slot = col16 >> 5
    before = jnp.sum(jnp.where(row < slot, cnt, 0.0), 0, keepdims=True)
    here = jnp.sum(jnp.where(row == slot, cnt, 0.0), 0, keepdims=True)
    inside = (col16[:1] & 31).astype(F32)
    goal = jnp.where(inside < here, before + inside, -1.0)
    chosen = jnp.where(iota((T, 512), 0).astype(F32) == goal, 1.0, 0.0).astype(BF)

    def land(i):
        lay_o[:, ds(i, 256)] = mm(chosen, slots_r[:, :, ds(i, 256)].reshape(512, 256)).astype(BF)

    rep(4, land)
    cp_sum.wait_recv()
    w_o[...] = wall[...]
    for copy in cover + [cross["x"], cross["y"]]:
        copy.wait_recv()
    h_o[...] = hall[...]
    assert net.n == NSEM, net.n
    net.drain()


def train_call(lengths, destinations, hist, neg, events, in_weight, out_weight, item_table):
    vm = lambda *shape, dtype=BF: pltpu.VMEM(shape, dtype)
    f32 = dict(dtype=F32)
    halves = [(2, 4, 16, 640), (4, 2, 16, 640), (4, 32, 256), (4, 32, 256)]
    wholes = [(4, 16, 640), (4, 16, 640), (32, 512), (32, 512)]
    sem = pltpu.SemaphoreType.DMA
    scratch = [
        vm(T, D), vm(D, 4 * HID), vm(D, HID), vm(512, D), vm(8, 4, 4, 32, D), vm(T, D),
        vm(T, 4 * HID, **f32), vm(T, 4 * HID), vm(HEADS, T, T), vm(HEADS, T, T, **f32),
        vm(T, HID, **f32), vm(T, HID, **f32), vm(T, 128, **f32), vm(T, HID), vm(T, HID),
        vm(T, D, **f32), vm(T, 128, **f32), vm(8, T, D), vm(T, D), vm(128, T, **f32), vm(2 * T, 128, dtype=I32),
        vm(8, 8, T, dtype=I32), vm(8, 8, T, **f32), vm(8, T, **f32), vm(2 * T, 128, **f32),
        vm(2 * T, 128, **f32), vm(8, 2 * T, **f32), vm(8, 2 * T, **f32), vm(2 * T, 128, **f32), vm(2 * T, 512),
        vm(8, 2 * T, D), vm(T, D, **f32), vm(T, D), vm(T, D), vm(T, D),
        vm(T, HID, **f32), vm(T, HID), vm(T, 4 * HID), vm(T, 4 * HID), vm(8, 2, 64, T), vm(8, 64, T),
        vm(8, 2, 64, T), vm(8, 64, T), vm(512, D), vm(512, D), vm(T, T, **f32), vm(T, D),
        vm(4, 8, 4, 16, 640), vm(4, 4, 32, D),
        vm(4, 4, 16, 640), vm(4, 4, 16, 640), vm(4, 32, 512), vm(4, 32, 512), vm(8, 16, 640), vm(8, 16, 640),
        vm(16, 640), vm(32, D), vm(16, 16, 640), vm(4, 4, 32, D), vm(16, 32, D), vm(16, 32, D),
        vm(8, 128, **f32), vm(16, 8, 128, **f32),
        sem((4,)), sem((NSEM,)), sem((NSEM,)),
    ] + [vm(2, *shape) for shape in halves for _ in range(4)] + [vm(4, *shape) for shape in wholes]
    any_ = pl.BlockSpec(memory_space=pl.ANY)
    vmem = pl.BlockSpec(memory_space=pltpu.VMEM)
    smem = pl.BlockSpec(memory_space=pltpu.SMEM)
    return pl.pallas_call(
        train_kernel,
        out_shape=(jax.ShapeDtypeStruct((T, D), BF), jax.ShapeDtypeStruct((16, 16, 640), BF),
                   jax.ShapeDtypeStruct((4, 4, 32, D), BF)),
        in_specs=[smem, smem, vmem, vmem, any_, any_, any_, any_],
        out_specs=(vmem, vmem, vmem),
        scratch_shapes=scratch,
        compiler_params=pltpu.CompilerParams(collective_id=0, has_side_effects=True, vmem_limit_bytes=VMEM_BYTES),
        name="train",
    )(lengths, destinations, hist, neg, events, in_weight, out_weight, item_table)


def last_kernel(lay, w, h, lay_o, in_o, out_o, tab_o):
    lay_o[...] = lay[...]
    part = lambda i, a, b: w[i, 0][:, a:b].astype(F32)
    in_o[...] = jnp.concatenate([part(0, 0, 256), part(1, 0, 256)] + [part(i, 256, 640) for i in range(4)], 1)
    out_o[...] = jnp.concatenate([part(2, 0, 256), part(3, 0, 256)], 1)
    tab_o[...] = h[0].reshape(128, D).astype(F32)


def last_call(lay, w, h):
    rows = lambda n, m: pl.BlockSpec((n, m), lambda i: (i, 0))
    return pl.pallas_call(
        last_kernel,
        grid=(4,),
        out_shape=(jax.ShapeDtypeStruct((T, D), BF), jax.ShapeDtypeStruct((64, 4 * HID), F32),
                   jax.ShapeDtypeStruct((64, HID), F32), jax.ShapeDtypeStruct((512, D), F32)),
        in_specs=[rows(64, D), pl.BlockSpec((4, 1, 16, 640), lambda i: (0, i, 0, 0)),
                  pl.BlockSpec((1, 4, 32, D), lambda i: (i, 0, 0, 0))],
        out_specs=(rows(64, D), rows(16, 4 * HID), rows(16, HID), rows(128, D)),
        name="last",
    )(lay, w, h)


def body(events, lengths, destinations, history, negatives, in_weight, out_weight, item_table):
    result, wsum, hsum = train_call(lengths, destinations, history.reshape(1, T), negatives.T, events,
                                    in_weight, out_weight, item_table)
    return last_call(result, wsum.reshape(4, 4, 16, 640), hsum)


def solution(mesh):
    return jax.shard_map(
        body,
        mesh=mesh,
        in_specs=(
            P(("grp", "seq"), None),
            P(("grp", "seq"), None),
            P(("grp", "seq"), None),
            P(("grp", "seq")),
            P(("grp", "seq"), None),
            P(),
            P(),
            P("seq", None),
        ),
        out_specs=(P(("grp", "seq"), None), P("seq", None), P("seq", None), P("seq", None)),
        check_vma=False,
    )
```
